32 devices in a mesh: groups: 2 (over y), ctx: 16 (over z, x, core).
Axes of the slice: x: 2, y: 2, z: 4, core: 2. Of those that a mesh axis runs over, the one named last changes fastest.
Arguments:
- old_cache: bfloat16 [4096, 2048], P(('groups', 'ctx')), parts along dimension 0, may hold values from -10 to 10
- new_slot: int32 [4096], P(('groups', 'ctx')), parts along dimension 0, may hold values from -1 to 1023, as said below
- lengths: int32 [8], P('groups'), parts along dimension 0, may hold values from 1 to 768, 1024 in all
- old_angle: float32 [768, 64], replicated, may hold values from -3.15 to 3.15
- new_angle: float32 [768, 64], replicated, may hold values from -3.15 to 4.15
- queries: bfloat16 [64, 8192], P(('groups', 'ctx')), parts along dimension 0, may hold values from -128 to 128
- new_kv: bfloat16 [64, 2048], P(('groups', 'ctx')), parts along dimension 0, may hold values from -6 to 6
- resid: bfloat16 [64, 8192], P(('groups', 'ctx')), parts along dimension 0, may hold values from -6 to 6
- gain: bfloat16 [8192], replicated, may hold values from 0.25 to 1.75
- w_gate: bfloat16 [8192, 28672], P(None, 'ctx'), may hold values from -0.0625 to 0.0625
- w_up: bfloat16 [8192, 28672], P(None, 'ctx'), may hold values from -0.0625 to 0.0625
- w_down: bfloat16 [28672, 8192], P('ctx'), may hold values from -0.03125 to 0.03125
Outputs:
- new_cache: bfloat16 [2048, 2048], P(('groups', 'ctx')), parts along dimension 0
- layer_out: bfloat16 [64, 8192], P(('groups', 'ctx')), parts along dimension 0
The draws below stay inside these ranges and needn't reach their ends.
There are 2 independent parts, one for each index of `groups`. The reference program is written for one: setup_inputs(seed, part) draws one part's arguments, and reference() takes and returns one part's arrays. A program takes and returns all parts, laid end to end along the dimension named above; an argument that names none is the same for every part. Nothing has to cross between parts.
Inputs may be any that keep to these rules, and one draw needn't show every extreme that they name: `new_slot`: for slots below 1024: distinct slots of the new layout; the tokens of each holding device go to every device of ctx, exactly 8 to each. Slots from 1024 on hold -1.
All inputs are finite; a program needn't handle non-finite values.
Results may differ from the reference program's by a relative error of at most 0.0057.
Values may be sent and summed in bfloat16 or wider, within the bound.
No kernel may reach another device: no remote copies, remote signals or barrier semaphores. Data moves between devices by JAX's collectives and lax.ppermute only.
A program may use at most 128 MiB of HBM per device.

```python
import math
import jax
import jax.numpy as jnp
import numpy as np
from jax import lax

D = 8192
QH = 64
KVH = 8
HD = 128
FF = 28672
CTOK_DEV = 64
SAMPLES = 4
SLOTS = 128
CACHE = 1024
R = 4
MAXLEN = 768
M = 32
G = 8
W = 2048
HALF = 64
N_CTX = 16


def draw_new_slot(key, part):
    per_peer = SLOTS // N_CTX
    first_key = jax.random.fold_in(key, 11)
    second_key = jax.random.fold_in(key, 23)
    sender_perm = jax.vmap(lambda sender: jax.random.permutation(jax.random.fold_in(first_key, sender), SLOTS))(jnp.arange(N_CTX, dtype=jnp.int32)).astype(jnp.int32)
    place_perm = jax.vmap(lambda target: jax.random.permutation(jax.random.fold_in(second_key, target), CTOK_DEV))(jnp.arange(N_CTX, dtype=jnp.int32)).astype(jnp.int32)
    slot_index = jnp.arange(N_CTX * SLOTS, dtype=jnp.int32)
    sender = slot_index // SLOTS
    local = slot_index % SLOTS
    mixed = sender_perm[sender, local]
    target = mixed // per_peer
    within = sender * per_peer + mixed % per_peer
    within = jnp.minimum(within, CTOK_DEV - 1)
    placed = target * CTOK_DEV + place_perm[target, within]
    return jnp.where(slot_index < CACHE, placed, -1).astype(jnp.int32)


def angle_tables(key):
    old_table = jax.random.uniform(jax.random.fold_in(key, 31), (MAXLEN, HALF), jnp.float32, -math.pi, math.pi)
    rates = jnp.exp(jax.random.uniform(jax.random.fold_in(key, 37), (HALF,), jnp.float32, math.log(0.03), math.log(1.0)))
    ramp = jnp.arange(MAXLEN, dtype=jnp.float32)[:, None] / float(MAXLEN)
    return (old_table, old_table + rates[None, :] * ramp)


def draw_old_angle(key, part):
    return angle_tables(key)[0]


def draw_new_angle(key, part):
    return angle_tables(key)[1]


def directions(key):
    base = jax.random.fold_in(key, 101)
    key_dir = jax.random.normal(jax.random.fold_in(base, 1), (KVH, HD), jnp.float32)
    sign_dir = jax.random.normal(jax.random.fold_in(base, 2), (KVH, HD), jnp.float32)
    value_dir = jnp.where(jax.random.uniform(jax.random.fold_in(base, 3), (KVH, HD), jnp.float32) < 0.5, -1.0, 1.0)
    return (key_dir, sign_dir, value_dir)


def draw_old_cache(key, part):
    total_rows = N_CTX * SLOTS
    key_dir, sign_dir, value_dir = directions(key)
    root = float(HD) ** 0.5
    signs = jnp.where(jax.random.uniform(jax.random.fold_in(key, 41), (total_rows, KVH), jnp.float32) < 0.5, -1.0, 1.0)
    blocks = total_rows // 256
    offset = jax.random.randint(jax.random.fold_in(key, 43), (blocks,), 0, 255)
    slot_index = jnp.arange(total_rows, dtype=jnp.int32)
    block_of = jnp.minimum(slot_index // 256, blocks - 1)
    within = slot_index % 256
    start_mark = within == offset[block_of]
    follow_mark = within == offset[block_of] + 1
    lift = jax.random.uniform(jax.random.fold_in(key, 47), (blocks,), jnp.float32, 1.5, 2.5)[block_of]
    shrink = jax.random.uniform(jax.random.fold_in(key, 53), (blocks,), jnp.float32, 0.004, 0.012)[block_of]
    key_noise = jnp.clip(jax.random.normal(jax.random.fold_in(key, 59), (total_rows, KVH, HD), jnp.float32), -6.0, 6.0)
    value_noise = jnp.clip(jax.random.normal(jax.random.fold_in(key, 61), (total_rows, KVH, HD), jnp.float32), -6.0, 6.0)
    level = 1.5 * jnp.where(start_mark | follow_mark, 1.0 + lift, 1.0)
    keys = 0.15 * key_noise + level[:, None, None] * key_dir[None] / root + signs[:, :, None] * sign_dir[None] / root
    keys = jnp.where(follow_mark[:, None, None], (1.0 - shrink)[:, None, None] * jnp.roll(keys, 1, axis=0), keys)
    values = 2.0 * signs[:, :, None] * value_dir[None] + 0.7 * value_noise
    joined = jnp.stack([keys, values], axis=1).reshape(total_rows, 2 * KVH * HD)
    return jnp.clip(joined, -10.0, 10.0).astype(jnp.bfloat16)


def draw_queries(key, part):
    key_dir, sign_dir, value_dir = directions(key)
    head_keys = jnp.repeat(key_dir, G, axis=0)
    head_signs_dir = jnp.repeat(sign_dir, G, axis=0)
    strength = jnp.exp(jax.random.uniform(jax.random.fold_in(key, 61), (M, 1), jnp.float32, math.log(0.8), math.log(3.5)))
    spread = jnp.exp(jax.random.uniform(jax.random.fold_in(key, 67), (M, QH), jnp.float32, math.log(0.85), math.log(1.18)))
    head_sign = jnp.where(jax.random.uniform(jax.random.fold_in(key, 71), (M, QH), jnp.float32) < 0.5, -1.0, 1.0)
    noise = 0.5 * jnp.clip(jax.random.normal(jax.random.fold_in(key, 5), (M, QH, HD), jnp.float32), -6.0, 6.0)
    base = (strength * spread)[:, :, None] * head_keys[None] + head_sign[:, :, None] * head_signs_dir[None] + noise
    return jnp.clip(base, -128.0, 128.0).reshape(M, D).astype(jnp.bfloat16)


def levels(stream_key, dims, shards, low, high):
    level = 1.0
    for axis_at, blocks in shards:
        heights = jax.random.uniform(jax.random.fold_in(jax.random.fold_in(stream_key, 6), axis_at), (blocks,), jnp.float32, low / len(shards), high / len(shards))
        level = level * jnp.repeat(jnp.exp(heights), dims[axis_at] // blocks).reshape((-1,) + (1,) * (len(dims) - 1 - axis_at))
    return level


def split_up(amount, total, reach, skew):
    weights = [(1 << 20) // math.isqrt(rank ** skew) + 1 for rank in range(2, amount + 1)]
    surplus, holding = total - reach - (amount - 1), [1] * (amount - 1)
    while surplus > 0:
        free = [i for i in range(amount - 1) if holding[i] < reach]
        pool, budget = sum([weights[i] for i in free]), surplus
        for i in free:
            addition = min(reach - holding[i], max(1, budget * weights[i] // pool), surplus)
            holding[i] = holding[i] + addition
            surplus = surplus - addition
    return np.array([reach] + holding)


def uneven(rng, number_of, total, limit, slope):
    if number_of == 2:
        one = jax.random.randint(rng, (), max(1, total - limit), min(limit, total - 1) + 1)
        return jnp.stack([one, total - one])
    sizes = jnp.asarray(split_up(number_of, total, limit, slope), jnp.int32)
    pairs = (number_of - 1) // 2
    giver, taker = sizes[1:1 + 2 * pairs:2], sizes[2:2 + 2 * pairs:2]
    margin = jnp.minimum(giver - 1, limit - taker)
    shifted = jax.random.randint(jax.random.fold_in(rng, 1), (pairs,), 0, 1 << 20) % (margin + 1)
    sizes = sizes.at[1:1 + 2 * pairs:2].set(giver - shifted).at[2:2 + 2 * pairs:2].set(taker + shifted)
    return sizes[jax.random.permutation(jax.random.fold_in(rng, 2), number_of)]


def normal_values(rng, dims, deviation, reach, pieces=(), held_as=jnp.bfloat16):
    values = jax.random.normal(rng, dims, jnp.float32) * deviation
    if len(pieces) > 0:
        values = levels(rng, dims, pieces, -0.22, 0.18) * values
    return jnp.clip(values, min=-reach, max=reach).astype(held_as)


def setup_inputs(seed: int = 0, part: int = 0) -> dict:
    arg_keys = jax.random.split(jax.random.key(seed), 13)
    own_keys = jax.random.split(jax.random.fold_in(arg_keys[12], part), 13)
    old_cache = draw_old_cache(jax.random.fold_in(jax.random.fold_in(arg_keys[12], part), 71), part)
    new_slot = draw_new_slot(jax.random.fold_in(jax.random.fold_in(arg_keys[12], part), 71), part)
    lengths = uneven(own_keys[2], R, CACHE, MAXLEN, 2).astype(jnp.int32)
    old_angle = draw_old_angle(jax.random.fold_in(arg_keys[12], 71), part)
    new_angle = draw_new_angle(jax.random.fold_in(arg_keys[12], 71), part)
    queries = draw_queries(jax.random.fold_in(jax.random.fold_in(arg_keys[12], part), 71), part)
    new_kv = normal_values(own_keys[6], (M, W), 1.0, 6.0, ((0, 16),))
    resid = normal_values(own_keys[7], (M, D), 1.0, 6.0, ((0, 16),))
    gain = jnp.clip(1.0 + 0.15 * jax.random.normal(arg_keys[8], (D,), jnp.float32), 0.25, 1.75).astype(jnp.bfloat16)
    w_gate = normal_values(arg_keys[9], (D, FF), D ** -0.5, 0.0625, ((1, 16),))
    w_up = normal_values(arg_keys[10], (D, FF), D ** -0.5, 0.0625, ((1, 16),))
    w_down = normal_values(arg_keys[11], (FF, D), FF ** -0.5, 0.03125, ((0, 16),))
    return dict(old_cache=old_cache, new_slot=new_slot, lengths=lengths, old_angle=old_angle, new_angle=new_angle, queries=queries, new_kv=new_kv, resid=resid, gain=gain, w_gate=w_gate, w_up=w_up, w_down=w_down)


def rotate_keys(block, where_pos, old_angle, new_angle):
    rows_here = block.shape[0]
    parts = block.reshape(rows_here, 2, KVH, HD)
    keys = parts[:, 0].astype(jnp.float32)
    delta = jnp.take(new_angle, where_pos, axis=0) - jnp.take(old_angle, where_pos, axis=0)
    cosine = jnp.cos(delta)[:, None, :]
    sine = jnp.sin(delta)[:, None, :]
    first = keys[..., :HALF]
    second = keys[..., HALF:]
    turned = jnp.concatenate([first * cosine - second * sine, second * cosine + first * sine], axis=-1).astype(jnp.bfloat16)
    return jnp.stack([turned, parts[:, 1]], axis=1).reshape(rows_here, 2 * KVH * HD)

def reference(old_cache, new_slot, lengths, old_angle, new_angle, queries, new_kv, resid, gain, w_gate, w_up, w_down):
    tokens = jnp.arange(CACHE, dtype=jnp.int32)
    row_ends = jnp.cumsum(lengths).astype(jnp.int32)
    token_row = jnp.searchsorted(row_ends, tokens, side='right').astype(jnp.int32)
    row_starts = (row_ends - lengths).astype(jnp.int32)
    token_pos = (tokens - jnp.take(row_starts, token_row)).astype(jnp.int32)
    turned = rotate_keys(old_cache[:CACHE], token_pos, old_angle, new_angle)
    new_cache = jnp.zeros((CACHE, 2 * KVH * HD), jnp.bfloat16).at[new_slot[:CACHE]].set(turned)
    cached = turned.reshape(CACHE, 2, KVH, HD)
    query_four = queries.reshape(M, KVH, G, HD)
    fresh_kv = new_kv.reshape(M // 2, 2, 2, KVH, HD)
    query_row = jnp.arange(M, dtype=jnp.int32) // (2 * SAMPLES)
    query_sample = jnp.arange(M, dtype=jnp.int32) // 2
    query_step = jnp.arange(M, dtype=jnp.int32) % 2
    matching = query_row[:, None] == token_row[None, :]
    own_steps = jnp.arange(2, dtype=jnp.int32)[None, :] <= query_step[:, None]
    fresh_rows = jnp.take(fresh_kv, query_sample, axis=0)
    scale = 1.0 / float(HD) ** 0.5
    high = lax.Precision.HIGHEST

    def one_head(head_index):
        query_head = jnp.take(query_four, head_index, axis=1).astype(jnp.float32)
        key_head = jnp.take(cached[:, 0], head_index, axis=1).astype(jnp.float32)
        value_head = jnp.take(cached[:, 1], head_index, axis=1).astype(jnp.float32)
        fresh_keys = jnp.take(fresh_rows[:, :, 0], head_index, axis=2).astype(jnp.float32)
        fresh_values = jnp.take(fresh_rows[:, :, 1], head_index, axis=2).astype(jnp.float32)
        scores = jnp.einsum('mge,ce->mgc', query_head, key_head, precision=high) * scale
        scores = jnp.where(matching[:, None, :], scores, -1e+30)
        own_scores = jnp.einsum('mge,mse->mgs', query_head, fresh_keys, precision=high) * scale
        own_scores = jnp.where(own_steps[:, None, :], own_scores, -1e+30)
        row_top = jnp.maximum(lax.optimization_barrier(jnp.max(scores, axis=-1)), lax.optimization_barrier(jnp.max(own_scores, axis=-1)))
        weights_cache = jnp.exp(scores - row_top[..., None])
        weights_own = jnp.exp(own_scores - row_top[..., None])
        summed = jnp.einsum('mgc,ce->mge', weights_cache, value_head, precision=high)
        summed = summed + jnp.einsum('mgs,mse->mge', weights_own, fresh_values, precision=high)
        totals = lax.optimization_barrier(jnp.sum(weights_cache, axis=-1)) + lax.optimization_barrier(jnp.sum(weights_own, axis=-1))
        return summed / totals[..., None]
    per_head = lax.map(one_head, jnp.arange(KVH, dtype=jnp.int32))
    attn = jnp.transpose(per_head, (1, 0, 2, 3)).reshape(M, QH * HD)
    hstate = resid.astype(jnp.float32) + attn
    normed = (hstate * lax.rsqrt(lax.optimization_barrier(jnp.mean(hstate * hstate, axis=-1, keepdims=True)) + 1e-05) * gain.astype(jnp.float32)).astype(jnp.bfloat16)
    gate_out = jnp.dot(normed, w_gate, preferred_element_type=jnp.float32)
    up_out = jnp.dot(normed, w_up, preferred_element_type=jnp.float32)
    hidden = (jax.nn.silu(gate_out) * up_out).astype(jnp.bfloat16)
    ffn_out = jnp.dot(hidden, w_down, preferred_element_type=jnp.float32)
    layer_out = (hstate + ffn_out).astype(jnp.bfloat16)
    return (new_cache, layer_out)
```

```python
import jax
import jax.numpy as jnp
from jax import lax
from jax.experimental import pallas as pl
from jax.experimental.pallas import tpu as pltpu
from jax.sharding import PartitionSpec as P

QH = 64
KVH = 8
HD = 128
CTOK_DEV = 64
SAMPLES = 4
CELL = 4
F32 = jnp.float32
BF16 = jnp.bfloat16
EXTRA = 128


def vmem():
    return pl.BlockSpec(memory_space=pltpu.VMEM)


def smem():
    return pl.BlockSpec(memory_space=pltpu.SMEM)


def hbm():
    return pl.BlockSpec(memory_space=pl.ANY)


def call(body, name, ins, outs, args, limit_mib, scratch=()):
    return pl.pallas_call(
        body,
        name=name,
        in_specs=ins,
        out_specs=[vmem() for _ in outs],
        out_shape=[jax.ShapeDtypeStruct(s, d) for s, d in outs],
        scratch_shapes=list(scratch),
        compiler_params=pltpu.CompilerParams(vmem_limit_bytes=limit_mib << 20),
    )(*args)


def three_parts(value):
    first = value.astype(BF16).astype(F32)
    rest = value - first
    second = rest.astype(BF16).astype(F32)
    return first, second, rest - second


def row_of(tokens, scal, requests):
    end = scal[1]
    passed = tokens >= end
    row = passed.astype(jnp.int32)
    prior = jnp.where(passed, end, 0)
    for r in range(1, requests):
        end = end + scal[1 + r]
        passed = tokens >= end
        row = row + passed.astype(jnp.int32)
        prior = jnp.where(passed, end, prior)
    return row, prior


def to_sublanes(lane_row):
    n = lane_row.shape[1]
    sub = lax.broadcasted_iota(jnp.int32, (n, n), 0)
    lane = lax.broadcasted_iota(jnp.int32, (n, n), 1)
    return jnp.sum(jnp.where(sub == lane, lane_row, 0), axis=1, keepdims=True)


def turn_body(requests, devices, scal, slot, cache, old_angle, new_angle, q, kv, res, *outs):
    msgs, sends, relay = outs[:CELL], outs[CELL : 2 * CELL], outs[2 * CELL]
    me = scal[0]
    pos_in_cell = me % CELL
    tok_n, width = cache.shape
    table_n = old_angle.shape[0]
    heads_here = KVH // CELL
    key_cols = heads_here * HD
    tokens = me * tok_n + lax.broadcasted_iota(jnp.int32, (tok_n, 1), 0)
    _, prior = row_of(tokens, scal, requests)
    position = jnp.clip(tokens - prior, 0, table_n - 1)
    hot = (lax.broadcasted_iota(jnp.int32, (tok_n, table_n), 1) == position).astype(F32)
    diff = new_angle[...] - old_angle[...]
    diff = jnp.concatenate([diff, diff], axis=1)
    delta = jnp.dot(hot, diff, precision=lax.Precision.HIGHEST, preferred_element_type=F32)
    cosine = jnp.cos(delta)
    lane = lax.broadcasted_iota(jnp.int32, (tok_n, HD), 1)
    sine = jnp.where(lane < HD // 2, -jnp.sin(delta), jnp.sin(delta))
    half = width // 2
    pieces = []
    for h in range(KVH):
        key = cache[:, h * HD : (h + 1) * HD].astype(F32)
        pieces.append((key * cosine + pltpu.roll(key, HD // 2, 1) * sine).astype(BF16))
    turned = jnp.concatenate(pieces + [cache[:, half:]], axis=1)
    for k in range(CELL):
        peer = pos_in_cell ^ k
        for g in range(CELL):

            @pl.when(peer == g)
            def _():
                sends[k][:, :key_cols] = turned[:, g * key_cols : (g + 1) * key_cols]
                sends[k][:, key_cols:] = turned[:, half + g * key_cols : half + (g + 1) * key_cols]
                wide = q.shape[1] // CELL
                msgs[k][:, :wide] = q[:, g * wide : (g + 1) * wide]
                msgs[k][:, wide : wide + key_cols] = kv[:, g * key_cols : (g + 1) * key_cols]
                msgs[k][:, wide + key_cols : wide + 2 * key_cols] = kv[
                    :, half + g * key_cols : half + (g + 1) * key_cols
                ]
                msgs[k][:, wide + 2 * key_cols :] = res[:, g * wide : (g + 1) * wide]

    place = slot[...]
    per_peer = tok_n // devices
    lanes = lax.broadcasted_iota(jnp.int32, (1, tok_n), 1)
    target = jnp.where(place >= 0, place // CTOK_DEV, lanes // per_peer)
    landing = jnp.where(place >= 0, place % CTOK_DEV, -1)
    target_s = to_sublanes(target)
    sub2 = lax.broadcasted_iota(jnp.int32, (tok_n, tok_n), 0)
    lane2 = lax.broadcasted_iota(jnp.int32, (tok_n, tok_n), 1)
    ahead = ((target_s == target) & (sub2 < lane2)).astype(jnp.int32)
    rank = jnp.sum(ahead, axis=0, keepdims=True)
    pick = sub2 == (target * per_peer + rank)
    moved = jnp.dot(pick.astype(BF16), turned, preferred_element_type=F32)
    relay[:, :width] = moved.astype(BF16)
    land_s = jnp.sum(jnp.where(pick, landing, 0), axis=1, keepdims=True)
    relay[:, width:] = jnp.broadcast_to(land_s.astype(F32), (tok_n, EXTRA)).astype(BF16)


def place_body(got, out):
    width = out.shape[1]
    rows = got.shape[0]
    land = got[:, width:].astype(F32)[:, :CTOK_DEV]
    want = lax.broadcasted_iota(jnp.int32, (rows, CTOK_DEV), 1).astype(F32)
    pick = (land == want).astype(BF16)
    out[...] = lax.dot_general(
        pick, got[:, :width], (((0,), (0,)), ((), ())), preferred_element_type=F32
    ).astype(BF16)


def scores_body(requests, planes, scal, *refs):
    qs, kvs, outs = refs[:planes], refs[planes : planes + CELL], refs[planes + CELL :]
    me = scal[0]
    plane, pos_in_cell = me // CELL, me % CELL
    rows = qs[0].shape[0]
    tok_n, both = kvs[0].shape
    key_cols = both // 2
    heads_here = key_cols // HD
    group = QH // KVH
    all_rows = rows * planes
    query = jnp.concatenate([r[...].astype(F32) for r in qs], axis=0).astype(BF16)
    token_rows = []
    for k in range(CELL):
        base = (plane * CELL + (pos_in_cell ^ k)) * tok_n
        tokens = base + lax.broadcasted_iota(jnp.int32, (1, tok_n), 1)
        token_rows.append(row_of(tokens, scal, requests)[0])
    token_row = jnp.concatenate(token_rows, axis=1)
    index = lax.broadcasted_iota(jnp.int32, (group * all_rows, 1), 0)
    query_row = ((index // rows) % planes) ^ plane
    matching = query_row == token_row
    lane = lax.broadcasted_iota(jnp.int32, (all_rows, EXTRA), 1)
    extra = jnp.zeros((all_rows, EXTRA), F32)
    count = heads_here * group
    scale = 1.0 / float(HD) ** 0.5
    for j in range(heads_here):
        keys = jnp.concatenate([r[:, j * HD : (j + 1) * HD] for r in kvs], axis=0)
        values = jnp.concatenate(
            [r[:, key_cols + j * HD : key_cols + (j + 1) * HD] for r in kvs], axis=0
        )
        stacked = jnp.concatenate(
            [query[:, (j * group + g) * HD : (j * group + g + 1) * HD] for g in range(group)],
            axis=0,
        )
        scores = (
            lax.dot_general(stacked, keys, (((1,), (1,)), ((), ())), preferred_element_type=F32)
            * scale
        )
        top = jnp.max(jnp.where(matching, scores, -1e30), axis=1, keepdims=True)
        weights = jnp.where(matching, jnp.exp(scores - top), 0.0)
        total = jnp.sum(weights, axis=1, keepdims=True)
        high = weights.astype(BF16)
        low = (weights - high.astype(F32)).astype(BF16)
        summed = jnp.dot(high, values, preferred_element_type=F32) + jnp.dot(
            low, values, preferred_element_type=F32
        )
        mean = summed / jnp.where(total > 0, total, 1.0)
        top = jnp.where(total > 0, top, 0.0)
        tops = three_parts(top)
        totals = three_parts(total)
        for g in range(group):
            h = j * group + g
            part = slice(g * all_rows, (g + 1) * all_rows)
            for k in range(planes):
                outs[k][:, h * HD : (h + 1) * HD] = mean[
                    g * all_rows + k * rows : g * all_rows + (k + 1) * rows
                ].astype(BF16)
            for i in range(3):
                extra = jnp.where(lane == i * count + h, tops[i][part], extra)
                extra = jnp.where(lane == (3 + i) * count + h, totals[i][part], extra)
    for k in range(planes):
        outs[k][:, count * HD :] = extra[k * rows : (k + 1) * rows].astype(BF16)


def merge_body(planes, scal, *refs):
    parts, cat, gain, norm_out, h_out = refs[:planes], *refs[planes:]
    rows = cat.shape[0]
    wide = norm_out.shape[1] - EXTRA
    count = wide // HD
    group = QH // KVH
    heads_here = count // group
    key_cols = heads_here * HD
    scale = 1.0 / float(HD) ** 0.5
    lane = lax.broadcasted_iota(jnp.int32, (rows, EXTRA), 1)
    odd = lax.broadcasted_iota(jnp.int32, (rows, 1), 0) % 2 == 1
    fresh = cat[:, wide : wide + 2 * key_cols].astype(F32)
    before = pltpu.roll(fresh, 1, 0)
    score_self = jnp.zeros((rows, EXTRA), F32)
    score_before = jnp.zeros((rows, EXTRA), F32)
    for h in range(count):
        j = h // group
        query = cat[:, h * HD : (h + 1) * HD].astype(F32)
        one = jnp.sum(query * fresh[:, j * HD : (j + 1) * HD], axis=1, keepdims=True) * scale
        two = jnp.sum(query * before[:, j * HD : (j + 1) * HD], axis=1, keepdims=True) * scale
        score_self = jnp.where(lane == h, one, score_self)
        score_before = jnp.where(lane == h, two, score_before)
    tops, totals = [], []
    for part in parts:
        extra = part[:, wide:].astype(F32)
        shifted = [extra] + [pltpu.roll(extra, EXTRA - i * count, 1) for i in range(1, 6)]
        tops.append(shifted[0] + shifted[1] + shifted[2])
        totals.append(shifted[3] + shifted[4] + shifted[5])
    highest = jnp.where(odd, jnp.maximum(score_self, score_before), score_self)
    for top, total in zip(tops, totals):
        highest = jnp.where(total > 0, jnp.maximum(highest, top), highest)
    shares = [
        jnp.where(total > 0, total * jnp.exp(jnp.where(total > 0, top, highest) - highest), 0.0)
        for top, total in zip(tops, totals)
    ]
    share_self = jnp.exp(score_self - highest)
    share_before = jnp.where(odd, jnp.exp(score_before - highest), 0.0)
    whole = share_self + share_before
    for share in shares:
        whole = whole + share
    squares = jnp.zeros((rows, 1), F32)
    for h in range(count):
        j = h // group
        value = slice(key_cols + j * HD, key_cols + (j + 1) * HD)
        here = slice(h * HD, (h + 1) * HD)
        attn = share_self[:, h : h + 1] * fresh[:, value]
        attn = attn + share_before[:, h : h + 1] * before[:, value]
        for part, share in zip(parts, shares):
            attn = attn + share[:, h : h + 1] * part[:, here].astype(F32)
        attn = attn / whole[:, h : h + 1]
        base = wide + 2 * key_cols + h * HD
        state = cat[:, base : base + HD].astype(F32) + attn
        h_out[:, here] = state
        squares = squares + jnp.sum(state * state, axis=1, keepdims=True)
        norm_out[:, here] = (state * gain[:, here].astype(F32)).astype(BF16)
    pieces = three_parts(squares)
    extra = jnp.zeros((rows, EXTRA), F32)
    for i in range(3):
        extra = jnp.where(lane == i, pieces[i], extra)
    norm_out[:, wide:] = extra.astype(BF16)


GU_ROWS = 512
DOWN_ROWS = 256


def stream(copies, depth):
    for c in copies[:depth]:
        c.start()

    def ready(i):
        copies[i].wait()

    def freed(i):
        if i + depth < len(copies):
            copies[i + depth].start()

    return ready, freed


def gate_up_copies(slices, w_gate, w_up, buf, sem, wide, start=0):
    copies = []
    for first_row in slices:
        for i in range(wide // GU_ROWS):
            for w in (w_gate, w_up):
                slot = len(copies) % buf.shape[0]
                rows = pl.ds(pl.multiple_of(first_row + i * GU_ROWS, GU_ROWS), GU_ROWS)
                copies.append(pltpu.make_async_copy(w.at[rows, :], buf.at[slot], sem.at[slot]))
    return copies


def first_gate_up_body(flip, has_acc, scal, *refs):
    if has_acc:
        x, acc_in, w_gate, w_up, acc_out, buf, sem = refs
    else:
        x, w_gate, w_up, acc_out, buf, sem = refs
    wide = x.shape[1] - EXTRA
    ff = w_gate.shape[1]
    pos = (scal[0] % CELL) ^ flip
    copies = gate_up_copies([pos * wide], w_gate, w_up, buf, sem, wide)
    ready, freed = stream(copies, buf.shape[0])
    for i in range(len(copies)):
        ready(i)
        k = i // 2
        cols = slice((i % 2) * ff, (i % 2 + 1) * ff)
        part = jnp.dot(
            x[:, k * GU_ROWS : (k + 1) * GU_ROWS],
            buf[i % buf.shape[0]],
            preferred_element_type=F32,
        )
        if k == 0:
            acc_out[:, cols] = acc_in[:, cols] + part if has_acc else part
        else:
            acc_out[:, cols] += part
        freed(i)


def rest_body(scal, own, xs, near, far, acc_in, h, w_gate, w_up, w_down, send, keep, *scratch):
    acc, out, buf, sem, dbuf, dsem = scratch
    wide = near.shape[1] - EXTRA
    ff = w_gate.shape[1]
    me = scal[0]
    pos = me % CELL
    depth = buf.shape[0]
    copies = gate_up_copies([(pos ^ 1) * wide, (pos ^ 3) * wide], w_gate, w_up, buf, sem, wide)
    downs = []
    for i in range(ff // DOWN_ROWS):
        slot = i % dbuf.shape[0]
        downs.append(
            pltpu.make_async_copy(
                w_down.at[pl.ds(i * DOWN_ROWS, DOWN_ROWS), :], dbuf.at[slot], dsem.at[slot]
            )
        )
    order = copies + downs
    ready, freed = stream(order, depth)
    for i in range(len(copies)):
        ready(i)
        k = i // 2
        per = wide // GU_ROWS
        x = near if k < per else far
        k = k % per
        cols = slice((i % 2) * ff, (i % 2 + 1) * ff)
        part = jnp.dot(
            x[:, k * GU_ROWS : (k + 1) * GU_ROWS], buf[i % depth], preferred_element_type=F32
        )
        if i < 2:
            acc[:, cols] = acc_in[:, cols] + part
        else:
            acc[:, cols] += part
        freed(i)
    squares = jnp.zeros((near.shape[0], 1), F32)
    for x in (own, xs, near, far):
        extra = x[:, wide : wide + EXTRA].astype(F32)
        squares = squares + extra[:, 0:1] + extra[:, 1:2] + extra[:, 2:3]
    inv = lax.rsqrt(squares / float(wide * CELL) + 1e-05)
    gate = acc[:, :ff] * inv
    hidden = gate / (1.0 + jnp.exp(-gate)) * (acc[:, ff:] * inv)
    planes = near.shape[0] // (2 * CELL)
    hidden = jnp.concatenate(
        [
            hidden[k * 2 * CELL + a * 2 : k * 2 * CELL + a * 2 + 2]
            for a in (0, 2, 1, 3)
            for k in range(planes)
        ],
        axis=0,
    ).astype(BF16)
    for i in range(len(downs)):
        ready(len(copies) + i)
        part = jnp.dot(
            hidden[:, i * DOWN_ROWS : (i + 1) * DOWN_ROWS],
            dbuf[i % dbuf.shape[0]],
            preferred_element_type=F32,
        )
        if i == 0:
            out[...] = part
        else:
            out[...] += part
        freed(len(copies) + i)
    per = 2 * planes
    for g in range(CELL):

        @pl.when(pos == g)
        def _():
            cols = slice(g * wide, (g + 1) * wide)
            for n, a in enumerate((0, 2, 1, 3)):
                out[n * per : n * per + 2, cols] += h[2 * a : 2 * a + 2]

    half = 2 * per
    other = jnp.where(pos % 2 == 0, out[half:], out[:half])
    mine = jnp.where(pos % 2 == 0, out[:half], out[half:])
    send[...] = other.astype(BF16)
    keep[...] = mine


def halve_body(scal, mine, got, send, keep):
    total = mine[...] + got[...].astype(F32)
    half = total.shape[0] // 2
    low = (scal[0] % CELL) // 2 == 0
    send[...] = jnp.where(low, total[half:], total[:half]).astype(BF16)
    keep[...] = jnp.where(low, total[:half], total[half:])


def spread_body(planes, mine, got, *outs):
    total = mine[...] + got[...].astype(F32)
    outs[0][...] = total[0:2]
    for k in range(1, planes):
        outs[k][...] = total[2 * k : 2 * k + 2].astype(BF16)


def final_body(mine, *refs):
    total = mine[...]
    for r in refs[:-1]:
        total = total + r[...].astype(F32)
    refs[-1][...] = total.astype(BF16)


def swap(x, k, devices):
    return lax.ppermute(x, "ctx", [(i, i ^ k) for i in range(devices)])


def cells_program(
    old_cache,
    new_slot,
    lengths,
    old_angle,
    new_angle,
    queries,
    new_kv,
    resid,
    gain,
    w_gate,
    w_up,
    w_down,
):
    devices = lax.axis_size("ctx")
    planes = devices // CELL
    me = lax.axis_index("ctx").astype(jnp.int32)
    pos = me % CELL
    tok_n, width = old_cache.shape
    requests = lengths.shape[0]
    rows_dev, model = queries.shape
    wide = model // CELL
    key_cols = KVH // CELL * HD
    msg_cols = 2 * wide + 2 * key_cols
    cell_rows = rows_dev * CELL
    all_rows = cell_rows * planes
    ff = w_gate.shape[1]
    scal = jnp.concatenate([me[None], lengths])
    turned = call(
        lambda *r: turn_body(requests, devices, *r),
        "turn",
        [smem()] + [vmem()] * 7,
        [((rows_dev, msg_cols), BF16)] * CELL
        + [((tok_n, 2 * key_cols), BF16)] * CELL
        + [((tok_n, width + EXTRA), BF16)],
        (scal, new_slot[None, :], old_cache, old_angle, new_angle, queries, new_kv, resid),
        32,
    )
    msgs, sends, relay = turned[:CELL], turned[CELL : 2 * CELL], turned[2 * CELL]
    msgs = [msgs[0]] + [swap(msgs[k], k, devices) for k in range(1, CELL)]
    kvs = [sends[0]] + [swap(sends[k], k, devices) for k in range(1, CELL)]
    for bit in (1, 2):
        flip = (pos & bit) != 0
        msgs = [jnp.where(flip, msgs[a ^ bit], msgs[a]) for a in range(CELL)]
    cat = jnp.concatenate(msgs, axis=0)
    own_q = cat[:, :wide]
    qs = [own_q] + [swap(own_q, CELL * k, devices) for k in range(1, planes)]
    parts = call(
        lambda *r: scores_body(requests, planes, *r),
        "scores",
        [smem()] + [vmem()] * (planes + CELL),
        [((cell_rows, wide + EXTRA), BF16)] * planes,
        (scal, *qs, *kvs),
        32,
    )
    parts = [parts[0]] + [swap(parts[k], CELL * k, devices) for k in range(1, planes)]
    own_gain = lax.dynamic_slice(gain, (pos * wide,), (wide,))[None, :]
    normed, hstate = call(
        lambda *r: merge_body(planes, *r),
        "merge",
        [smem()] + [vmem()] * (planes + 2),
        [((cell_rows, wide + EXTRA), BF16), ((cell_rows, wide), F32)],
        (scal, *parts, cat, own_gain),
        16,
    )
    blocks = [normed] + [swap(normed, CELL * k, devices) for k in range(1, planes)]
    own = jnp.concatenate(blocks, axis=0)
    across = swap(own, 2, devices)
    gu_scratch = [pltpu.VMEM((8, GU_ROWS, ff), BF16), pltpu.SemaphoreType.DMA((8,))]
    acc = call(
        lambda *r: first_gate_up_body(0, False, *r),
        "gate_up_own",
        [smem(), vmem(), hbm(), hbm()],
        [((all_rows, 2 * ff), F32)],
        (scal, own, w_gate, w_up),
        24,
        gu_scratch,
    )[0]
    near = swap(own, 1, devices)
    far = swap(across, 1, devices)
    acc = call(
        lambda *r: first_gate_up_body(2, True, *r),
        "gate_up_x",
        [smem(), vmem(), vmem(), hbm(), hbm()],
        [((all_rows, 2 * ff), F32)],
        (scal, across, acc, w_gate, w_up),
        24,
        gu_scratch,
    )[0]
    got_relay = lax.all_to_all(
        relay.reshape(devices, tok_n // devices, width + EXTRA),
        "ctx",
        split_axis=0,
        concat_axis=0,
        tiled=True,
    ).reshape(tok_n, width + EXTRA)
    send, keep = call(
        rest_body,
        "rest",
        [smem()] + [vmem()] * 6 + [hbm()] * 3,
        [((all_rows // 2, model), BF16), ((all_rows // 2, model), F32)],
        (scal, own, across, near, far, acc, hstate, w_gate, w_up, w_down),
        56,
        [
            pltpu.VMEM((all_rows, 2 * ff), F32),
            pltpu.VMEM((all_rows, model), F32),
            pltpu.VMEM((8, GU_ROWS, ff), BF16),
            pltpu.SemaphoreType.DMA((8,)),
            pltpu.VMEM((ff // DOWN_ROWS, DOWN_ROWS, model), BF16),
            pltpu.SemaphoreType.DMA((ff // DOWN_ROWS,)),
        ],
    )
    got = swap(send, 1, devices)
    send, keep = call(
        halve_body,
        "halve",
        [smem(), vmem(), vmem()],
        [((all_rows // 4, model), BF16), ((all_rows // 4, model), F32)],
        (scal, keep, got),
        16,
    )
    got = swap(send, 2, devices)
    pieces = call(
        lambda *r: spread_body(planes, *r),
        "spread",
        [vmem(), vmem()],
        [((rows_dev, model), F32)] + [((rows_dev, model), BF16)] * (planes - 1),
        (keep, got),
        16,
    )
    pieces = [pieces[0]] + [swap(pieces[k], CELL * k, devices) for k in range(1, planes)]
    layer_out = call(
        final_body,
        "final",
        [vmem()] * planes,
        [((rows_dev, model), BF16)],
        tuple(pieces),
        16,
    )[0]
    new_cache = call(
        place_body,
        "place",
        [vmem()],
        [((CTOK_DEV, width), BF16)],
        (got_relay,),
        16,
    )[0]
    return (new_cache, layer_out)


def rotate_block(block, where_pos, old_angle, new_angle):
    rows_here = block.shape[0]
    half_size = HD // 2
    parts = block.reshape(rows_here, 2, KVH, HD)
    keys = parts[:, 0].astype(jnp.float32)
    delta = jnp.take(new_angle, where_pos, axis=0) - jnp.take(old_angle, where_pos, axis=0)
    cosine = jnp.cos(delta)[:, None, :]
    sine = jnp.sin(delta)[:, None, :]
    first = keys[..., :half_size]
    second = keys[..., half_size:]
    turned = jnp.concatenate(
        [first * cosine - second * sine, second * cosine + first * sine], axis=-1
    ).astype(jnp.bfloat16)
    return jnp.stack([turned, parts[:, 1]], axis=1).reshape(rows_here, 2 * KVH * HD)


def general_program(
    old_cache,
    new_slot,
    lengths,
    old_angle,
    new_angle,
    queries,
    new_kv,
    resid,
    gain,
    w_gate,
    w_up,
    w_down,
):
    devices = lax.axis_size("ctx")
    own_index = lax.axis_index("ctx")
    slot_count = old_cache.shape[0]
    row_width = old_cache.shape[1]
    per_peer = slot_count // devices
    rows_dev = queries.shape[0]
    all_rows = rows_dev * devices
    group_size = QH // KVH
    high = lax.Precision.HIGHEST
    scale = 1.0 / float(HD) ** 0.5
    tokens = own_index * slot_count + jnp.arange(slot_count, dtype=jnp.int32)
    row_ends = jnp.cumsum(lengths)
    passed = row_ends[None, :] <= tokens[:, None]
    owner_row = jnp.minimum(jnp.sum(passed.astype(jnp.int32), axis=1), lengths.shape[0] - 1)
    row_prior = jnp.sum(jnp.where(passed, lengths[None, :], 0), axis=1)
    position = jnp.clip(tokens - row_prior, 0, old_angle.shape[0] - 1)
    filled = new_slot >= 0
    all_queries = lax.all_gather(queries, "ctx", axis=0, tiled=True)
    target = jnp.where(
        filled, new_slot // CTOK_DEV, jnp.arange(slot_count, dtype=jnp.int32) // per_peer
    )
    sorted_order = jnp.argsort(target, stable=True)
    new_place = jnp.where(filled, new_slot % CTOK_DEV, -1)
    slot_info = jnp.stack([new_place, owner_row, position], axis=1)[sorted_order]
    sent_rows = old_cache[sorted_order].reshape(devices, per_peer, row_width)
    got_rows = lax.all_to_all(sent_rows, "ctx", split_axis=0, concat_axis=0, tiled=True)
    got_info = lax.all_to_all(
        slot_info.reshape(devices, per_peer, 3), "ctx", split_axis=0, concat_axis=0, tiled=True
    )
    got_rows = got_rows.reshape(slot_count, row_width)
    got_info = got_info.reshape(slot_count, 3)
    landing = jnp.where(got_info[:, 0] >= 0, got_info[:, 0], CTOK_DEV)
    placed = jnp.zeros((CTOK_DEV, row_width), jnp.bfloat16).at[landing].set(got_rows, mode="drop")
    placed_row = jnp.zeros((CTOK_DEV,), jnp.int32).at[landing].set(got_info[:, 1], mode="drop")
    placed_pos = jnp.zeros((CTOK_DEV,), jnp.int32).at[landing].set(got_info[:, 2], mode="drop")
    placed, moved_row, moved_pos = (placed, placed_row, placed_pos)
    new_cache = rotate_block(placed, moved_pos, old_angle, new_angle)
    key_count = new_cache.shape[0]
    key_split = new_cache.reshape(key_count, 2, KVH, HD)
    value_four = key_split[:, 1].astype(jnp.float32)
    query_four = all_queries.reshape(all_rows, KVH, group_size, HD)
    scores = (
        jnp.einsum(
            "mjge,cje->mjgc", query_four, key_split[:, 0], preferred_element_type=jnp.float32
        )
        * scale
    )
    query_row = jnp.arange(all_rows, dtype=jnp.int32) // (2 * SAMPLES)
    matching = query_row[:, None] == moved_row[None, :]
    scores = jnp.where(matching[:, None, None, :], scores, -1e30)
    local_top = jnp.max(scores, axis=-1)
    own_query = queries.reshape(rows_dev, KVH, group_size, HD).astype(jnp.float32)
    fresh_kv = jnp.repeat(new_kv.reshape(rows_dev // 2, 2, 2, KVH, HD), 2, axis=0).astype(
        jnp.float32
    )
    own_steps = (
        jnp.arange(2, dtype=jnp.int32)[None, :]
        <= (jnp.arange(rows_dev, dtype=jnp.int32) % 2)[:, None]
    )
    own_scores = jnp.einsum("mjge,msje->mjgs", own_query, fresh_kv[:, :, 0], precision=high) * scale
    own_scores = jnp.where(own_steps[:, None, None, :], own_scores, -1e30)
    own_top = jnp.max(own_scores, axis=-1)
    floor_top = jnp.maximum(local_top, -10000.0)
    weights_local = jnp.exp(scores - floor_top[..., None])
    summed = jnp.einsum("mjgc,cje->mjge", weights_local, value_four, precision=high)
    totals = jnp.sum(weights_local, axis=-1)
    got_sums, got_totals, got_tops = (
        lax.all_to_all(
            summed.reshape(devices, rows_dev, QH * HD),
            "ctx",
            split_axis=0,
            concat_axis=0,
            tiled=True,
        ),
        lax.all_to_all(
            totals.reshape(devices, rows_dev, QH), "ctx", split_axis=0, concat_axis=0, tiled=True
        ),
        lax.all_to_all(
            floor_top.reshape(devices, rows_dev, QH), "ctx", split_axis=0, concat_axis=0, tiled=True
        ),
    )
    got_tops = got_tops.reshape(devices, rows_dev, KVH, group_size)
    row_top = jnp.maximum(jnp.max(got_tops, axis=0), own_top)
    rescale = jnp.exp(got_tops - row_top[None])
    weights_own = jnp.exp(own_scores - row_top[..., None])
    row_sums = jnp.sum(
        rescale[..., None] * got_sums.reshape(devices, rows_dev, KVH, group_size, HD), axis=0
    )
    row_sums = row_sums + jnp.einsum(
        "mjgs,msje->mjge", weights_own, fresh_kv[:, :, 1], precision=high
    )
    row_totals = jnp.sum(
        rescale * got_totals.reshape(devices, rows_dev, KVH, group_size), axis=0
    ) + jnp.sum(weights_own, axis=-1)
    attn = (row_sums / row_totals[..., None]).reshape(rows_dev, QH * HD)
    hstate = resid.astype(jnp.float32) + attn
    normed = (
        hstate
        * lax.rsqrt(jnp.mean(hstate * hstate, axis=-1, keepdims=True) + 1e-05)
        * gain.astype(jnp.float32)
    ).astype(jnp.bfloat16)
    piece = lax.all_gather(normed, "ctx", axis=0, tiled=True)
    gate_out = jnp.dot(piece, w_gate, preferred_element_type=jnp.float32)
    up_out = jnp.dot(piece, w_up, preferred_element_type=jnp.float32)
    hidden_all = (jax.nn.silu(gate_out) * up_out).astype(jnp.bfloat16)
    ffn_out = lax.psum_scatter(
        jnp.dot(hidden_all, w_down, preferred_element_type=jnp.float32),
        "ctx",
        scatter_dimension=0,
        tiled=True,
    )
    layer_out = (hstate + ffn_out).astype(jnp.bfloat16)
    return (new_cache, layer_out)


def solution(mesh):
    per_device = cells_program if mesh.shape["ctx"] == 4 * CELL else general_program
    return jax.shard_map(
        per_device,
        mesh=mesh,
        in_specs=(
            P(("groups", "ctx"), None),
            P(("groups", "ctx")),
            P("groups"),
            P(),
            P(),
            P(("groups", "ctx"), None),
            P(("groups", "ctx"), None),
            P(("groups", "ctx"), None),
            P(),
            P(None, "ctx"),
            P(None, "ctx"),
            P("ctx", None),
        ),
        out_specs=(P(("groups", "ctx"), None), P(("groups", "ctx"), None)),
        check_vma=False,
    )
```

```python
import jax
import jax.numpy as jnp
from jax import lax
from jax.experimental import pallas as pl
from jax.experimental.pallas import tpu as pltpu
from jax.sharding import PartitionSpec as P

QH = 64
KVH = 8
HD = 128
CTOK_DEV = 64
SAMPLES = 4
CELL = 4
F32 = jnp.float32
BF16 = jnp.bfloat16
EXTRA = 128


def vmem():
    return pl.BlockSpec(memory_space=pltpu.VMEM)


def smem():
    return pl.BlockSpec(memory_space=pltpu.SMEM)


def hbm():
    return pl.BlockSpec(memory_space=pl.ANY)


def in_hbm(x):
    return pltpu.with_memory_space_constraint(x, pltpu.HBM)


def in_vmem(x):
    return pltpu.with_memory_space_constraint(x, pltpu.VMEM)


def call(body, ins, outs, args, limit_mib, scratch=(), fetch=(), moved=0, on_chip=False):
    kind = pltpu.VMEM if on_chip else jax.ShapeDtypeStruct
    shapes = [kind(s, d) for s, d in outs]
    shapes += [pltpu.VMEM(piece_shape(p), BF16) for p in fetch]
    return pl.pallas_call(
        body,
        in_specs=ins,
        out_specs=[vmem() for _ in shapes],
        out_shape=shapes,
        scratch_shapes=list(scratch),
        compiler_params=pltpu.CompilerParams(vmem_limit_bytes=limit_mib << 20),
        cost_estimate=pl.CostEstimate(flops=0, transcendentals=0, bytes_accessed=moved << 20),
    )(*args)


def here():
    return lax.axis_index("ctx").astype(jnp.int32)


def three_parts(value):
    first = value.astype(BF16).astype(F32)
    rest = value - first
    second = rest.astype(BF16).astype(F32)
    return first, second, rest - second


def row_of(tokens, scal, requests):
    end = scal[0]
    passed = tokens >= end
    row = passed.astype(jnp.int32)
    prior = jnp.where(passed, end, 0)
    for r in range(1, requests):
        end = end + scal[r]
        passed = tokens >= end
        row = row + passed.astype(jnp.int32)
        prior = jnp.where(passed, end, prior)
    return row, prior


def to_sublanes(lane_row):
    n = lane_row.shape[1]
    sub = lax.broadcasted_iota(jnp.int32, (n, n), 0)
    lane = lax.broadcasted_iota(jnp.int32, (n, n), 1)
    return jnp.sum(jnp.where(sub == lane, lane_row, 0), axis=1, keepdims=True)


GU_ROWS = 512
DOWN_ROWS = 256


def piece_shape(piece):
    kind, _, n, cols = piece
    return (n * DOWN_ROWS, cols) if kind == "down" else (n, GU_ROWS, cols)


def fetch_copies(fetch, weights, pieces, sem):
    w_gate, w_up, w_down = weights
    copies = []
    for (kind, first, n, _), out in zip(fetch, pieces):
        for i in range(n):
            if kind == "down":
                src = w_down.at[pl.ds((first + i) * DOWN_ROWS, DOWN_ROWS), :]
                dst = out.at[pl.ds(i * DOWN_ROWS, DOWN_ROWS), :]
            else:
                wide = w_gate.shape[0] // CELL
                row = (here() % CELL ^ 1) * wide + (first + i) // 2 * GU_ROWS
                w = w_gate if (first + i) % 2 == 0 else w_up
                src = w.at[pl.ds(pl.multiple_of(row, GU_ROWS), GU_ROWS), :]
                dst = out.at[i]
            copies.append(pltpu.make_async_copy(src, dst, sem.at[len(copies)]))
    return copies


def count_of(fetch):
    return max(1, sum(p[2] for p in fetch))


def warm_body(fetch, dep, w_gate, w_up, w_down, *refs):
    copies = fetch_copies(fetch, (w_gate, w_up, w_down), refs[:-1], refs[-1])
    for c in copies:
        c.start()
    for c in copies:
        c.wait()


def turn_body(requests, devices, fetch, scal, *refs):
    sources, weights, refs = refs[:8], refs[8:11], refs[11:]
    outs, refs = refs[: 3 * CELL + 1], refs[3 * CELL + 1 :]
    msgs, sends, relays = outs[:CELL], outs[CELL : 2 * CELL], outs[2 * CELL : 3 * CELL]
    own_gain = outs[3 * CELL]
    pieces, refs = refs[: len(fetch)], refs[len(fetch) :]
    locals_, sems, fetch_sem = refs[:8], refs[8], refs[9]
    loads = [pltpu.make_async_copy(a, b, sems.at[i]) for i, (a, b) in enumerate(zip(sources, locals_))]
    for c in loads:
        c.start()
    fetched = fetch_copies(fetch, weights, pieces, fetch_sem)
    for c in fetched:
        c.start()
    for c in loads:
        c.wait()
    slot, cache, old_angle, new_angle, q, kv, res, gain = locals_
    me = here()
    pos_in_cell = me % CELL
    tok_n, width = cache.shape
    table_n = old_angle.shape[1]
    heads_here = KVH // CELL
    key_cols = heads_here * HD
    tokens = me * tok_n + lax.broadcasted_iota(jnp.int32, (tok_n, 1), 0)
    _, prior = row_of(tokens, scal, requests)
    position = jnp.clip(tokens - prior, 0, table_n - 1)
    hot = (lax.broadcasted_iota(jnp.int32, (tok_n, table_n), 1) == position).astype(F32)
    diff = new_angle[...] - old_angle[...]
    diff = jnp.concatenate([diff, diff], axis=0)
    delta = lax.dot_general(
        hot,
        diff,
        (((1,), (1,)), ((), ())),
        precision=lax.Precision.HIGHEST,
        preferred_element_type=F32,
    )
    cosine = jnp.cos(delta)
    lane = lax.broadcasted_iota(jnp.int32, (tok_n, HD), 1)
    sine = jnp.where(lane < HD // 2, -jnp.sin(delta), jnp.sin(delta))
    half = width // 2
    keys = []
    for h in range(KVH):
        key = cache[:, h * HD : (h + 1) * HD].astype(F32)
        keys.append((key * cosine + pltpu.roll(key, HD // 2, 1) * sine).astype(BF16))
    turned = jnp.concatenate(keys + [cache[:, half:]], axis=1)
    for k in range(CELL):
        peer = pos_in_cell ^ k
        for g in range(CELL):

            @pl.when(peer == g)
            def _():
                sends[k][:, :key_cols] = turned[:, g * key_cols : (g + 1) * key_cols]
                sends[k][:, key_cols:] = turned[:, half + g * key_cols : half + (g + 1) * key_cols]
                wide = q.shape[1] // CELL
                msgs[k][:, :wide] = q[:, g * wide : (g + 1) * wide]
                msgs[k][:, wide : wide + key_cols] = kv[:, g * key_cols : (g + 1) * key_cols]
                msgs[k][:, wide + key_cols : wide + 2 * key_cols] = kv[
                    :, half + g * key_cols : half + (g + 1) * key_cols
                ]
                msgs[k][:, wide + 2 * key_cols :] = res[:, g * wide : (g + 1) * wide]
                if k == 0:
                    own_gain[...] = gain[:, g * wide : (g + 1) * wide]

    place = slot[...]
    per_peer = tok_n // devices
    lanes = lax.broadcasted_iota(jnp.int32, (1, tok_n), 1)
    target = jnp.where(place >= 0, place // CTOK_DEV, lanes // per_peer)
    landing = jnp.where(place >= 0, place % CTOK_DEV, -1)
    target_s = to_sublanes(target)
    sub2 = lax.broadcasted_iota(jnp.int32, (tok_n, tok_n), 0)
    lane2 = lax.broadcasted_iota(jnp.int32, (tok_n, tok_n), 1)
    ahead = ((target_s == target) & (sub2 < lane2)).astype(jnp.int32)
    rank = jnp.sum(ahead, axis=0, keepdims=True)
    order = (target % CELL) * (devices // CELL) + target // CELL
    pick = sub2 == (order * per_peer + rank)
    moved = jnp.dot(pick.astype(BF16), turned, preferred_element_type=F32).astype(BF16)
    land_s = jnp.sum(jnp.where(pick, landing, 0), axis=1, keepdims=True)
    land_wide = jnp.broadcast_to(land_s.astype(F32), (tok_n, EXTRA)).astype(BF16)
    block = tok_n // CELL
    for k in range(CELL):
        for g in range(CELL):

            @pl.when((pos_in_cell ^ k) == g)
            def _():
                relays[k][:, :width] = moved[g * block : (g + 1) * block]
                relays[k][:, width:] = land_wide[g * block : (g + 1) * block]

    for c in fetched:
        c.wait()


def assemble_body(*refs):
    msgs, cat, query = refs[:CELL], refs[CELL], refs[CELL + 1]
    pos = here() % CELL
    wide = query.shape[1]
    whole = [r[...].astype(F32) for r in msgs]
    for bit in (1, 2):
        flip = (pos & bit) != 0
        whole = [jnp.where(flip, whole[a ^ bit], whole[a]) for a in range(CELL)]
    whole = jnp.concatenate(whole, axis=0).astype(BF16)
    cat[...] = whole
    query[...] = whole[:, :wide]


def place_body(*refs):
    out = refs[-1]
    got = jnp.concatenate([r[...] for r in refs[:-1]], axis=0)
    width = out.shape[1]
    rows = got.shape[0]
    land = got[:, width:].astype(F32)[:, :CTOK_DEV]
    want = lax.broadcasted_iota(jnp.int32, (rows, CTOK_DEV), 1).astype(F32)
    pick = (land == want).astype(BF16)
    out[...] = lax.dot_general(
        pick, got[:, :width], (((0,), (0,)), ((), ())), preferred_element_type=F32
    ).astype(BF16)


def scores_body(requests, planes, fetch, scal, *refs):
    qs, kvs, refs = refs[:planes], refs[planes : planes + CELL], refs[planes + CELL :]
    weights, outs, refs = refs[:3], refs[3 : 3 + planes], refs[3 + planes :]
    fetched = fetch_copies(fetch, weights, refs[: len(fetch)], refs[-1])
    for c in fetched:
        c.start()
    me = here()
    plane, pos_in_cell = me // CELL, me % CELL
    rows = qs[0].shape[0]
    tok_n, both = kvs[0].shape
    key_cols = both // 2
    heads_here = key_cols // HD
    group = QH // KVH
    all_rows = rows * planes
    query = jnp.concatenate([r[...].astype(F32) for r in qs], axis=0).astype(BF16)
    token_rows = []
    for k in range(CELL):
        base = (plane * CELL + (pos_in_cell ^ k)) * tok_n
        tokens = base + lax.broadcasted_iota(jnp.int32, (1, tok_n), 1)
        token_rows.append(row_of(tokens, scal, requests)[0])
    token_row = jnp.concatenate(token_rows, axis=1)
    index = lax.broadcasted_iota(jnp.int32, (group * all_rows, 1), 0)
    query_row = ((index // rows) % planes) ^ plane
    matching = query_row == token_row
    lane = lax.broadcasted_iota(jnp.int32, (all_rows, EXTRA), 1)
    extra = jnp.zeros((all_rows, EXTRA), F32)
    count = heads_here * group
    scale = 1.0 / float(HD) ** 0.5
    for j in range(heads_here):
        keys = jnp.concatenate([r[:, j * HD : (j + 1) * HD] for r in kvs], axis=0)
        values = jnp.concatenate(
            [r[:, key_cols + j * HD : key_cols + (j + 1) * HD] for r in kvs], axis=0
        )
        stacked = jnp.concatenate(
            [query[:, (j * group + g) * HD : (j * group + g + 1) * HD] for g in range(group)],
            axis=0,
        )
        scores = (
            lax.dot_general(stacked, keys, (((1,), (1,)), ((), ())), preferred_element_type=F32)
            * scale
        )
        top = jnp.max(jnp.where(matching, scores, -1e30), axis=1, keepdims=True)
        weights = jnp.where(matching, jnp.exp(scores - top), 0.0)
        total = jnp.sum(weights, axis=1, keepdims=True)
        high = weights.astype(BF16)
        low = (weights - high.astype(F32)).astype(BF16)
        summed = jnp.dot(high, values, preferred_element_type=F32) + jnp.dot(
            low, values, preferred_element_type=F32
        )
        mean = summed / jnp.where(total > 0, total, 1.0)
        top = jnp.where(total > 0, top, 0.0)
        tops = three_parts(top)
        totals = three_parts(total)
        for g in range(group):
            h = j * group + g
            part = slice(g * all_rows, (g + 1) * all_rows)
            for k in range(planes):
                outs[k][:, h * HD : (h + 1) * HD] = mean[
                    g * all_rows + k * rows : g * all_rows + (k + 1) * rows
                ].astype(BF16)
            for i in range(3):
                extra = jnp.where(lane == i * count + h, tops[i][part], extra)
                extra = jnp.where(lane == (3 + i) * count + h, totals[i][part], extra)
    for k in range(planes):
        outs[k][:, count * HD :] = extra[k * rows : (k + 1) * rows].astype(BF16)
    for c in fetched:
        c.wait()


def merge_body(planes, fetch, *refs):
    parts, cat, gain, refs = refs[:planes], *refs[planes : planes + 2], refs[planes + 2 :]
    moved, weights, refs = refs[:CELL], refs[CELL : CELL + 3], refs[CELL + 3 :]
    norm_out, h_out, regrouped, refs = *refs[:2], refs[2 : 2 + planes], refs[2 + planes :]
    fetched = fetch_copies(fetch, weights, refs[: len(fetch)], refs[-1])
    for c in fetched:
        c.start()
    rows = cat.shape[0]
    wide = norm_out.shape[1] - EXTRA
    count = wide // HD
    group = QH // KVH
    heads_here = count // group
    key_cols = heads_here * HD
    scale = 1.0 / float(HD) ** 0.5
    lane = lax.broadcasted_iota(jnp.int32, (rows, EXTRA), 1)
    odd = lax.broadcasted_iota(jnp.int32, (rows, 1), 0) % 2 == 1
    fresh = cat[:, wide : wide + 2 * key_cols].astype(F32)
    before = pltpu.roll(fresh, 1, 0)
    score_self = jnp.zeros((rows, EXTRA), F32)
    score_before = jnp.zeros((rows, EXTRA), F32)
    for h in range(count):
        j = h // group
        query = cat[:, h * HD : (h + 1) * HD].astype(F32)
        one = jnp.sum(query * fresh[:, j * HD : (j + 1) * HD], axis=1, keepdims=True) * scale
        two = jnp.sum(query * before[:, j * HD : (j + 1) * HD], axis=1, keepdims=True) * scale
        score_self = jnp.where(lane == h, one, score_self)
        score_before = jnp.where(lane == h, two, score_before)
    tops, totals = [], []
    for part in parts:
        extra = part[:, wide:].astype(F32)
        shifted = [extra] + [pltpu.roll(extra, EXTRA - i * count, 1) for i in range(1, 6)]
        tops.append(shifted[0] + shifted[1] + shifted[2])
        totals.append(shifted[3] + shifted[4] + shifted[5])
    highest = jnp.where(odd, jnp.maximum(score_self, score_before), score_self)
    for top, total in zip(tops, totals):
        highest = jnp.where(total > 0, jnp.maximum(highest, top), highest)
    shares = [
        jnp.where(total > 0, total * jnp.exp(jnp.where(total > 0, top, highest) - highest), 0.0)
        for top, total in zip(tops, totals)
    ]
    share_self = jnp.exp(score_self - highest)
    share_before = jnp.where(odd, jnp.exp(score_before - highest), 0.0)
    whole = share_self + share_before
    for share in shares:
        whole = whole + share
    squares = jnp.zeros((rows, 1), F32)
    for h in range(count):
        j = h // group
        value = slice(key_cols + j * HD, key_cols + (j + 1) * HD)
        lanes = slice(h * HD, (h + 1) * HD)
        attn = share_self[:, h : h + 1] * fresh[:, value]
        attn = attn + share_before[:, h : h + 1] * before[:, value]
        for part, share in zip(parts, shares):
            attn = attn + share[:, h : h + 1] * part[:, lanes].astype(F32)
        attn = attn / whole[:, h : h + 1]
        base = wide + 2 * key_cols + h * HD
        state = cat[:, base : base + HD].astype(F32) + attn
        h_out[:, lanes] = state
        squares = squares + jnp.sum(state * state, axis=1, keepdims=True)
        norm_out[:, lanes] = (state * gain[:, lanes].astype(F32)).astype(BF16)
    pieces = three_parts(squares)
    extra = jnp.zeros((rows, EXTRA), F32)
    for i in range(3):
        extra = jnp.where(lane == i, pieces[i], extra)
    norm_out[:, wide:] = extra.astype(BF16)
    plane = here() // CELL
    per = moved[0].shape[0] // planes
    for k in range(planes):
        for g in range(planes):

            @pl.when((plane ^ k) == g)
            def _():
                for a in range(CELL):
                    regrouped[k][a * per : (a + 1) * per] = moved[a][g * per : (g + 1) * per]

    for c in fetched:
        c.wait()


def stream(copies, depth):
    for c in copies[:depth]:
        c.start()

    def ready(i):
        copies[i].wait()

    def freed(i):
        if i + depth < len(copies):
            copies[i + depth].start()

    return ready, freed


def gate_up_copies(slices, w_gate, w_up, buf, sem, wide):
    copies = []
    for first_row in slices:
        for i in range(wide // GU_ROWS):
            for w in (w_gate, w_up):
                slot = len(copies) % buf.shape[0]
                rows = pl.ds(pl.multiple_of(first_row + i * GU_ROWS, GU_ROWS), GU_ROWS)
                copies.append(pltpu.make_async_copy(w.at[rows, :], buf.at[slot], sem.at[slot]))
    return copies


def first_gate_up_body(flip, has_acc, *refs):
    if has_acc:
        x, acc_in, w_gate, w_up, acc_out, buf, sem = refs
    else:
        x, w_gate, w_up, acc_out, buf, sem = refs
    wide = x.shape[1] - EXTRA
    ff = w_gate.shape[1]
    pos = (here() % CELL) ^ flip
    copies = gate_up_copies([pos * wide], w_gate, w_up, buf, sem, wide)
    ready, freed = stream(copies, buf.shape[0])
    for i in range(len(copies)):
        ready(i)
        k = i // 2
        cols = slice((i % 2) * ff, (i % 2 + 1) * ff)
        part = jnp.dot(
            x[:, k * GU_ROWS : (k + 1) * GU_ROWS],
            buf[i % buf.shape[0]],
            preferred_element_type=F32,
        )
        if k == 0:
            acc_out[:, cols] = acc_in[:, cols] + part if has_acc else part
        else:
            acc_out[:, cols] += part
        freed(i)


def rest_body(planes, nears, downs, own, xs, near, far, acc_in, h, *refs):
    near_refs, refs = refs[: len(nears)], refs[len(nears) :]
    down_refs, refs = refs[: len(downs)], refs[len(downs) :]
    w_gate, w_up, send, keep, acc, out, buf, sem = refs
    wide = near.shape[1] - EXTRA
    ff = w_gate.shape[1]
    me = here()
    pos = me % CELL
    depth = buf.shape[0]
    copies = gate_up_copies([(pos ^ 3) * wide], w_gate, w_up, buf, sem, wide)
    ready, freed = stream(copies, depth)
    near_w = {}
    for (_, first, n, _), r in zip(nears, near_refs):
        for i in range(n):
            near_w[first + i] = r.at[i]
    down_w = {}
    for (_, first, n, _), r in zip(downs, down_refs):
        for i in range(n):
            down_w[first + i] = r.at[pl.ds(i * DOWN_ROWS, DOWN_ROWS), :]
    for x, streamed in ((near, False), (far, True)):
        for i in range(len(copies)):
            k = i // 2
            cols = slice((i % 2) * ff, (i % 2 + 1) * ff)
            if streamed:
                ready(i)
            w = buf.at[i % depth] if streamed else near_w[i]
            part = jnp.dot(
                x[:, k * GU_ROWS : (k + 1) * GU_ROWS], w[...], preferred_element_type=F32
            )
            if i < 2 and not streamed:
                acc[:, cols] = acc_in[:, cols] + part
            else:
                acc[:, cols] += part
            if streamed:
                freed(i)
    squares = jnp.zeros((near.shape[0], 1), F32)
    for x in (own, xs, near, far):
        extra = x[:, wide : wide + EXTRA].astype(F32)
        squares = squares + extra[:, 0:1] + extra[:, 1:2] + extra[:, 2:3]
    inv = lax.rsqrt(squares / float(wide * CELL) + 1e-05)
    gate = acc[:, :ff] * inv
    hidden = gate / (1.0 + jnp.exp(-gate)) * (acc[:, ff:] * inv)
    hidden = jnp.concatenate(
        [
            hidden[k * 2 * CELL + a * 2 : k * 2 * CELL + a * 2 + 2]
            for a in (0, 2, 1, 3)
            for k in range(planes)
        ],
        axis=0,
    ).astype(BF16)
    for i in range(ff // DOWN_ROWS):
        part = jnp.dot(
            hidden[:, i * DOWN_ROWS : (i + 1) * DOWN_ROWS],
            down_w[i][...],
            preferred_element_type=F32,
        )
        if i == 0:
            out[...] = part
        else:
            out[...] += part
    per = 2 * planes
    for g in range(CELL):

        @pl.when(pos == g)
        def _():
            cols = slice(g * wide, (g + 1) * wide)
            for n, a in enumerate((0, 2, 1, 3)):
                out[n * per : n * per + 2, cols] += h[2 * a : 2 * a + 2]

    half = 2 * per
    other = jnp.where(pos % 2 == 0, out[half:], out[:half])
    mine = jnp.where(pos % 2 == 0, out[:half], out[half:])
    send[...] = other
    keep[...] = mine


def halve_body(mine, got, send, send_low, keep):
    total = mine[...] + got[...]
    half = total.shape[0] // 2
    low = (here() % CELL) // 2 == 0
    other = jnp.where(low, total[half:], total[:half])
    high = other.astype(BF16)
    send[...] = high
    send_low[...] = (other[:2] - high[:2].astype(F32)).astype(BF16)
    keep[...] = jnp.where(low, total[:half], total[half:])


def spread_body(planes, mine, got, got_low, *outs):
    total = mine[...] + got[...].astype(F32)
    outs[0][...] = total[0:2] + got_low[...].astype(F32)
    for k in range(1, planes):
        outs[k][...] = total[2 * k : 2 * k + 2].astype(BF16)


def final_body(mine, *refs):
    total = mine[...]
    for r in refs[:-1]:
        total = total + r[...].astype(F32)
    refs[-1][...] = total.astype(BF16)


def swap(x, k, devices):
    return lax.ppermute(x, "ctx", [(i, i ^ k) for i in range(devices)])


def cells_program(*args):
    return cells_steps(*args)


def cells_steps(
    old_cache,
    new_slot,
    lengths,
    old_angle,
    new_angle,
    queries,
    new_kv,
    resid,
    gain,
    w_gate,
    w_up,
    w_down,
):
    devices = lax.axis_size("ctx")
    planes = devices // CELL
    tok_n, width = old_cache.shape
    requests = lengths.shape[0]
    rows_dev, model = queries.shape
    wide = model // CELL
    key_cols = KVH // CELL * HD
    msg_cols = 2 * wide + 2 * key_cols
    cell_rows = rows_dev * CELL
    all_rows = cell_rows * planes
    ff = w_gate.shape[1]
    w_gate, w_up, w_down = in_hbm(w_gate), in_hbm(w_up), in_hbm(w_down)
    weights = (w_gate, w_up, w_down)
    n_down = ff // DOWN_ROWS
    n_near = 2 * wide // GU_ROWS
    plans = {
        "turn": [("down", 0, 2, model)],
        "warm_q": [("down", 2, 3, model)],
        "scores": [("down", 5, 1, model)],
        "warm_p": [("near", 0, 4, ff)],
        "merge": [("down", 6, n_down - 6, model)],
        "warm_z": [("near", 4, n_near - 4, ff)],
    }
    held = []

    def keep_pieces(name, values):
        held.extend(zip(plans[name], values))

    def warm(name, dep):
        plan = plans[name]
        keep_pieces(
            name,
            call(
                lambda *r: warm_body(plan, *r),
                [hbm()] * 4,
                [],
                (dep, *weights),
                1,
                [pltpu.SemaphoreType.DMA((count_of(plan),))],
                plan,
                8,
            ),
        )

    sources = (
        new_slot[None, :],
        old_cache,
        old_angle.T,
        new_angle.T,
        queries,
        new_kv,
        resid,
        gain[None, :],
    )
    plan = plans["turn"]
    turned = call(
        lambda *r: turn_body(requests, devices, plan, *r),
        [smem()] + [hbm()] * 11,
        [((rows_dev, msg_cols), BF16)] * CELL
        + [((tok_n, 2 * key_cols), BF16)] * CELL
        + [((tok_n // CELL, width + EXTRA), BF16)] * CELL
        + [((1, wide), BF16)],
        (lengths, *[in_hbm(x) for x in sources], *weights),
        10,
        [pltpu.VMEM(x.shape, x.dtype) for x in sources]
        + [pltpu.SemaphoreType.DMA((len(sources),)), pltpu.SemaphoreType.DMA((count_of(plan),))],
        plan,
        8,
    )
    msgs, sends = turned[:CELL], turned[CELL : 2 * CELL]
    relays, own_gain = turned[2 * CELL : 3 * CELL], turned[3 * CELL]
    keep_pieces("turn", turned[3 * CELL + 1 :])
    msgs = [msgs[0]] + [swap(msgs[k], k, devices) for k in range(1, CELL)]
    kvs = [sends[0]] + [swap(sends[k], k, devices) for k in range(1, CELL)]
    cat, own_q = call(
        assemble_body,
        [vmem()] * CELL,
        [((cell_rows, msg_cols), BF16), ((cell_rows, wide), BF16)],
        tuple(msgs),
        4,
    )
    qs = [own_q] + [swap(own_q, CELL * k, devices) for k in range(1, planes)]
    warm("warm_q", own_q)
    relays = [relays[0]] + [swap(relays[k], k, devices) for k in range(1, CELL)]
    plan = plans["scores"]
    parts = call(
        lambda *r: scores_body(requests, planes, plan, *r),
        [smem()] + [vmem()] * (planes + CELL) + [hbm()] * 3,
        [((cell_rows, wide + EXTRA), BF16)] * planes,
        (lengths, *qs, *kvs, *weights),
        10,
        [pltpu.SemaphoreType.DMA((count_of(plan),))],
        plan,
        5,
    )
    keep_pieces("scores", parts[planes:])
    warm("warm_p", parts[0])
    parts = [parts[0]] + [swap(parts[k], CELL * k, devices) for k in range(1, planes)]
    plan = plans["merge"]
    merged = call(
        lambda *r: merge_body(planes, plan, *r),
        [vmem()] * (planes + 2 + CELL) + [hbm()] * 3,
        [((cell_rows, wide + EXTRA), BF16), ((cell_rows, wide), F32)]
        + [((tok_n // planes, width + EXTRA), BF16)] * planes,
        (*parts, cat, own_gain, *relays, *weights),
        6,
        [pltpu.SemaphoreType.DMA((count_of(plan),))],
        plan,
        4,
    )
    normed, hstate = merged[:2]
    relays = merged[2 : 2 + planes]
    keep_pieces("merge", merged[2 + planes :])
    warm("warm_z", normed)
    blocks = [normed] + [swap(normed, CELL * k, devices) for k in range(1, planes)]
    own = jnp.concatenate(blocks, axis=0)
    across = swap(own, 2, devices)
    near = swap(own, 1, devices)
    gu_scratch = [pltpu.VMEM((4, GU_ROWS, ff), BF16), pltpu.SemaphoreType.DMA((4,))]
    acc = call(
        lambda *r: first_gate_up_body(0, False, *r),
        [vmem(), hbm(), hbm()],
        [((all_rows, 2 * ff), F32)],
        (own, w_gate, w_up),
        9,
        gu_scratch,
        moved=14,
    )[0]
    far = swap(across, 1, devices)
    acc = call(
        lambda *r: first_gate_up_body(2, True, *r),
        [vmem(), vmem(), hbm(), hbm()],
        [((all_rows, 2 * ff), F32)],
        (across, acc, w_gate, w_up),
        9,
        gu_scratch,
        moved=14,
    )[0]
    relays = [relays[0]] + [swap(relays[k], CELL * k, devices) for k in range(1, planes)]
    nears = [h for h in held if h[0][0] == "near"]
    downs = [h for h in held if h[0][0] == "down"]
    send, keep = call(
        lambda *r: rest_body(planes, [h[0] for h in nears], [h[0] for h in downs], *r),
        [vmem()] * (6 + len(held)) + [hbm()] * 2,
        [((all_rows // 2, model), F32)] * 2,
        (
            own,
            across,
            near,
            far,
            acc,
            hstate,
            *[in_vmem(h[1]) for h in nears],
            *[in_vmem(h[1]) for h in downs],
            w_gate,
            w_up,
        ),
        10,
        [pltpu.VMEM((all_rows, 2 * ff), F32), pltpu.VMEM((all_rows, model), F32)] + gu_scratch,
        moved=40,
        on_chip=True,
    )
    got = swap(send, 1, devices)
    send, send_low, keep = call(
        lambda *r: halve_body(*r),
        [vmem(), vmem()],
        [((all_rows // 4, model), BF16), ((rows_dev, model), BF16), ((all_rows // 4, model), F32)],
        (in_vmem(keep), got),
        8,
    )
    got = swap(send, 2, devices)
    got_low = swap(send_low, 2, devices)
    pieces = call(
        lambda *r: spread_body(planes, *r),
        [vmem()] * 3,
        [((rows_dev, model), F32)] + [((rows_dev, model), BF16)] * (planes - 1),
        (keep, got, got_low),
        8,
    )
    pieces = [pieces[0]] + [swap(pieces[k], CELL * k, devices) for k in range(1, planes)]
    layer_out = call(
        final_body, [vmem()] * planes, [((rows_dev, model), BF16)], tuple(pieces), 8
    )[0]
    new_cache = call(
        place_body, [vmem()] * planes, [((CTOK_DEV, width), BF16)], tuple(relays), 8, moved=1
    )[0]
    return (new_cache, layer_out)


def rotate_block(block, where_pos, old_angle, new_angle):
    rows_here = block.shape[0]
    half_size = HD // 2
    parts = block.reshape(rows_here, 2, KVH, HD)
    keys = parts[:, 0].astype(jnp.float32)
    delta = jnp.take(new_angle, where_pos, axis=0) - jnp.take(old_angle, where_pos, axis=0)
    cosine = jnp.cos(delta)[:, None, :]
    sine = jnp.sin(delta)[:, None, :]
    first = keys[..., :half_size]
    second = keys[..., half_size:]
    turned = jnp.concatenate(
        [first * cosine - second * sine, second * cosine + first * sine], axis=-1
    ).astype(jnp.bfloat16)
    return jnp.stack([turned, parts[:, 1]], axis=1).reshape(rows_here, 2 * KVH * HD)


def general_program(
    old_cache,
    new_slot,
    lengths,
    old_angle,
    new_angle,
    queries,
    new_kv,
    resid,
    gain,
    w_gate,
    w_up,
    w_down,
):
    devices = lax.axis_size("ctx")
    own_index = lax.axis_index("ctx")
    slot_count = old_cache.shape[0]
    row_width = old_cache.shape[1]
    per_peer = slot_count // devices
    rows_dev = queries.shape[0]
    all_rows = rows_dev * devices
    group_size = QH // KVH
    high = lax.Precision.HIGHEST
    scale = 1.0 / float(HD) ** 0.5
    tokens = own_index * slot_count + jnp.arange(slot_count, dtype=jnp.int32)
    row_ends = jnp.cumsum(lengths)
    passed = row_ends[None, :] <= tokens[:, None]
    owner_row = jnp.minimum(jnp.sum(passed.astype(jnp.int32), axis=1), lengths.shape[0] - 1)
    row_prior = jnp.sum(jnp.where(passed, lengths[None, :], 0), axis=1)
    position = jnp.clip(tokens - row_prior, 0, old_angle.shape[0] - 1)
    filled = new_slot >= 0
    all_queries = lax.all_gather(queries, "ctx", axis=0, tiled=True)
    target = jnp.where(
        filled, new_slot // CTOK_DEV, jnp.arange(slot_count, dtype=jnp.int32) // per_peer
    )
    sorted_order = jnp.argsort(target, stable=True)
    new_place = jnp.where(filled, new_slot % CTOK_DEV, -1)
    slot_info = jnp.stack([new_place, owner_row, position], axis=1)[sorted_order]
    sent_rows = old_cache[sorted_order].reshape(devices, per_peer, row_width)
    got_rows = lax.all_to_all(sent_rows, "ctx", split_axis=0, concat_axis=0, tiled=True)
    got_info = lax.all_to_all(
        slot_info.reshape(devices, per_peer, 3), "ctx", split_axis=0, concat_axis=0, tiled=True
    )
    got_rows = got_rows.reshape(slot_count, row_width)
    got_info = got_info.reshape(slot_count, 3)
    landing = jnp.where(got_info[:, 0] >= 0, got_info[:, 0], CTOK_DEV)
    placed = jnp.zeros((CTOK_DEV, row_width), jnp.bfloat16).at[landing].set(got_rows, mode="drop")
    placed_row = jnp.zeros((CTOK_DEV,), jnp.int32).at[landing].set(got_info[:, 1], mode="drop")
    placed_pos = jnp.zeros((CTOK_DEV,), jnp.int32).at[landing].set(got_info[:, 2], mode="drop")
    placed, moved_row, moved_pos = (placed, placed_row, placed_pos)
    new_cache = rotate_block(placed, moved_pos, old_angle, new_angle)
    key_count = new_cache.shape[0]
    key_split = new_cache.reshape(key_count, 2, KVH, HD)
    value_four = key_split[:, 1].astype(jnp.float32)
    query_four = all_queries.reshape(all_rows, KVH, group_size, HD)
    scores = (
        jnp.einsum(
            "mjge,cje->mjgc", query_four, key_split[:, 0], preferred_element_type=jnp.float32
        )
        * scale
    )
    query_row = jnp.arange(all_rows, dtype=jnp.int32) // (2 * SAMPLES)
    matching = query_row[:, None] == moved_row[None, :]
    scores = jnp.where(matching[:, None, None, :], scores, -1e30)
    local_top = jnp.max(scores, axis=-1)
    own_query = queries.reshape(rows_dev, KVH, group_size, HD).astype(jnp.float32)
    fresh_kv = jnp.repeat(new_kv.reshape(rows_dev // 2, 2, 2, KVH, HD), 2, axis=0).astype(
        jnp.float32
    )
    own_steps = (
        jnp.arange(2, dtype=jnp.int32)[None, :]
        <= (jnp.arange(rows_dev, dtype=jnp.int32) % 2)[:, None]
    )
    own_scores = jnp.einsum("mjge,msje->mjgs", own_query, fresh_kv[:, :, 0], precision=high) * scale
    own_scores = jnp.where(own_steps[:, None, None, :], own_scores, -1e30)
    own_top = jnp.max(own_scores, axis=-1)
    floor_top = jnp.maximum(local_top, -10000.0)
    weights_local = jnp.exp(scores - floor_top[..., None])
    summed = jnp.einsum("mjgc,cje->mjge", weights_local, value_four, precision=high)
    totals = jnp.sum(weights_local, axis=-1)
    got_sums, got_totals, got_tops = (
        lax.all_to_all(
            summed.reshape(devices, rows_dev, QH * HD),
            "ctx",
            split_axis=0,
            concat_axis=0,
            tiled=True,
        ),
        lax.all_to_all(
            totals.reshape(devices, rows_dev, QH), "ctx", split_axis=0, concat_axis=0, tiled=True
        ),
        lax.all_to_all(
            floor_top.reshape(devices, rows_dev, QH), "ctx", split_axis=0, concat_axis=0, tiled=True
        ),
    )
    got_tops = got_tops.reshape(devices, rows_dev, KVH, group_size)
    row_top = jnp.maximum(jnp.max(got_tops, axis=0), own_top)
    rescale = jnp.exp(got_tops - row_top[None])
    weights_own = jnp.exp(own_scores - row_top[..., None])
    row_sums = jnp.sum(
        rescale[..., None] * got_sums.reshape(devices, rows_dev, KVH, group_size, HD), axis=0
    )
    row_sums = row_sums + jnp.einsum(
        "mjgs,msje->mjge", weights_own, fresh_kv[:, :, 1], precision=high
    )
    row_totals = jnp.sum(
        rescale * got_totals.reshape(devices, rows_dev, KVH, group_size), axis=0
    ) + jnp.sum(weights_own, axis=-1)
    attn = (row_sums / row_totals[..., None]).reshape(rows_dev, QH * HD)
    hstate = resid.astype(jnp.float32) + attn
    normed = (
        hstate
        * lax.rsqrt(jnp.mean(hstate * hstate, axis=-1, keepdims=True) + 1e-05)
        * gain.astype(jnp.float32)
    ).astype(jnp.bfloat16)
    piece = lax.all_gather(normed, "ctx", axis=0, tiled=True)
    gate_out = jnp.dot(piece, w_gate, preferred_element_type=jnp.float32)
    up_out = jnp.dot(piece, w_up, preferred_element_type=jnp.float32)
    hidden_all = (jax.nn.silu(gate_out) * up_out).astype(jnp.bfloat16)
    ffn_out = lax.psum_scatter(
        jnp.dot(hidden_all, w_down, preferred_element_type=jnp.float32),
        "ctx",
        scatter_dimension=0,
        tiled=True,
    )
    layer_out = (hstate + ffn_out).astype(jnp.bfloat16)
    return (new_cache, layer_out)


def solution(mesh):
    per_device = cells_program if mesh.shape["ctx"] == 4 * CELL else general_program
    return jax.shard_map(
        per_device,
        mesh=mesh,
        in_specs=(
            P(("groups", "ctx"), None),
            P(("groups", "ctx")),
            P("groups"),
            P(),
            P(),
            P(("groups", "ctx"), None),
            P(("groups", "ctx"), None),
            P(("groups", "ctx"), None),
            P(),
            P(None, "ctx"),
            P(None, "ctx"),
            P("ctx", None),
        ),
        out_specs=(P(("groups", "ctx"), None), P(("groups", "ctx"), None)),
        check_vma=False,
    )
```

```python
import jax
import jax.numpy as jnp
from jax import lax
from jax.experimental import pallas as pl
from jax.experimental.pallas import tpu as pltpu
from jax.sharding import PartitionSpec as P

QH = 64
KVH = 8
HD = 128
CTOK_DEV = 64
SAMPLES = 4
CELL = 4
F32 = jnp.float32
BF16 = jnp.bfloat16
EXTRA = 128


def vmem():
    return pl.BlockSpec(memory_space=pltpu.VMEM)


def hbm():
    return pl.BlockSpec(memory_space=pl.ANY)


def in_hbm(x):
    return pltpu.with_memory_space_constraint(x, pltpu.HBM)


def in_vmem(x):
    return pltpu.with_memory_space_constraint(x, pltpu.VMEM)


def call(body, ins, outs, args, limit_mib, scratch=(), fetch=(), moved=0, on_chip=False, flags=None):
    kind = pltpu.VMEM if on_chip else jax.ShapeDtypeStruct
    shapes = [kind(s, d) for s, d in outs]
    shapes += [pltpu.VMEM(piece_shape(p), BF16) for p in fetch]
    extra = {} if flags is None else {"flags": flags}
    return pl.pallas_call(
        body,
        in_specs=ins,
        out_specs=[vmem() for _ in shapes],
        out_shape=shapes,
        scratch_shapes=list(scratch),
        compiler_params=pltpu.CompilerParams(vmem_limit_bytes=limit_mib << 20, **extra),
        cost_estimate=pl.CostEstimate(flops=0, transcendentals=0, bytes_accessed=moved << 20),
    )(*args)


def here():
    return lax.axis_index("ctx").astype(jnp.int32)


def three_parts(value):
    first = value.astype(BF16).astype(F32)
    rest = value - first
    second = rest.astype(BF16).astype(F32)
    return first, second, rest - second


def row_of(tokens, scal, requests):
    end = scal[0]
    passed = tokens >= end
    row = passed.astype(jnp.int32)
    prior = jnp.where(passed, end, 0)
    for r in range(1, requests):
        end = end + scal[r]
        passed = tokens >= end
        row = row + passed.astype(jnp.int32)
        prior = jnp.where(passed, end, prior)
    return row, prior


def to_sublanes(lane_row):
    n = lane_row.shape[1]
    sub = lax.broadcasted_iota(jnp.int32, (n, n), 0)
    lane = lax.broadcasted_iota(jnp.int32, (n, n), 1)
    return jnp.sum(jnp.where(sub == lane, lane_row, 0), axis=1, keepdims=True)


GU_ROWS = 512
DOWN_ROWS = 256


def piece_shape(piece):
    kind, _, n, cols = piece
    return (n * DOWN_ROWS, cols) if kind == "down" else (n, GU_ROWS, cols)


def gate_up_block(flip, i, w_gate, w_up):
    wide = w_gate.shape[0] // CELL
    row = (here() % CELL ^ flip) * wide + i // 2 * GU_ROWS
    w = w_gate if i % 2 == 0 else w_up
    return w.at[pl.ds(pl.multiple_of(row, GU_ROWS), GU_ROWS), :]


def fetch_copies(fetch, weights, pieces, sem):
    w_gate, w_up, w_down = weights
    copies = []
    for (kind, first, n, _), out in zip(fetch, pieces):
        for i in range(n):
            if kind == "down":
                src = w_down.at[pl.ds((first + i) * DOWN_ROWS, DOWN_ROWS), :]
                dst = out.at[pl.ds(i * DOWN_ROWS, DOWN_ROWS), :]
            else:
                src, dst = gate_up_block(kind, first + i, w_gate, w_up), out.at[i]
            copies.append(pltpu.make_async_copy(src, dst, sem.at[len(copies)]))
    return copies


def count_of(fetch):
    return max(1, sum(p[2] for p in fetch))


def warm_body(fetch, dep, w_gate, w_up, w_down, *refs):
    copies = fetch_copies(fetch, (w_gate, w_up, w_down), refs[:-1], refs[-1])
    for c in copies:
        c.start()
    for c in copies:
        c.wait()


def prep_body(q, kv, res, gain, *refs):
    msgs, own_gain, sem = refs[:CELL], refs[CELL], refs[CELL + 1]
    pos = here() % CELL
    wide, key_cols = q.shape[1] // CELL, kv.shape[1] // (2 * CELL)
    copies = []

    def move(src, width, first, dst):
        at = pl.multiple_of(first, HD)
        src = src.at[:, pl.ds(at, width)]
        copies.append(pltpu.make_async_copy(src, dst, sem.at[len(copies)]))

    for k in range(CELL):
        g = pos ^ k
        half = kv.shape[1] // 2
        ends = [0, wide, wide + key_cols, wide + 2 * key_cols, 2 * wide + 2 * key_cols]
        dst = [msgs[k].at[:, a:b] for a, b in zip(ends, ends[1:])]
        move(q, wide, g * wide, dst[0])
        move(kv, key_cols, g * key_cols, dst[1])
        move(kv, key_cols, half + g * key_cols, dst[2])
        move(res, wide, g * wide, dst[3])
    rows = own_gain.shape[0]
    src = gain.at[pl.ds(pl.multiple_of(pos * rows, rows), rows), :]
    copies.append(pltpu.make_async_copy(src, own_gain, sem.at[len(copies)]))
    for c in copies:
        c.start()
    for c in copies:
        c.wait()


def turn_body(requests, devices, fetch, *refs):
    sources, weights, refs = refs[:5], refs[5:8], refs[8:]
    sends, relays, refs = refs[:CELL], refs[CELL : 2 * CELL], refs[2 * CELL :]
    pieces, refs = refs[: len(fetch)], refs[len(fetch) :]
    locals_, sems, fetch_sem = refs[:5], refs[5], refs[6]
    loads = [pltpu.make_async_copy(a, b, sems.at[i]) for i, (a, b) in enumerate(zip(sources, locals_))]
    for c in loads:
        c.start()
    fetched = fetch_copies(fetch, weights, pieces, fetch_sem)
    for c in fetched:
        c.start()
    for c in loads:
        c.wait()

    @pl.when(here() >= 0)
    def _():
        turn_steps(requests, devices, *locals_, sends, relays)

    for c in fetched:
        c.wait()


def turn_steps(requests, devices, scal, slot, cache, old_angle, new_angle, sends, relays):
    me = here()
    pos_in_cell = me % CELL
    tok_n, width = cache.shape
    table_n = old_angle.shape[1]
    heads_here = KVH // CELL
    key_cols = heads_here * HD
    tokens = me * tok_n + lax.broadcasted_iota(jnp.int32, (tok_n, 1), 0)
    _, prior = row_of(tokens, scal, requests)
    position = jnp.clip(tokens - prior, 0, table_n - 1)
    hot = (lax.broadcasted_iota(jnp.int32, (tok_n, table_n), 1) == position).astype(F32)
    diff = new_angle[...] - old_angle[...]
    diff = jnp.concatenate([diff, diff], axis=0)
    delta = lax.dot_general(
        hot,
        diff,
        (((1,), (1,)), ((), ())),
        precision=lax.Precision.HIGHEST,
        preferred_element_type=F32,
    )
    cosine = jnp.cos(delta)
    lane = lax.broadcasted_iota(jnp.int32, (tok_n, HD), 1)
    sine = jnp.where(lane < HD // 2, -jnp.sin(delta), jnp.sin(delta))
    half = width // 2
    keys = []
    for h in range(KVH):
        key = cache[:, h * HD : (h + 1) * HD].astype(F32)
        keys.append((key * cosine + pltpu.roll(key, HD // 2, 1) * sine).astype(BF16))
    turned = jnp.concatenate(keys + [cache[:, half:]], axis=1)
    for k in range(CELL):
        peer = pos_in_cell ^ k
        for g in range(CELL):

            @pl.when(peer == g)
            def _():
                sends[k][:, :key_cols] = turned[:, g * key_cols : (g + 1) * key_cols]
                sends[k][:, key_cols:] = turned[:, half + g * key_cols : half + (g + 1) * key_cols]

    place = slot[...]
    per_peer = tok_n // devices
    lanes = lax.broadcasted_iota(jnp.int32, (1, tok_n), 1)
    target = jnp.where(place >= 0, place // CTOK_DEV, lanes // per_peer)
    landing = jnp.where(place >= 0, place % CTOK_DEV, -1)
    target_s = to_sublanes(target)
    sub2 = lax.broadcasted_iota(jnp.int32, (tok_n, tok_n), 0)
    lane2 = lax.broadcasted_iota(jnp.int32, (tok_n, tok_n), 1)
    ahead = ((target_s == target) & (sub2 < lane2)).astype(jnp.int32)
    rank = jnp.sum(ahead, axis=0, keepdims=True)
    order = (target % CELL) * (devices // CELL) + target // CELL
    pick = sub2 == (order * per_peer + rank)
    moved = jnp.dot(pick.astype(BF16), turned, preferred_element_type=F32).astype(BF16)
    land_s = jnp.sum(jnp.where(pick, landing, 0), axis=1, keepdims=True)
    land_wide = jnp.broadcast_to(land_s.astype(F32), (tok_n, EXTRA)).astype(BF16)
    block = tok_n // CELL
    for k in range(CELL):
        for g in range(CELL):

            @pl.when((pos_in_cell ^ k) == g)
            def _():
                relays[k][:, :width] = moved[g * block : (g + 1) * block]
                relays[k][:, width:] = land_wide[g * block : (g + 1) * block]


def assemble_body(*refs):
    msgs, cat, query = refs[:CELL], refs[CELL], refs[CELL + 1]
    pos = here() % CELL
    wide = query.shape[1]
    whole = [r[...].astype(F32) for r in msgs]
    for bit in (1, 2):
        flip = (pos & bit) != 0
        whole = [jnp.where(flip, whole[a ^ bit], whole[a]) for a in range(CELL)]
    whole = jnp.concatenate(whole, axis=0).astype(BF16)
    cat[...] = whole
    query[...] = whole[:, :wide]


def place_body(mine, far, near, out):
    got = jnp.concatenate([mine[...], far[: mine.shape[0]], near[...]], axis=0)
    width = out.shape[1]
    rows = got.shape[0]
    land = got[:, width:].astype(F32)[:, :CTOK_DEV]
    want = lax.broadcasted_iota(jnp.int32, (rows, CTOK_DEV), 1).astype(F32)
    pick = (land == want).astype(BF16)
    out[...] = lax.dot_general(
        pick, got[:, :width], (((0,), (0,)), ((), ())), preferred_element_type=F32
    ).astype(BF16)


def scores_body(requests, planes, fetch, lengths, *refs):
    qs, kvs, refs = refs[:planes], refs[planes : planes + CELL], refs[planes + CELL :]
    weights, outs, refs = refs[:3], refs[3 : 3 + planes], refs[3 + planes :]
    scal, sem, fetch_sem = refs[len(fetch) :]
    load = pltpu.make_async_copy(lengths, scal, sem.at[0])
    load.start()
    fetched = fetch_copies(fetch, weights, refs[: len(fetch)], fetch_sem)
    for c in fetched:
        c.start()
    load.wait()

    @pl.when(here() >= 0)
    def _():
        scores_steps(requests, planes, scal, qs, kvs, outs)

    for c in fetched:
        c.wait()


def scores_steps(requests, planes, scal, qs, kvs, outs):
    me = here()
    plane, pos_in_cell = me // CELL, me % CELL
    rows = qs[0].shape[0]
    tok_n, both = kvs[0].shape
    key_cols = both // 2
    heads_here = key_cols // HD
    group = QH // KVH
    all_rows = rows * planes
    query = jnp.concatenate([r[...].astype(F32) for r in qs], axis=0).astype(BF16)
    token_rows = []
    for k in range(CELL):
        base = (plane * CELL + (pos_in_cell ^ k)) * tok_n
        tokens = base + lax.broadcasted_iota(jnp.int32, (1, tok_n), 1)
        token_rows.append(row_of(tokens, scal, requests)[0])
    token_row = jnp.concatenate(token_rows, axis=1)
    index = lax.broadcasted_iota(jnp.int32, (group * all_rows, 1), 0)
    query_row = ((index // rows) % planes) ^ plane
    matching = query_row == token_row
    lane = lax.broadcasted_iota(jnp.int32, (all_rows, EXTRA), 1)
    extra = jnp.zeros((all_rows, EXTRA), F32)
    count = heads_here * group
    scale = 1.0 / float(HD) ** 0.5
    for j in range(heads_here):
        keys = jnp.concatenate([r[:, j * HD : (j + 1) * HD] for r in kvs], axis=0)
        values = jnp.concatenate(
            [r[:, key_cols + j * HD : key_cols + (j + 1) * HD] for r in kvs], axis=0
        )
        stacked = jnp.concatenate(
            [query[:, (j * group + g) * HD : (j * group + g + 1) * HD] for g in range(group)],
            axis=0,
        )
        scores = (
            lax.dot_general(stacked, keys, (((1,), (1,)), ((), ())), preferred_element_type=F32)
            * scale
        )
        top = jnp.max(jnp.where(matching, scores, -1e30), axis=1, keepdims=True)
        weights = jnp.where(matching, jnp.exp(scores - top), 0.0)
        total = jnp.sum(weights, axis=1, keepdims=True)
        high = weights.astype(BF16)
        low = (weights - high.astype(F32)).astype(BF16)
        summed = jnp.dot(high, values, preferred_element_type=F32) + jnp.dot(
            low, values, preferred_element_type=F32
        )
        mean = summed / jnp.where(total > 0, total, 1.0)
        top = jnp.where(total > 0, top, 0.0)
        tops = three_parts(top)
        totals = three_parts(total)
        for g in range(group):
            h = j * group + g
            part = slice(g * all_rows, (g + 1) * all_rows)
            for k in range(planes):
                outs[k][:, h * HD : (h + 1) * HD] = mean[
                    g * all_rows + k * rows : g * all_rows + (k + 1) * rows
                ].astype(BF16)
            for i in range(3):
                extra = jnp.where(lane == i * count + h, tops[i][part], extra)
                extra = jnp.where(lane == (3 + i) * count + h, totals[i][part], extra)
    for k in range(planes):
        outs[k][:, count * HD :] = extra[k * rows : (k + 1) * rows].astype(BF16)


def regroup_body(planes, *refs):
    moved, (mine, far, near) = refs[:CELL], refs[CELL:]
    plane = here() // CELL
    per = moved[0].shape[0] // planes
    block = CELL * per
    for out, at, k in ((mine, 0, 0), (far, 0, 2), (far, block, 3), (near, 0, 1)):
        for g in range(planes):

            @pl.when((plane ^ k) == g)
            def _():
                for a in range(CELL):
                    out[at + a * per : at + (a + 1) * per] = moved[a][g * per : (g + 1) * per]


def merge_body(planes, fetch, *refs):
    parts, cat, gain, refs = refs[:planes], *refs[planes : planes + 2], refs[planes + 2 :]
    weights, norm_out, h_out, refs = refs[:3], *refs[3:5], refs[5:]
    fetched = fetch_copies(fetch, weights, refs[: len(fetch)], refs[-1])
    for c in fetched:
        c.start()

    @pl.when(here() >= 0)
    def _():
        merge_steps(parts, cat, gain, norm_out, h_out)

    for c in fetched:
        c.wait()


def merge_steps(parts, cat, gain, norm_out, h_out):
    rows = cat.shape[0]
    wide = norm_out.shape[1] - EXTRA
    count = wide // HD
    group = QH // KVH
    heads_here = count // group
    key_cols = heads_here * HD
    scale = 1.0 / float(HD) ** 0.5
    lane = lax.broadcasted_iota(jnp.int32, (rows, EXTRA), 1)
    odd = lax.broadcasted_iota(jnp.int32, (rows, 1), 0) % 2 == 1
    fresh = cat[:, wide : wide + 2 * key_cols].astype(F32)
    before = pltpu.roll(fresh, 1, 0)
    score_self = jnp.zeros((rows, EXTRA), F32)
    score_before = jnp.zeros((rows, EXTRA), F32)
    for h in range(count):
        j = h // group
        query = cat[:, h * HD : (h + 1) * HD].astype(F32)
        one = jnp.sum(query * fresh[:, j * HD : (j + 1) * HD], axis=1, keepdims=True) * scale
        two = jnp.sum(query * before[:, j * HD : (j + 1) * HD], axis=1, keepdims=True) * scale
        score_self = jnp.where(lane == h, one, score_self)
        score_before = jnp.where(lane == h, two, score_before)
    tops, totals = [], []
    for part in parts:
        extra = part[:, wide:].astype(F32)
        shifted = [extra] + [pltpu.roll(extra, EXTRA - i * count, 1) for i in range(1, 6)]
        tops.append(shifted[0] + shifted[1] + shifted[2])
        totals.append(shifted[3] + shifted[4] + shifted[5])
    highest = jnp.where(odd, jnp.maximum(score_self, score_before), score_self)
    for top, total in zip(tops, totals):
        highest = jnp.where(total > 0, jnp.maximum(highest, top), highest)
    shares = [
        jnp.where(total > 0, total * jnp.exp(jnp.where(total > 0, top, highest) - highest), 0.0)
        for top, total in zip(tops, totals)
    ]
    share_self = jnp.exp(score_self - highest)
    share_before = jnp.where(odd, jnp.exp(score_before - highest), 0.0)
    whole = share_self + share_before
    for share in shares:
        whole = whole + share
    squares = jnp.zeros((rows, 1), F32)
    for h in range(count):
        j = h // group
        value = slice(key_cols + j * HD, key_cols + (j + 1) * HD)
        lanes = slice(h * HD, (h + 1) * HD)
        attn = share_self[:, h : h + 1] * fresh[:, value]
        attn = attn + share_before[:, h : h + 1] * before[:, value]
        for part, share in zip(parts, shares):
            attn = attn + share[:, h : h + 1] * part[:, lanes].astype(F32)
        attn = attn / whole[:, h : h + 1]
        base = wide + 2 * key_cols + h * HD
        state = cat[:, base : base + HD].astype(F32) + attn
        h_out[:, lanes] = state
        squares = squares + jnp.sum(state * state, axis=1, keepdims=True)
        norm_out[:, lanes] = (state * gain[h : h + 1, :].astype(F32)).astype(BF16)
    pieces = three_parts(squares)
    extra = jnp.zeros((rows, EXTRA), F32)
    for i in range(3):
        extra = jnp.where(lane == i, pieces[i], extra)
    norm_out[:, wide:] = extra.astype(BF16)


def stream(copies, depth):
    for c in copies[:depth]:
        c.start()

    def ready(i):
        copies[i].wait()

    def freed(i):
        if i + depth < len(copies):
            copies[i + depth].start()

    return ready, freed


def ring_copies(blocks, w_gate, w_up, buf, sem):
    copies = []
    for flip, i in blocks:
        slot = len(copies) % buf.shape[0]
        src = gate_up_block(flip, i, w_gate, w_up)
        copies.append(pltpu.make_async_copy(src, buf.at[slot], sem.at[slot]))
    return copies


def gate_up_body(flip, fetch, has_acc, *refs):
    if has_acc:
        x, acc_in, held, refs = *refs[:3], refs[3:]
    else:
        x, held, acc_in, refs = *refs[:2], None, refs[2:]
    w_gate, w_up, w_down, acc_out, piece, buf, sem, fetch_sem = refs
    ff = w_gate.shape[1]
    n_held = held.shape[0]
    total = 2 * (x.shape[1] - EXTRA) // GU_ROWS
    copies = ring_copies([(flip, i) for i in range(n_held, total)], w_gate, w_up, buf, sem)
    ready, freed = stream(copies, buf.shape[0])
    fetched = fetch_copies(fetch, (w_gate, w_up, w_down), [piece], fetch_sem)
    for c in fetched:
        c.start()
    for i in range(total):
        k = i // 2
        cols = slice((i % 2) * ff, (i % 2 + 1) * ff)
        if i >= n_held:
            ready(i - n_held)
        w = held[i] if i < n_held else buf[(i - n_held) % buf.shape[0]]
        part = jnp.dot(x[:, k * GU_ROWS : (k + 1) * GU_ROWS], w, preferred_element_type=F32)
        if k == 0:
            acc_out[:, cols] = acc_in[:, cols] + part if has_acc else part
        else:
            acc_out[:, cols] += part
        if i >= n_held:
            freed(i - n_held)
    for c in fetched:
        c.wait()


def rest_body(planes, downs, own, xs, near, far, acc_in, h, held, *refs):
    down_refs, refs = refs[: len(downs)], refs[len(downs) :]
    w_gate, w_up, send, keep, acc, out, buf, sem = refs
    wide = near.shape[1] - EXTRA
    ff = w_gate.shape[1]
    pos = here() % CELL
    depth = buf.shape[0]
    n_held = held.shape[0]
    per = 2 * wide // GU_ROWS
    blocks = [(1, i) for i in range(per)] + [(3, i) for i in range(per)]
    copies = ring_copies(blocks[n_held:], w_gate, w_up, buf, sem)
    ready, freed = stream(copies, depth)
    down_w = {}
    for (_, first, n, _), r in zip(downs, down_refs):
        for i in range(n):
            down_w[first + i] = r.at[pl.ds(i * DOWN_ROWS, DOWN_ROWS), :]
    for n, (flip, i) in enumerate(blocks):
        x = near if flip == 1 else far
        k = i // 2
        cols = slice((i % 2) * ff, (i % 2 + 1) * ff)
        if n >= n_held:
            ready(n - n_held)
        w = held[n] if n < n_held else buf[(n - n_held) % depth]
        part = jnp.dot(x[:, k * GU_ROWS : (k + 1) * GU_ROWS], w, preferred_element_type=F32)
        if n < 2:
            acc[:, cols] = acc_in[:, cols] + part
        else:
            acc[:, cols] += part
        if n >= n_held:
            freed(n - n_held)
    squares = jnp.zeros((near.shape[0], 1), F32)
    for x in (own, xs, near, far):
        extra = x[:, wide : wide + EXTRA].astype(F32)
        squares = squares + extra[:, 0:1] + extra[:, 1:2] + extra[:, 2:3]
    inv = lax.rsqrt(squares / float(wide * CELL) + 1e-05)
    gate = acc[:, :ff] * inv
    hidden = gate / (1.0 + jnp.exp(-gate)) * (acc[:, ff:] * inv)
    hidden = jnp.concatenate(
        [
            hidden[k * 2 * CELL + a * 2 : k * 2 * CELL + a * 2 + 2]
            for a in (0, 2, 1, 3)
            for k in range(planes)
        ],
        axis=0,
    ).astype(BF16)
    step = 1024
    for n in range(out.shape[1] // step):
        total = None
        for i in range(ff // DOWN_ROWS):
            part = jnp.dot(
                hidden[:, i * DOWN_ROWS : (i + 1) * DOWN_ROWS],
                down_w[i][:, n * step : (n + 1) * step],
                preferred_element_type=F32,
            )
            total = part if total is None else total + part
        out[:, n * step : (n + 1) * step] = total
    per = 2 * planes
    for g in range(CELL):

        @pl.when(pos == g)
        def _():
            cols = slice(g * wide, (g + 1) * wide)
            for n, a in enumerate((0, 2, 1, 3)):
                out[n * per : n * per + 2, cols] += h[2 * a : 2 * a + 2]

    half = 2 * per
    other = jnp.where(pos % 2 == 0, out[half:], out[:half])
    mine = jnp.where(pos % 2 == 0, out[:half], out[half:])
    send[...] = other
    keep[...] = mine


def halve_body(mine, got, send, send_low, keep):
    total = mine[...] + got[...]
    half = total.shape[0] // 2
    low = (here() % CELL) // 2 == 0
    other = jnp.where(low, total[half:], total[:half])
    high = other.astype(BF16)
    send[...] = high
    send_low[...] = (other[:2] - high[:2].astype(F32)).astype(BF16)
    keep[...] = jnp.where(low, total[:half], total[half:])


def spread_body(planes, mine, got, got_low, *outs):
    total = mine[...] + got[...].astype(F32)
    outs[0][...] = total[0:2] + got_low[...].astype(F32)
    for k in range(1, planes):
        outs[k][...] = total[2 * k : 2 * k + 2].astype(BF16)


def final_body(mine, *refs):
    total = mine[...]
    for r in refs[:-1]:
        total = total + r[...].astype(F32)
    refs[-1][...] = total.astype(BF16)


def swap(x, k, devices):
    return lax.ppermute(x, "ctx", [(i, i ^ k) for i in range(devices)])


def cells_program(*args):
    return cells_steps(*args)


def cells_steps(
    old_cache,
    new_slot,
    lengths,
    old_angle,
    new_angle,
    queries,
    new_kv,
    resid,
    gain,
    w_gate,
    w_up,
    w_down,
):
    devices = lax.axis_size("ctx")
    planes = devices // CELL
    tok_n, width = old_cache.shape
    requests = lengths.shape[0]
    rows_dev, model = queries.shape
    wide = model // CELL
    key_cols = KVH // CELL * HD
    msg_cols = 2 * wide + 2 * key_cols
    cell_rows = rows_dev * CELL
    all_rows = cell_rows * planes
    ff = w_gate.shape[1]
    w_gate, w_up, w_down = in_hbm(w_gate), in_hbm(w_up), in_hbm(w_down)
    weights = (w_gate, w_up, w_down)
    n_down = ff // DOWN_ROWS
    plans = {
        "turn": [("down", 0, 2, model)],
        "warm_q": [("down", 2, 3, model)],
        "scores": [("down", 5, n_down - 5, model)],
        "merge": [(0, 0, 2, ff)],
        "gate_up_own": [(2, 0, 2, ff)],
        "gate_up_x": [(1, 0, 2, ff)],
    }
    held = []

    def keep_pieces(name, values):
        held.extend(zip(plans[name], values))

    def warm(name, dep):
        plan = plans[name]
        keep_pieces(
            name,
            call(
                lambda *r: warm_body(plan, *r),
                [hbm()] * 4,
                [],
                (dep, *weights),
                1,
                [pltpu.SemaphoreType.DMA((count_of(plan),))],
                plan,
                8,
            ),
        )

    sources = (queries, new_kv, resid, gain.reshape(model // HD, HD))
    prepared = call(
        prep_body,
        [hbm()] * 4,
        [((rows_dev, msg_cols), BF16)] * CELL + [((wide // HD, HD), BF16)],
        tuple(in_hbm(x) for x in sources),
        2,
        [pltpu.SemaphoreType.DMA((4 * CELL + 1,))],
    )
    msgs, own_gain = prepared[:CELL], prepared[CELL]
    msgs = [msgs[0]] + [swap(msgs[k], k, devices) for k in range(1, CELL)]
    plan = plans["turn"]
    sources = (lengths, new_slot[None, :], old_cache, old_angle.T, new_angle.T)
    turned = call(
        lambda *r: turn_body(requests, devices, plan, *r),
        [hbm()] * 8,
        [((tok_n, 2 * key_cols), BF16)] * CELL
        + [((tok_n // CELL, width + EXTRA), BF16)] * CELL,
        (*[in_hbm(x) for x in sources], *weights),
        10,
        [pltpu.SMEM(lengths.shape, lengths.dtype)]
        + [pltpu.VMEM(x.shape, x.dtype) for x in sources[1:]]
        + [pltpu.SemaphoreType.DMA((len(sources),)), pltpu.SemaphoreType.DMA((count_of(plan),))],
        plan,
        8,
    )
    sends, relays = turned[:CELL], turned[CELL : 2 * CELL]
    keep_pieces("turn", turned[2 * CELL :])
    kvs = [sends[0]] + [swap(sends[k], k, devices) for k in range(1, CELL)]
    cat, own_q = call(
        assemble_body,
        [vmem()] * CELL,
        [((cell_rows, msg_cols), BF16), ((cell_rows, wide), BF16)],
        tuple(msgs),
        4,
    )
    qs = [own_q] + [swap(own_q, CELL * k, devices) for k in range(1, planes)]
    warm("warm_q", own_q)
    relays = [relays[0]] + [swap(relays[k], k, devices) for k in range(1, CELL)]
    plan = plans["scores"]
    parts = call(
        lambda *r: scores_body(requests, planes, plan, *r),
        [hbm()] + [vmem()] * (planes + CELL) + [hbm()] * 3,
        [((cell_rows, wide + EXTRA), BF16)] * planes,
        (in_hbm(lengths), *qs, *kvs, *weights),
        10,
        [
            pltpu.SMEM(lengths.shape, lengths.dtype),
            pltpu.SemaphoreType.DMA((1,)),
            pltpu.SemaphoreType.DMA((count_of(plan),)),
        ],
        plan,
        5,
    )
    keep_pieces("scores", parts[planes:])
    parts = [parts[0]] + [swap(parts[k], CELL * k, devices) for k in range(1, planes)]
    plan = plans["merge"]
    merged = call(
        lambda *r: merge_body(planes, plan, *r),
        [vmem()] * (planes + 2) + [hbm()] * 3,
        [((cell_rows, wide + EXTRA), BF16), ((cell_rows, wide), F32)],
        (*parts, cat, own_gain, *weights),
        6,
        [pltpu.SemaphoreType.DMA((count_of(plan),))],
        plan,
        4,
    )
    normed, hstate, own_held = merged
    block = tok_n // planes
    relay_mine, relay_far, relay_near = call(
        lambda *r: regroup_body(planes, *r),
        [vmem()] * CELL,
        [((n * block, width + EXTRA), BF16) for n in (1, 2, 1)],
        tuple(relays),
        4,
    )
    relay_far = swap(relay_far, 2 * CELL, devices)
    blocks = [normed] + [swap(normed, CELL * k, devices) for k in range(1, planes)]
    own = jnp.concatenate(blocks, axis=0)
    across = swap(own, 2, devices)
    near = swap(own, 1, devices)
    gu_scratch = [pltpu.VMEM((6, GU_ROWS, ff), BF16), pltpu.SemaphoreType.DMA((6,))]
    fetch_sem = [pltpu.SemaphoreType.DMA((2,))]
    acc, x_held = call(
        lambda *r: gate_up_body(0, plans["gate_up_own"], False, *r),
        [vmem()] * 2 + [hbm()] * 3,
        [((all_rows, 2 * ff), F32)],
        (own, in_vmem(own_held), *weights),
        12,
        gu_scratch + fetch_sem,
        plans["gate_up_own"],
        14,
    )
    far = swap(across, 1, devices)
    acc, near_held = call(
        lambda *r: gate_up_body(2, plans["gate_up_x"], True, *r),
        [vmem()] * 3 + [hbm()] * 3,
        [((all_rows, 2 * ff), F32)],
        (across, acc, in_vmem(x_held), *weights),
        12,
        gu_scratch + fetch_sem,
        plans["gate_up_x"],
        14,
    )
    relay_near = jnp.concatenate([relay_near, relay_far[block:]], axis=0)
    relay_near = swap(relay_near, CELL, devices)
    downs = [h for h in held if h[0][0] == "down"]
    send, keep = call(
        lambda *r: rest_body(planes, [h[0] for h in downs], *r),
        [vmem()] * (7 + len(downs)) + [hbm()] * 2,
        [((all_rows // 2, model), F32)] * 2,
        (
            own,
            across,
            in_vmem(near),
            in_vmem(far),
            acc,
            hstate,
            in_vmem(near_held),
            *[in_vmem(h[1]) for h in downs],
            w_gate,
            w_up,
        ),
        18,
        [
            pltpu.VMEM((all_rows, 2 * ff), F32),
            pltpu.VMEM((all_rows, model), F32),
            pltpu.VMEM((8, GU_ROWS, ff), BF16),
            pltpu.SemaphoreType.DMA((8,)),
        ],
        moved=40,
        on_chip=True,
    )
    got = swap(send, 1, devices)
    send, send_low, keep = call(
        lambda *r: halve_body(*r),
        [vmem(), vmem()],
        [((all_rows // 4, model), BF16), ((rows_dev, model), BF16), ((all_rows // 4, model), F32)],
        (in_vmem(keep), got),
        8,
    )
    got = swap(send, 2, devices)
    got_low = swap(send_low, 2, devices)
    pieces = call(
        lambda *r: spread_body(planes, *r),
        [vmem()] * 3,
        [((rows_dev, model), F32)] + [((rows_dev, model), BF16)] * (planes - 1),
        (keep, got, got_low),
        8,
    )
    pieces = [pieces[0]] + [swap(pieces[k], CELL * k, devices) for k in range(1, planes)]
    layer_out = call(
        final_body, [vmem()] * planes, [((rows_dev, model), BF16)], tuple(pieces), 8
    )[0]
    new_cache = call(
        place_body,
        [vmem()] * 3,
        [((CTOK_DEV, width), BF16)],
        (relay_mine, relay_far, relay_near),
        8,
        moved=1,
    )[0]
    return (new_cache, layer_out)


def rotate_block(block, where_pos, old_angle, new_angle):
    rows_here = block.shape[0]
    half_size = HD // 2
    parts = block.reshape(rows_here, 2, KVH, HD)
    keys = parts[:, 0].astype(jnp.float32)
    delta = jnp.take(new_angle, where_pos, axis=0) - jnp.take(old_angle, where_pos, axis=0)
    cosine = jnp.cos(delta)[:, None, :]
    sine = jnp.sin(delta)[:, None, :]
    first = keys[..., :half_size]
    second = keys[..., half_size:]
    turned = jnp.concatenate(
        [first * cosine - second * sine, second * cosine + first * sine], axis=-1
    ).astype(jnp.bfloat16)
    return jnp.stack([turned, parts[:, 1]], axis=1).reshape(rows_here, 2 * KVH * HD)


def general_program(
    old_cache,
    new_slot,
    lengths,
    old_angle,
    new_angle,
    queries,
    new_kv,
    resid,
    gain,
    w_gate,
    w_up,
    w_down,
):
    devices = lax.axis_size("ctx")
    own_index = lax.axis_index("ctx")
    slot_count = old_cache.shape[0]
    row_width = old_cache.shape[1]
    per_peer = slot_count // devices
    rows_dev = queries.shape[0]
    all_rows = rows_dev * devices
    group_size = QH // KVH
    high = lax.Precision.HIGHEST
    scale = 1.0 / float(HD) ** 0.5
    tokens = own_index * slot_count + jnp.arange(slot_count, dtype=jnp.int32)
    row_ends = jnp.cumsum(lengths)
    passed = row_ends[None, :] <= tokens[:, None]
    owner_row = jnp.minimum(jnp.sum(passed.astype(jnp.int32), axis=1), lengths.shape[0] - 1)
    row_prior = jnp.sum(jnp.where(passed, lengths[None, :], 0), axis=1)
    position = jnp.clip(tokens - row_prior, 0, old_angle.shape[0] - 1)
    filled = new_slot >= 0
    all_queries = lax.all_gather(queries, "ctx", axis=0, tiled=True)
    target = jnp.where(
        filled, new_slot // CTOK_DEV, jnp.arange(slot_count, dtype=jnp.int32) // per_peer
    )
    sorted_order = jnp.argsort(target, stable=True)
    new_place = jnp.where(filled, new_slot % CTOK_DEV, -1)
    slot_info = jnp.stack([new_place, owner_row, position], axis=1)[sorted_order]
    sent_rows = old_cache[sorted_order].reshape(devices, per_peer, row_width)
    got_rows = lax.all_to_all(sent_rows, "ctx", split_axis=0, concat_axis=0, tiled=True)
    got_info = lax.all_to_all(
        slot_info.reshape(devices, per_peer, 3), "ctx", split_axis=0, concat_axis=0, tiled=True
    )
    got_rows = got_rows.reshape(slot_count, row_width)
    got_info = got_info.reshape(slot_count, 3)
    landing = jnp.where(got_info[:, 0] >= 0, got_info[:, 0], CTOK_DEV)
    placed = jnp.zeros((CTOK_DEV, row_width), jnp.bfloat16).at[landing].set(got_rows, mode="drop")
    placed_row = jnp.zeros((CTOK_DEV,), jnp.int32).at[landing].set(got_info[:, 1], mode="drop")
    placed_pos = jnp.zeros((CTOK_DEV,), jnp.int32).at[landing].set(got_info[:, 2], mode="drop")
    placed, moved_row, moved_pos = (placed, placed_row, placed_pos)
    new_cache = rotate_block(placed, moved_pos, old_angle, new_angle)
    key_count = new_cache.shape[0]
    key_split = new_cache.reshape(key_count, 2, KVH, HD)
    value_four = key_split[:, 1].astype(jnp.float32)
    query_four = all_queries.reshape(all_rows, KVH, group_size, HD)
    scores = (
        jnp.einsum(
            "mjge,cje->mjgc", query_four, key_split[:, 0], preferred_element_type=jnp.float32
        )
        * scale
    )
    query_row = jnp.arange(all_rows, dtype=jnp.int32) // (2 * SAMPLES)
    matching = query_row[:, None] == moved_row[None, :]
    scores = jnp.where(matching[:, None, None, :], scores, -1e30)
    local_top = jnp.max(scores, axis=-1)
    own_query = queries.reshape(rows_dev, KVH, group_size, HD).astype(jnp.float32)
    fresh_kv = jnp.repeat(new_kv.reshape(rows_dev // 2, 2, 2, KVH, HD), 2, axis=0).astype(
        jnp.float32
    )
    own_steps = (
        jnp.arange(2, dtype=jnp.int32)[None, :]
        <= (jnp.arange(rows_dev, dtype=jnp.int32) % 2)[:, None]
    )
    own_scores = jnp.einsum("mjge,msje->mjgs", own_query, fresh_kv[:, :, 0], precision=high) * scale
    own_scores = jnp.where(own_steps[:, None, None, :], own_scores, -1e30)
    own_top = jnp.max(own_scores, axis=-1)
    floor_top = jnp.maximum(local_top, -10000.0)
    weights_local = jnp.exp(scores - floor_top[..., None])
    summed = jnp.einsum("mjgc,cje->mjge", weights_local, value_four, precision=high)
    totals = jnp.sum(weights_local, axis=-1)
    got_sums, got_totals, got_tops = (
        lax.all_to_all(
            summed.reshape(devices, rows_dev, QH * HD),
            "ctx",
            split_axis=0,
            concat_axis=0,
            tiled=True,
        ),
        lax.all_to_all(
            totals.reshape(devices, rows_dev, QH), "ctx", split_axis=0, concat_axis=0, tiled=True
        ),
        lax.all_to_all(
            floor_top.reshape(devices, rows_dev, QH), "ctx", split_axis=0, concat_axis=0, tiled=True
        ),
    )
    got_tops = got_tops.reshape(devices, rows_dev, KVH, group_size)
    row_top = jnp.maximum(jnp.max(got_tops, axis=0), own_top)
    rescale = jnp.exp(got_tops - row_top[None])
    weights_own = jnp.exp(own_scores - row_top[..., None])
    row_sums = jnp.sum(
        rescale[..., None] * got_sums.reshape(devices, rows_dev, KVH, group_size, HD), axis=0
    )
    row_sums = row_sums + jnp.einsum(
        "mjgs,msje->mjge", weights_own, fresh_kv[:, :, 1], precision=high
    )
    row_totals = jnp.sum(
        rescale * got_totals.reshape(devices, rows_dev, KVH, group_size), axis=0
    ) + jnp.sum(weights_own, axis=-1)
    attn = (row_sums / row_totals[..., None]).reshape(rows_dev, QH * HD)
    hstate = resid.astype(jnp.float32) + attn
    normed = (
        hstate
        * lax.rsqrt(jnp.mean(hstate * hstate, axis=-1, keepdims=True) + 1e-05)
        * gain.astype(jnp.float32)
    ).astype(jnp.bfloat16)
    piece = lax.all_gather(normed, "ctx", axis=0, tiled=True)
    gate_out = jnp.dot(piece, w_gate, preferred_element_type=jnp.float32)
    up_out = jnp.dot(piece, w_up, preferred_element_type=jnp.float32)
    hidden_all = (jax.nn.silu(gate_out) * up_out).astype(jnp.bfloat16)
    ffn_out = lax.psum_scatter(
        jnp.dot(hidden_all, w_down, preferred_element_type=jnp.float32),
        "ctx",
        scatter_dimension=0,
        tiled=True,
    )
    layer_out = (hstate + ffn_out).astype(jnp.bfloat16)
    return (new_cache, layer_out)


def solution(mesh):
    per_device = cells_program if mesh.shape["ctx"] == 4 * CELL else general_program
    return jax.shard_map(
        per_device,
        mesh=mesh,
        in_specs=(
            P(("groups", "ctx"), None),
            P(("groups", "ctx")),
            P("groups"),
            P(),
            P(),
            P(("groups", "ctx"), None),
            P(("groups", "ctx"), None),
            P(("groups", "ctx"), None),
            P(),
            P(None, "ctx"),
            P(None, "ctx"),
            P("ctx", None),
        ),
        out_specs=(P(("groups", "ctx"), None), P(("groups", "ctx"), None)),
        check_vma=False,
    )
```

```python
import jax
import jax.numpy as jnp
from jax import lax
from jax.experimental import pallas as pl
from jax.experimental.pallas import tpu as pltpu
from jax.sharding import PartitionSpec as P

QH = 64
KVH = 8
HD = 128
CTOK_DEV = 64
SAMPLES = 4
CELL = 4
F32 = jnp.float32
BF16 = jnp.bfloat16
EXTRA = 128


def vmem():
    return pl.BlockSpec(memory_space=pltpu.VMEM)


def hbm():
    return pl.BlockSpec(memory_space=pl.ANY)


def in_hbm(x):
    return pltpu.with_memory_space_constraint(x, pltpu.HBM)


def in_vmem(x):
    return pltpu.with_memory_space_constraint(x, pltpu.VMEM)


def call(body, ins, outs, args, limit_mib, scratch=(), fetch=(), moved=0, on_chip=False, flags=None):
    kind = pltpu.VMEM if on_chip else jax.ShapeDtypeStruct
    shapes = [kind(s, d) for s, d in outs]
    shapes += [pltpu.VMEM(piece_shape(p), BF16) for p in fetch]
    extra = {} if flags is None else {"flags": flags}
    return pl.pallas_call(
        body,
        in_specs=ins,
        out_specs=[vmem() for _ in shapes],
        out_shape=shapes,
        scratch_shapes=list(scratch),
        compiler_params=pltpu.CompilerParams(vmem_limit_bytes=limit_mib << 20, **extra),
        cost_estimate=pl.CostEstimate(flops=0, transcendentals=0, bytes_accessed=moved << 20),
    )(*args)


def here():
    return lax.axis_index("ctx").astype(jnp.int32)


def three_parts(value):
    first = value.astype(BF16).astype(F32)
    rest = value - first
    second = rest.astype(BF16).astype(F32)
    return first, second, rest - second


def row_of(tokens, scal, requests):
    end = scal[0]
    passed = tokens >= end
    row = passed.astype(jnp.int32)
    prior = jnp.where(passed, end, 0)
    for r in range(1, requests):
        end = end + scal[r]
        passed = tokens >= end
        row = row + passed.astype(jnp.int32)
        prior = jnp.where(passed, end, prior)
    return row, prior


def to_sublanes(lane_row):
    n = lane_row.shape[1]
    sub = lax.broadcasted_iota(jnp.int32, (n, n), 0)
    lane = lax.broadcasted_iota(jnp.int32, (n, n), 1)
    return jnp.sum(jnp.where(sub == lane, lane_row, 0), axis=1, keepdims=True)


GU_ROWS = 512
DOWN_COLS = 1024


def piece_shape(piece):
    _, _, n, cols = piece
    return (n, GU_ROWS, cols)


def gate_up_block(flip, i, w_gate, w_up):
    wide = w_gate.shape[0] // CELL
    row = (here() % CELL ^ flip) * wide + i // 2 * GU_ROWS
    w = w_gate if i % 2 == 0 else w_up
    return w.at[pl.ds(pl.multiple_of(row, GU_ROWS), GU_ROWS), :]


def fetch_copies(fetch, weights, pieces, sem):
    copies = []
    for (flip, first, n, _), out in zip(fetch, pieces):
        for i in range(n):
            src = gate_up_block(flip, first + i, *weights)
            copies.append(pltpu.make_async_copy(src, out.at[i], sem.at[len(copies)]))
    return copies


def blocks_of(held, refs):
    found = {}
    for (flip, first, n, _), r in zip(held, refs):
        for i in range(n):
            found[flip, first + i] = r.at[i]
    return found


def count_of(fetch):
    return max(1, sum(p[2] for p in fetch))


def warm_body(fetch, dep, w_gate, w_up, *refs):
    copies = fetch_copies(fetch, (w_gate, w_up), refs[:-1], refs[-1])
    for c in copies:
        c.start()
    for c in copies:
        c.wait()


def prep_body(q, kv, res, gain, *refs):
    msgs, own_gain, sem = refs[:CELL], refs[CELL], refs[CELL + 1]
    pos = here() % CELL
    wide, key_cols = q.shape[1] // CELL, kv.shape[1] // (2 * CELL)
    copies = []

    def move(src, width, first, dst):
        at = pl.multiple_of(first, HD)
        src = src.at[:, pl.ds(at, width)]
        copies.append(pltpu.make_async_copy(src, dst, sem.at[len(copies)]))

    for k in range(CELL):
        g = pos ^ k
        half = kv.shape[1] // 2
        ends = [0, wide, wide + key_cols, wide + 2 * key_cols, 2 * wide + 2 * key_cols]
        dst = [msgs[k].at[:, a:b] for a, b in zip(ends, ends[1:])]
        move(q, wide, g * wide, dst[0])
        move(kv, key_cols, g * key_cols, dst[1])
        move(kv, key_cols, half + g * key_cols, dst[2])
        move(res, wide, g * wide, dst[3])
    rows = own_gain.shape[0]
    src = gain.at[pl.ds(pl.multiple_of(pos * rows, rows), rows), :]
    copies.append(pltpu.make_async_copy(src, own_gain, sem.at[len(copies)]))
    for c in copies:
        c.start()
    for c in copies:
        c.wait()


def turn_body(requests, devices, fetch, *refs):
    sources, weights, refs = refs[:5], refs[5:7], refs[7:]
    sends, relays, token_row = refs[:CELL], refs[CELL : 2 * CELL], refs[2 * CELL]
    refs = refs[2 * CELL + 1 :]
    pieces, refs = refs[: len(fetch)], refs[len(fetch) :]
    locals_, sems, fetch_sem = refs[:5], refs[5], refs[6]
    loads = [pltpu.make_async_copy(a, b, sems.at[i]) for i, (a, b) in enumerate(zip(sources, locals_))]
    for c in loads:
        c.start()
    fetched = fetch_copies(fetch, weights, pieces, fetch_sem)
    for c in fetched:
        c.start()
    for c in loads:
        c.wait()

    @pl.when(here() >= 0)
    def _():
        turn_steps(requests, devices, *locals_, sends, relays, token_row)

    for c in fetched:
        c.wait()


def turn_steps(
    requests, devices, scal, slot, cache, old_angle, new_angle, sends, relays, token_row
):
    me = here()
    pos_in_cell = me % CELL
    tok_n, width = cache.shape
    table_n = old_angle.shape[1]
    heads_here = KVH // CELL
    key_cols = heads_here * HD
    tokens = me * tok_n + lax.broadcasted_iota(jnp.int32, (tok_n, 1), 0)
    for k in range(CELL):
        base = (me - pos_in_cell + (pos_in_cell ^ k)) * tok_n
        wide_tokens = base + lax.broadcasted_iota(jnp.int32, (1, tok_n), 1)
        token_row[:, k * tok_n : (k + 1) * tok_n] = row_of(wide_tokens, scal, requests)[0]
    _, prior = row_of(tokens, scal, requests)
    position = jnp.clip(tokens - prior, 0, table_n - 1)
    hot = (lax.broadcasted_iota(jnp.int32, (tok_n, table_n), 1) == position).astype(F32)
    diff = new_angle[...] - old_angle[...]
    diff = jnp.concatenate([diff, diff], axis=0)
    delta = lax.dot_general(
        hot,
        diff,
        (((1,), (1,)), ((), ())),
        precision=lax.Precision.HIGHEST,
        preferred_element_type=F32,
    )
    cosine = jnp.cos(delta)
    lane = lax.broadcasted_iota(jnp.int32, (tok_n, HD), 1)
    sine = jnp.where(lane < HD // 2, -jnp.sin(delta), jnp.sin(delta))
    half = width // 2
    keys = []
    for h in range(KVH):
        key = cache[:, h * HD : (h + 1) * HD].astype(F32)
        keys.append((key * cosine + pltpu.roll(key, HD // 2, 1) * sine).astype(BF16))
    turned = jnp.concatenate(keys + [cache[:, half:]], axis=1)
    for k in range(CELL):
        peer = pos_in_cell ^ k
        for g in range(CELL):

            @pl.when(peer == g)
            def _():
                sends[k][:, :key_cols] = turned[:, g * key_cols : (g + 1) * key_cols]
                sends[k][:, key_cols:] = turned[:, half + g * key_cols : half + (g + 1) * key_cols]

    place = slot[...]
    per_peer = tok_n // devices
    lanes = lax.broadcasted_iota(jnp.int32, (1, tok_n), 1)
    target = jnp.where(place >= 0, place // CTOK_DEV, lanes // per_peer)
    landing = jnp.where(place >= 0, place % CTOK_DEV, -1)
    target_s = to_sublanes(target)
    sub2 = lax.broadcasted_iota(jnp.int32, (tok_n, tok_n), 0)
    lane2 = lax.broadcasted_iota(jnp.int32, (tok_n, tok_n), 1)
    ahead = ((target_s == target) & (sub2 < lane2)).astype(jnp.int32)
    rank = jnp.sum(ahead, axis=0, keepdims=True)
    order = (target % CELL) * (devices // CELL) + target // CELL
    pick = sub2 == (order * per_peer + rank)
    moved = jnp.dot(pick.astype(BF16), turned, preferred_element_type=F32).astype(BF16)
    land_s = jnp.sum(jnp.where(pick, landing, 0), axis=1, keepdims=True)
    land_wide = jnp.broadcast_to(land_s.astype(F32), (tok_n, EXTRA)).astype(BF16)
    block = tok_n // CELL
    for k in range(CELL):
        for g in range(CELL):

            @pl.when((pos_in_cell ^ k) == g)
            def _():
                relays[k][:, :width] = moved[g * block : (g + 1) * block]
                relays[k][:, width:] = land_wide[g * block : (g + 1) * block]


def assemble_body(*refs):
    msgs, cat, query = refs[:CELL], refs[CELL], refs[CELL + 1]
    pos = here() % CELL
    wide = query.shape[1]
    whole = [r[...].astype(F32) for r in msgs]
    for bit in (1, 2):
        flip = (pos & bit) != 0
        whole = [jnp.where(flip, whole[a ^ bit], whole[a]) for a in range(CELL)]
    whole = jnp.concatenate(whole, axis=0).astype(BF16)
    cat[...] = whole
    query[...] = whole[:, :wide]


def place_body(mine, far, near, out):
    got = jnp.concatenate([mine[...], far[: mine.shape[0]], near[...]], axis=0)
    width = out.shape[1]
    rows = got.shape[0]
    land = got[:, width:].astype(F32)[:, :CTOK_DEV]
    want = lax.broadcasted_iota(jnp.int32, (rows, CTOK_DEV), 1).astype(F32)
    pick = (land == want).astype(BF16)
    out[...] = lax.dot_general(
        pick, got[:, :width], (((0,), (0,)), ((), ())), preferred_element_type=F32
    ).astype(BF16)


def scores_body(planes, fetch, token_row, *refs):
    qs, kvs, refs = refs[:planes], refs[planes : planes + CELL], refs[planes + CELL :]
    weights, outs, refs = refs[:2], refs[2 : 2 + planes], refs[2 + planes :]
    fetched = fetch_copies(fetch, weights, refs[: len(fetch)], refs[-1])
    for c in fetched:
        c.start()

    @pl.when(here() >= 0)
    def _():
        scores_steps(planes, token_row, qs, kvs, outs)

    for c in fetched:
        c.wait()


def scores_steps(planes, token_row, qs, kvs, outs):
    plane = here() // CELL
    rows = qs[0].shape[0]
    _, both = kvs[0].shape
    key_cols = both // 2
    heads_here = key_cols // HD
    group = QH // KVH
    all_rows = rows * planes
    query = jnp.concatenate([r[...].astype(F32) for r in qs], axis=0).astype(BF16)
    index = lax.broadcasted_iota(jnp.int32, (group * all_rows, 1), 0)
    query_row = ((index // rows) % planes) ^ plane
    matching = query_row == token_row[...]
    lane = lax.broadcasted_iota(jnp.int32, (all_rows, EXTRA), 1)
    extra = jnp.zeros((all_rows, EXTRA), F32)
    count = heads_here * group
    scale = 1.0 / float(HD) ** 0.5
    for j in range(heads_here):
        keys = jnp.concatenate([r[:, j * HD : (j + 1) * HD] for r in kvs], axis=0)
        values = jnp.concatenate(
            [r[:, key_cols + j * HD : key_cols + (j + 1) * HD] for r in kvs], axis=0
        )
        stacked = jnp.concatenate(
            [query[:, (j * group + g) * HD : (j * group + g + 1) * HD] for g in range(group)],
            axis=0,
        )
        scores = (
            lax.dot_general(stacked, keys, (((1,), (1,)), ((), ())), preferred_element_type=F32)
            * scale
        )
        top = jnp.max(jnp.where(matching, scores, -1e30), axis=1, keepdims=True)
        weights = jnp.where(matching, jnp.exp(scores - top), 0.0)
        total = jnp.sum(weights, axis=1, keepdims=True)
        high = weights.astype(BF16)
        low = (weights - high.astype(F32)).astype(BF16)
        summed = jnp.dot(high, values, preferred_element_type=F32) + jnp.dot(
            low, values, preferred_element_type=F32
        )
        mean = summed / jnp.where(total > 0, total, 1.0)
        top = jnp.where(total > 0, top, 0.0)
        tops = three_parts(top)
        totals = three_parts(total)
        for g in range(group):
            h = j * group + g
            part = slice(g * all_rows, (g + 1) * all_rows)
            for k in range(planes):
                outs[k][:, h * HD : (h + 1) * HD] = mean[
                    g * all_rows + k * rows : g * all_rows + (k + 1) * rows
                ].astype(BF16)
            for i in range(3):
                extra = jnp.where(lane == i * count + h, tops[i][part], extra)
                extra = jnp.where(lane == (3 + i) * count + h, totals[i][part], extra)
    for k in range(planes):
        outs[k][:, count * HD :] = extra[k * rows : (k + 1) * rows].astype(BF16)


def regroup_body(planes, fetch, *refs):
    moved, weights, (mine, far, near, *refs) = refs[:CELL], refs[CELL : CELL + 2], refs[CELL + 2 :]
    fetched = fetch_copies(fetch, weights, refs[: len(fetch)], refs[-1])
    for c in fetched:
        c.start()
    plane = here() // CELL
    per = moved[0].shape[0] // planes
    block = CELL * per
    for out, at, k in ((mine, 0, 0), (far, 0, 2), (far, block, 3), (near, 0, 1)):
        for g in range(planes):

            @pl.when((plane ^ k) == g)
            def _():
                for a in range(CELL):
                    out[at + a * per : at + (a + 1) * per] = moved[a][g * per : (g + 1) * per]

    for c in fetched:
        c.wait()


def merge_body(planes, fetch, *refs):
    parts, cat, gain, refs = refs[:planes], *refs[planes : planes + 2], refs[planes + 2 :]
    weights, norm_out, h_out, refs = refs[:2], *refs[2:4], refs[4:]
    fetched = fetch_copies(fetch, weights, refs[: len(fetch)], refs[-1])
    for c in fetched:
        c.start()

    @pl.when(here() >= 0)
    def _():
        merge_steps(parts, cat, gain, norm_out, h_out)

    for c in fetched:
        c.wait()


def merge_steps(parts, cat, gain, norm_out, h_out):
    rows = cat.shape[0]
    wide = norm_out.shape[1] - EXTRA
    count = wide // HD
    group = QH // KVH
    heads_here = count // group
    key_cols = heads_here * HD
    scale = 1.0 / float(HD) ** 0.5
    lane = lax.broadcasted_iota(jnp.int32, (rows, EXTRA), 1)
    odd = lax.broadcasted_iota(jnp.int32, (rows, 1), 0) % 2 == 1
    fresh = cat[:, wide : wide + 2 * key_cols].astype(F32)
    before = pltpu.roll(fresh, 1, 0)
    score_self = jnp.zeros((rows, EXTRA), F32)
    score_before = jnp.zeros((rows, EXTRA), F32)
    for h in range(count):
        j = h // group
        query = cat[:, h * HD : (h + 1) * HD].astype(F32)
        one = jnp.sum(query * fresh[:, j * HD : (j + 1) * HD], axis=1, keepdims=True) * scale
        two = jnp.sum(query * before[:, j * HD : (j + 1) * HD], axis=1, keepdims=True) * scale
        score_self = jnp.where(lane == h, one, score_self)
        score_before = jnp.where(lane == h, two, score_before)
    tops, totals = [], []
    for part in parts:
        extra = part[:, wide:].astype(F32)
        shifted = [extra] + [pltpu.roll(extra, EXTRA - i * count, 1) for i in range(1, 6)]
        tops.append(shifted[0] + shifted[1] + shifted[2])
        totals.append(shifted[3] + shifted[4] + shifted[5])
    highest = jnp.where(odd, jnp.maximum(score_self, score_before), score_self)
    for top, total in zip(tops, totals):
        highest = jnp.where(total > 0, jnp.maximum(highest, top), highest)
    shares = [
        jnp.where(total > 0, total * jnp.exp(jnp.where(total > 0, top, highest) - highest), 0.0)
        for top, total in zip(tops, totals)
    ]
    share_self = jnp.exp(score_self - highest)
    share_before = jnp.where(odd, jnp.exp(score_before - highest), 0.0)
    whole = share_self + share_before
    for share in shares:
        whole = whole + share
    squares = jnp.zeros((rows, 1), F32)
    for h in range(count):
        j = h // group
        value = slice(key_cols + j * HD, key_cols + (j + 1) * HD)
        lanes = slice(h * HD, (h + 1) * HD)
        attn = share_self[:, h : h + 1] * fresh[:, value]
        attn = attn + share_before[:, h : h + 1] * before[:, value]
        for part, share in zip(parts, shares):
            attn = attn + share[:, h : h + 1] * part[:, lanes].astype(F32)
        attn = attn / whole[:, h : h + 1]
        base = wide + 2 * key_cols + h * HD
        state = cat[:, base : base + HD].astype(F32) + attn
        h_out[:, lanes] = state
        squares = squares + jnp.sum(state * state, axis=1, keepdims=True)
        norm_out[:, lanes] = (state * gain[h : h + 1, :].astype(F32)).astype(BF16)
    pieces = three_parts(squares)
    extra = jnp.zeros((rows, EXTRA), F32)
    for i in range(3):
        extra = jnp.where(lane == i, pieces[i], extra)
    norm_out[:, wide:] = extra.astype(BF16)


def gate_up_body(flip, held, fetch, has_acc, *refs):
    x, refs = refs[0], refs[1:]
    acc_in, refs = (refs[0], refs[1:]) if has_acc else (None, refs)
    blocks, refs = blocks_of(held, refs[: len(held)]), refs[len(held) :]
    w_gate, w_up, acc_out, *pieces, fetch_sem = refs
    ff = w_gate.shape[1]
    fetched = fetch_copies(fetch, (w_gate, w_up), pieces, fetch_sem)
    for c in fetched:
        c.start()

    @pl.when(here() >= 0)
    def _():
        for i in range(2 * (x.shape[1] - EXTRA) // GU_ROWS):
            k = i // 2
            cols = slice((i % 2) * ff, (i % 2 + 1) * ff)
            part = jnp.dot(
                x[:, k * GU_ROWS : (k + 1) * GU_ROWS],
                blocks[flip, i][...],
                preferred_element_type=F32,
            )
            if k == 0:
                acc_out[:, cols] = acc_in[:, cols] + part if has_acc else part
            else:
                acc_out[:, cols] += part

    for c in fetched:
        c.wait()


def rest_body(planes, held, late, own, xs, near, far, acc_in, h, *refs):
    blocks, refs = blocks_of(held, refs[: len(held)]), refs[len(held) :]
    w_gate, w_up, w_down, send, keep, acc, out, buf, sem, dbuf, dsem = refs
    wide = near.shape[1] - EXTRA
    ff = w_gate.shape[1]
    pos = here() % CELL
    depth = dbuf.shape[0]
    fetched = fetch_copies([late], (w_gate, w_up), [buf], sem)
    downs = []
    for n in range(out.shape[1] // DOWN_COLS):
        src = w_down.at[:, n * DOWN_COLS : (n + 1) * DOWN_COLS]
        downs.append(pltpu.make_async_copy(src, dbuf.at[n % depth], dsem.at[n % depth]))
    for c in fetched + downs[:depth]:
        c.start()
    per = 2 * wide // GU_ROWS
    x_of = {1: near, 3: far}

    def add(flip, i, w):
        k = i // 2
        cols = slice((i % 2) * ff, (i % 2 + 1) * ff)
        part = jnp.dot(
            x_of[flip][:, k * GU_ROWS : (k + 1) * GU_ROWS], w, preferred_element_type=F32
        )
        if flip == 1 and k == 0:
            acc[:, cols] = acc_in[:, cols] + part
        else:
            acc[:, cols] += part

    @pl.when(pos >= 0)
    def _():
        for flip in (1, 3):
            for i in range(per):
                if (flip, i) in blocks:
                    add(flip, i, blocks[flip, i][...])

    for n, c in enumerate(fetched):
        c.wait()
        add(late[0], late[1] + n, buf[n])
    squares = jnp.zeros((near.shape[0], 1), F32)
    for x in (own, xs, near, far):
        extra = x[:, wide : wide + EXTRA].astype(F32)
        squares = squares + extra[:, 0:1] + extra[:, 1:2] + extra[:, 2:3]
    inv = lax.rsqrt(squares / float(wide * CELL) + 1e-05)
    gate = acc[:, :ff] * inv
    hidden = gate / (1.0 + jnp.exp(-gate)) * (acc[:, ff:] * inv)
    hidden = jnp.concatenate(
        [
            hidden[k * 2 * CELL + a * 2 : k * 2 * CELL + a * 2 + 2]
            for a in (0, 2, 1, 3)
            for k in range(planes)
        ],
        axis=0,
    ).astype(BF16)
    for n, c in enumerate(downs):
        c.wait()
        out[:, n * DOWN_COLS : (n + 1) * DOWN_COLS] = jnp.dot(
            hidden, dbuf[n % depth], preferred_element_type=F32
        )
        if n + depth < len(downs):
            downs[n + depth].start()
    per = 2 * planes
    for g in range(CELL):

        @pl.when(pos == g)
        def _():
            cols = slice(g * wide, (g + 1) * wide)
            for n, a in enumerate((0, 2, 1, 3)):
                out[n * per : n * per + 2, cols] += h[2 * a : 2 * a + 2]

    half = 2 * per
    other = jnp.where(pos % 2 == 0, out[half:], out[:half])
    mine = jnp.where(pos % 2 == 0, out[:half], out[half:])
    send[...] = other
    keep[...] = mine


def halve_body(mine, got, send, keep):
    total = mine[...] + got[...]
    half = total.shape[0] // 2
    low = (here() % CELL) // 2 == 0
    send[...] = jnp.where(low, total[half:], total[:half]).astype(BF16)
    keep[...] = jnp.where(low, total[:half], total[half:])


def spread_body(planes, mine, got, *outs):
    total = mine[...] + got[...].astype(F32)
    outs[0][...] = total[0:2]
    for k in range(1, planes):
        outs[k][...] = total[2 * k : 2 * k + 2].astype(BF16)


def final_body(mine, *refs):
    total = mine[...]
    for r in refs[:-1]:
        total = total + r[...].astype(F32)
    refs[-1][...] = total.astype(BF16)


def swap(x, k, devices, sends=None):
    pairs = [(i, i ^ k) for i in range(devices) if sends is None or sends(i)]
    return lax.ppermute(x, "ctx", pairs)


def cells_program(*args):
    return cells_steps(*args)


def cells_steps(
    old_cache,
    new_slot,
    lengths,
    old_angle,
    new_angle,
    queries,
    new_kv,
    resid,
    gain,
    w_gate,
    w_up,
    w_down,
):
    devices = lax.axis_size("ctx")
    planes = devices // CELL
    tok_n, width = old_cache.shape
    requests = lengths.shape[0]
    rows_dev, model = queries.shape
    wide = model // CELL
    key_cols = KVH // CELL * HD
    msg_cols = 2 * wide + 2 * key_cols
    cell_rows = rows_dev * CELL
    all_rows = cell_rows * planes
    ff = w_gate.shape[1]
    weights = (in_hbm(w_gate), in_hbm(w_up))
    per = 2 * wide // GU_ROWS
    plans = {
        "turn": [(0, 0, 4, ff)],
        "warm_q": [(0, 4, 2, ff)],
        "scores": [(0, 6, per - 6, ff)],
        "merge": [(2, 0, 2, ff)],
        "regroup": [(2, 2, 2, ff)],
        "gate_up_own": [(2, 4, per - 4, ff), (1, 0, 4, ff)],
        "gate_up_x": [(1, 4, per - 4, ff), (3, 0, 4, ff)],
        "rest": [(3, 4, per - 4, ff)],
    }
    held = []

    def keep_pieces(name, values):
        held.extend(zip(plans[name], values))

    def pieces_for(*flips):
        found = [h for h in held if h[0][0] in flips]
        return [h[0] for h in found], [in_vmem(h[1]) for h in found]

    def has_tokens(i):
        return i < devices // 2

    def warm(name, dep):
        plan = plans[name]
        values = call(
            lambda *r: warm_body(plan, *r),
            [hbm()] * 3,
            [],
            (dep, *weights),
            1,
            [pltpu.SemaphoreType.DMA((count_of(plan),))],
            plan,
            8,
        )
        keep_pieces(name, values)

    sources = (queries, new_kv, resid, gain.reshape(model // HD, HD))
    prepared = call(
        prep_body,
        [hbm()] * 4,
        [((rows_dev, msg_cols), BF16)] * CELL + [((wide // HD, HD), BF16)],
        tuple(in_hbm(x) for x in sources),
        2,
        [pltpu.SemaphoreType.DMA((4 * CELL + 1,))],
    )
    msgs, own_gain = prepared[:CELL], prepared[CELL]
    msgs = [msgs[0]] + [swap(msgs[k], k, devices) for k in range(1, CELL)]
    plan = plans["turn"]
    sources = (lengths, new_slot[None, :], old_cache, old_angle.T, new_angle.T)
    turned = call(
        lambda *r: turn_body(requests, devices, plan, *r),
        [hbm()] * 7,
        [((tok_n, 2 * key_cols), BF16)] * CELL
        + [((tok_n // CELL, width + EXTRA), BF16)] * CELL
        + [((1, CELL * tok_n), jnp.int32)],
        (*[in_hbm(x) for x in sources], *weights),
        10,
        [pltpu.SMEM(lengths.shape, lengths.dtype)]
        + [pltpu.VMEM(x.shape, x.dtype) for x in sources[1:]]
        + [pltpu.SemaphoreType.DMA((len(sources),)), pltpu.SemaphoreType.DMA((count_of(plan),))],
        plan,
        8,
    )
    sends, relays = turned[:CELL], turned[CELL : 2 * CELL]
    token_row = turned[2 * CELL]
    keep_pieces("turn", turned[2 * CELL + 1 :])
    kvs = [sends[0]] + [swap(sends[k], k, devices, has_tokens) for k in range(1, CELL)]
    cat, own_q = call(
        assemble_body,
        [vmem()] * CELL,
        [((cell_rows, msg_cols), BF16), ((cell_rows, wide), BF16)],
        tuple(msgs),
        4,
    )
    qs = [own_q] + [
        swap(own_q, CELL * k, devices, lambda i: has_tokens(i ^ (CELL * k)))
        for k in range(1, planes)
    ]
    warm("warm_q", own_q)
    relays = [relays[0]] + [swap(relays[k], k, devices, has_tokens) for k in range(1, CELL)]
    plan = plans["scores"]
    parts = call(
        lambda *r: scores_body(planes, plan, *r),
        [vmem()] * (1 + planes + CELL) + [hbm()] * 2,
        [((cell_rows, wide + EXTRA), BF16)] * planes,
        (token_row, *qs, *kvs, *weights),
        10,
        [pltpu.SemaphoreType.DMA((count_of(plan),))],
        plan,
        5,
    )
    keep_pieces("scores", parts[planes:])
    parts = [parts[0]] + [swap(parts[k], CELL * k, devices, has_tokens) for k in range(1, planes)]
    plan = plans["merge"]
    merged = call(
        lambda *r: merge_body(planes, plan, *r),
        [vmem()] * (planes + 2) + [hbm()] * 2,
        [((cell_rows, wide + EXTRA), BF16), ((cell_rows, wide), F32)],
        (*parts, cat, own_gain, *weights),
        6,
        [pltpu.SemaphoreType.DMA((count_of(plan),))],
        plan,
        4,
    )
    normed, hstate = merged[:2]
    keep_pieces("merge", merged[2:])
    block = tok_n // planes
    regroup_plan = plans["regroup"]
    grouped = call(
        lambda *r: regroup_body(planes, regroup_plan, *r),
        [vmem()] * CELL + [hbm()] * 2,
        [((n * block, width + EXTRA), BF16) for n in (1, 2, 1)],
        (*relays, *weights),
        4,
        [pltpu.SemaphoreType.DMA((count_of(regroup_plan),))],
        regroup_plan,
        4,
    )
    relay_mine, relay_far, relay_near = grouped[:3]
    keep_pieces("regroup", grouped[3:])
    relay_far = swap(relay_far, 2 * CELL, devices, has_tokens)
    blocks = [normed] + [swap(normed, CELL * k, devices) for k in range(1, planes)]
    own = jnp.concatenate(blocks, axis=0)
    across = swap(own, 2, devices)
    near = swap(own, 1, devices)

    def gate_up(name, flip, x, acc):
        specs, values = pieces_for(flip)
        plan = plans[name]
        more = [] if acc is None else [acc]
        acc, *pieces = call(
            lambda *r: gate_up_body(flip, specs, plan, len(more) > 0, *r),
            [vmem()] * (1 + len(more) + len(values)) + [hbm()] * 2,
            [((all_rows, 2 * ff), F32)],
            (x, *more, *values, *weights),
            4,
            [pltpu.SemaphoreType.DMA((count_of(plan),))],
            plan,
            14,
        )
        keep_pieces(name, pieces)
        return acc

    acc = gate_up("gate_up_own", 0, own, None)
    far = swap(across, 1, devices)
    acc = gate_up("gate_up_x", 2, across, acc)
    relay_near = jnp.concatenate([relay_near, relay_far[block:]], axis=0)
    relay_near = swap(relay_near, CELL, devices)
    specs, values = pieces_for(1, 3)
    late = plans["rest"][0]
    send, keep = call(
        lambda *r: rest_body(planes, specs, late, *r),
        [vmem()] * (6 + len(values)) + [hbm()] * 3,
        [((all_rows // 2, model), F32)] * 2,
        (
            own,
            across,
            in_vmem(near),
            in_vmem(far),
            acc,
            hstate,
            *values,
            *weights,
            in_hbm(w_down),
        ),
        32,
        [
            pltpu.VMEM((all_rows, 2 * ff), F32),
            pltpu.VMEM((all_rows, model), F32),
            pltpu.VMEM(piece_shape(late), BF16),
            pltpu.SemaphoreType.DMA((count_of([late]),)),
            pltpu.VMEM((6, ff, DOWN_COLS), BF16),
            pltpu.SemaphoreType.DMA((6,)),
        ],
        moved=40,
        on_chip=True,
    )
    got = swap(send, 1, devices)
    send, keep = call(
        lambda *r: halve_body(*r),
        [vmem(), vmem()],
        [((all_rows // 4, model), BF16), ((all_rows // 4, model), F32)],
        (in_vmem(keep), got),
        8,
    )
    got = swap(send, 2, devices)
    pieces = call(
        lambda *r: spread_body(planes, *r),
        [vmem()] * 2,
        [((rows_dev, model), F32)] + [((rows_dev, model), BF16)] * (planes - 1),
        (keep, got),
        8,
    )
    pieces = [pieces[0]] + [swap(pieces[k], CELL * k, devices) for k in range(1, planes)]
    layer_out = call(
        final_body, [vmem()] * planes, [((rows_dev, model), BF16)], tuple(pieces), 8
    )[0]
    new_cache = call(
        place_body,
        [vmem()] * 3,
        [((CTOK_DEV, width), BF16)],
        (relay_mine, relay_far, relay_near),
        8,
        moved=1,
    )[0]
    return (new_cache, layer_out)


def rotate_block(block, where_pos, old_angle, new_angle):
    rows_here = block.shape[0]
    half_size = HD // 2
    parts = block.reshape(rows_here, 2, KVH, HD)
    keys = parts[:, 0].astype(jnp.float32)
    delta = jnp.take(new_angle, where_pos, axis=0) - jnp.take(old_angle, where_pos, axis=0)
    cosine = jnp.cos(delta)[:, None, :]
    sine = jnp.sin(delta)[:, None, :]
    first = keys[..., :half_size]
    second = keys[..., half_size:]
    turned = jnp.concatenate(
        [first * cosine - second * sine, second * cosine + first * sine], axis=-1
    ).astype(jnp.bfloat16)
    return jnp.stack([turned, parts[:, 1]], axis=1).reshape(rows_here, 2 * KVH * HD)


def general_program(
    old_cache,
    new_slot,
    lengths,
    old_angle,
    new_angle,
    queries,
    new_kv,
    resid,
    gain,
    w_gate,
    w_up,
    w_down,
):
    devices = lax.axis_size("ctx")
    own_index = lax.axis_index("ctx")
    slot_count = old_cache.shape[0]
    row_width = old_cache.shape[1]
    per_peer = slot_count // devices
    rows_dev = queries.shape[0]
    all_rows = rows_dev * devices
    group_size = QH // KVH
    high = lax.Precision.HIGHEST
    scale = 1.0 / float(HD) ** 0.5
    tokens = own_index * slot_count + jnp.arange(slot_count, dtype=jnp.int32)
    row_ends = jnp.cumsum(lengths)
    passed = row_ends[None, :] <= tokens[:, None]
    owner_row = jnp.minimum(jnp.sum(passed.astype(jnp.int32), axis=1), lengths.shape[0] - 1)
    row_prior = jnp.sum(jnp.where(passed, lengths[None, :], 0), axis=1)
    position = jnp.clip(tokens - row_prior, 0, old_angle.shape[0] - 1)
    filled = new_slot >= 0
    all_queries = lax.all_gather(queries, "ctx", axis=0, tiled=True)
    target = jnp.where(
        filled, new_slot // CTOK_DEV, jnp.arange(slot_count, dtype=jnp.int32) // per_peer
    )
    sorted_order = jnp.argsort(target, stable=True)
    new_place = jnp.where(filled, new_slot % CTOK_DEV, -1)
    slot_info = jnp.stack([new_place, owner_row, position], axis=1)[sorted_order]
    sent_rows = old_cache[sorted_order].reshape(devices, per_peer, row_width)
    got_rows = lax.all_to_all(sent_rows, "ctx", split_axis=0, concat_axis=0, tiled=True)
    got_info = lax.all_to_all(
        slot_info.reshape(devices, per_peer, 3), "ctx", split_axis=0, concat_axis=0, tiled=True
    )
    got_rows = got_rows.reshape(slot_count, row_width)
    got_info = got_info.reshape(slot_count, 3)
    landing = jnp.where(got_info[:, 0] >= 0, got_info[:, 0], CTOK_DEV)
    placed = jnp.zeros((CTOK_DEV, row_width), jnp.bfloat16).at[landing].set(got_rows, mode="drop")
    placed_row = jnp.zeros((CTOK_DEV,), jnp.int32).at[landing].set(got_info[:, 1], mode="drop")
    placed_pos = jnp.zeros((CTOK_DEV,), jnp.int32).at[landing].set(got_info[:, 2], mode="drop")
    placed, moved_row, moved_pos = (placed, placed_row, placed_pos)
    new_cache = rotate_block(placed, moved_pos, old_angle, new_angle)
    key_count = new_cache.shape[0]
    key_split = new_cache.reshape(key_count, 2, KVH, HD)
    value_four = key_split[:, 1].astype(jnp.float32)
    query_four = all_queries.reshape(all_rows, KVH, group_size, HD)
    scores = (
        jnp.einsum(
            "mjge,cje->mjgc", query_four, key_split[:, 0], preferred_element_type=jnp.float32
        )
        * scale
    )
    query_row = jnp.arange(all_rows, dtype=jnp.int32) // (2 * SAMPLES)
    matching = query_row[:, None] == moved_row[None, :]
    scores = jnp.where(matching[:, None, None, :], scores, -1e30)
    local_top = jnp.max(scores, axis=-1)
    own_query = queries.reshape(rows_dev, KVH, group_size, HD).astype(jnp.float32)
    fresh_kv = jnp.repeat(new_kv.reshape(rows_dev // 2, 2, 2, KVH, HD), 2, axis=0).astype(
        jnp.float32
    )
    own_steps = (
        jnp.arange(2, dtype=jnp.int32)[None, :]
        <= (jnp.arange(rows_dev, dtype=jnp.int32) % 2)[:, None]
    )
    own_scores = jnp.einsum("mjge,msje->mjgs", own_query, fresh_kv[:, :, 0], precision=high) * scale
    own_scores = jnp.where(own_steps[:, None, None, :], own_scores, -1e30)
    own_top = jnp.max(own_scores, axis=-1)
    floor_top = jnp.maximum(local_top, -10000.0)
    weights_local = jnp.exp(scores - floor_top[..., None])
    summed = jnp.einsum("mjgc,cje->mjge", weights_local, value_four, precision=high)
    totals = jnp.sum(weights_local, axis=-1)
    got_sums, got_totals, got_tops = (
        lax.all_to_all(
            summed.reshape(devices, rows_dev, QH * HD),
            "ctx",
            split_axis=0,
            concat_axis=0,
            tiled=True,
        ),
        lax.all_to_all(
            totals.reshape(devices, rows_dev, QH), "ctx", split_axis=0, concat_axis=0, tiled=True
        ),
        lax.all_to_all(
            floor_top.reshape(devices, rows_dev, QH), "ctx", split_axis=0, concat_axis=0, tiled=True
        ),
    )
    got_tops = got_tops.reshape(devices, rows_dev, KVH, group_size)
    row_top = jnp.maximum(jnp.max(got_tops, axis=0), own_top)
    rescale = jnp.exp(got_tops - row_top[None])
    weights_own = jnp.exp(own_scores - row_top[..., None])
    row_sums = jnp.sum(
        rescale[..., None] * got_sums.reshape(devices, rows_dev, KVH, group_size, HD), axis=0
    )
    row_sums = row_sums + jnp.einsum(
        "mjgs,msje->mjge", weights_own, fresh_kv[:, :, 1], precision=high
    )
    row_totals = jnp.sum(
        rescale * got_totals.reshape(devices, rows_dev, KVH, group_size), axis=0
    ) + jnp.sum(weights_own, axis=-1)
    attn = (row_sums / row_totals[..., None]).reshape(rows_dev, QH * HD)
    hstate = resid.astype(jnp.float32) + attn
    normed = (
        hstate
        * lax.rsqrt(jnp.mean(hstate * hstate, axis=-1, keepdims=True) + 1e-05)
        * gain.astype(jnp.float32)
    ).astype(jnp.bfloat16)
    piece = lax.all_gather(normed, "ctx", axis=0, tiled=True)
    gate_out = jnp.dot(piece, w_gate, preferred_element_type=jnp.float32)
    up_out = jnp.dot(piece, w_up, preferred_element_type=jnp.float32)
    hidden_all = (jax.nn.silu(gate_out) * up_out).astype(jnp.bfloat16)
    ffn_out = lax.psum_scatter(
        jnp.dot(hidden_all, w_down, preferred_element_type=jnp.float32),
        "ctx",
        scatter_dimension=0,
        tiled=True,
    )
    layer_out = (hstate + ffn_out).astype(jnp.bfloat16)
    return (new_cache, layer_out)


def solution(mesh):
    per_device = cells_program if mesh.shape["ctx"] == 4 * CELL else general_program
    return jax.shard_map(
        per_device,
        mesh=mesh,
        in_specs=(
            P(("groups", "ctx"), None),
            P(("groups", "ctx")),
            P("groups"),
            P(),
            P(),
            P(("groups", "ctx"), None),
            P(("groups", "ctx"), None),
            P(("groups", "ctx"), None),
            P(),
            P(None, "ctx"),
            P(None, "ctx"),
            P("ctx", None),
        ),
        out_specs=(P(("groups", "ctx"), None), P(("groups", "ctx"), None)),
        check_vma=False,
    )
```

```python
import jax
import jax.numpy as jnp
from jax import lax
from jax.experimental import pallas as pl
from jax.experimental.pallas import tpu as pltpu
from jax.sharding import PartitionSpec as P

QH = 64
KVH = 8
HD = 128
CTOK_DEV = 64
SAMPLES = 4
CELL = 4
F32 = jnp.float32
BF16 = jnp.bfloat16
EXTRA = 128


def vmem():
    return pl.BlockSpec(memory_space=pltpu.VMEM)


def hbm():
    return pl.BlockSpec(memory_space=pl.ANY)


def in_hbm(x):
    return pltpu.with_memory_space_constraint(x, pltpu.HBM)


def in_vmem(x):
    return pltpu.with_memory_space_constraint(x, pltpu.VMEM)


def call(body, ins, outs, args, limit_mib, scratch=(), fetch=(), moved=0, on_chip=False, flags=None):
    kind = pltpu.VMEM if on_chip else jax.ShapeDtypeStruct
    shapes = [kind(s, d) for s, d in outs]
    shapes += [pltpu.VMEM(piece_shape(p), BF16) for p in fetch]
    extra = {} if flags is None else {"flags": flags}
    return pl.pallas_call(
        body,
        in_specs=ins,
        out_specs=[vmem() for _ in shapes],
        out_shape=shapes,
        scratch_shapes=list(scratch),
        compiler_params=pltpu.CompilerParams(vmem_limit_bytes=limit_mib << 20, **extra),
        cost_estimate=pl.CostEstimate(flops=0, transcendentals=0, bytes_accessed=moved << 20),
    )(*args)


def here():
    return lax.axis_index("ctx").astype(jnp.int32)


def three_parts(value):
    first = value.astype(BF16).astype(F32)
    rest = value - first
    second = rest.astype(BF16).astype(F32)
    return first, second, rest - second


def row_of(tokens, scal, requests):
    end = scal[0]
    passed = tokens >= end
    row = passed.astype(jnp.int32)
    prior = jnp.where(passed, end, 0)
    for r in range(1, requests):
        end = end + scal[r]
        passed = tokens >= end
        row = row + passed.astype(jnp.int32)
        prior = jnp.where(passed, end, prior)
    return row, prior


def to_sublanes(lane_row):
    n = lane_row.shape[1]
    sub = lax.broadcasted_iota(jnp.int32, (n, n), 0)
    lane = lax.broadcasted_iota(jnp.int32, (n, n), 1)
    return jnp.sum(jnp.where(sub == lane, lane_row, 0), axis=1, keepdims=True)


GU_ROWS = 512
DOWN_ROWS = 256


def piece_shape(piece):
    _, _, n, cols = piece
    return (n, GU_ROWS, cols)


def gate_up_block(flip, i, w_gate, w_up):
    wide = w_gate.shape[0] // CELL
    row = (here() % CELL ^ flip) * wide + i // 2 * GU_ROWS
    w = w_gate if i % 2 == 0 else w_up
    return w.at[pl.ds(pl.multiple_of(row, GU_ROWS), GU_ROWS), :]


def fetch_copies(fetch, weights, pieces, sem):
    copies = []
    for (flip, first, n, _), out in zip(fetch, pieces):
        for i in range(n):
            src = gate_up_block(flip, first + i, *weights)
            copies.append(pltpu.make_async_copy(src, out.at[i], sem.at[len(copies)]))
    return copies


def blocks_of(held, refs):
    found = {}
    for (flip, first, n, _), r in zip(held, refs):
        for i in range(n):
            found[flip, first + i] = r.at[i]
    return found


def count_of(fetch):
    return max(1, sum(p[2] for p in fetch))


def warm_body(fetch, dep, w_gate, w_up, *refs):
    copies = fetch_copies(fetch, (w_gate, w_up), refs[:-1], refs[-1])
    for c in copies:
        c.start()
    for c in copies:
        c.wait()


def prep_body(q, kv, res, gain, *refs):
    msgs, own_gain, sem = refs[:CELL], refs[CELL], refs[CELL + 1]
    pos = here() % CELL
    wide, key_cols = q.shape[1] // CELL, kv.shape[1] // (2 * CELL)
    copies = []

    def move(src, width, first, dst):
        at = pl.multiple_of(first, HD)
        src = src.at[:, pl.ds(at, width)]
        copies.append(pltpu.make_async_copy(src, dst, sem.at[len(copies)]))

    for k in range(CELL):
        g = pos ^ k
        half = kv.shape[1] // 2
        ends = [0, wide, wide + key_cols, wide + 2 * key_cols, 2 * wide + 2 * key_cols]
        dst = [msgs[k].at[:, a:b] for a, b in zip(ends, ends[1:])]
        move(q, wide, g * wide, dst[0])
        move(kv, key_cols, g * key_cols, dst[1])
        move(kv, key_cols, half + g * key_cols, dst[2])
        move(res, wide, g * wide, dst[3])
    rows = own_gain.shape[0]
    src = gain.at[pl.ds(pl.multiple_of(pos * rows, rows), rows), :]
    copies.append(pltpu.make_async_copy(src, own_gain, sem.at[len(copies)]))
    for c in copies:
        c.start()
    for c in copies:
        c.wait()


def turn_body(requests, devices, fetch, *refs):
    sources, weights, refs = refs[:5], refs[5:7], refs[7:]
    sends, relays, token_row = refs[:CELL], refs[CELL : 2 * CELL], refs[2 * CELL]
    refs = refs[2 * CELL + 1 :]
    pieces, refs = refs[: len(fetch)], refs[len(fetch) :]
    locals_, sems, fetch_sem = refs[:5], refs[5], refs[6]
    loads = [pltpu.make_async_copy(a, b, sems.at[i]) for i, (a, b) in enumerate(zip(sources, locals_))]
    for c in loads:
        c.start()
    fetched = fetch_copies(fetch, weights, pieces, fetch_sem)
    for c in fetched:
        c.start()
    for c in loads:
        c.wait()

    @pl.when(here() >= 0)
    def _():
        turn_steps(requests, devices, *locals_, sends, relays, token_row)

    for c in fetched:
        c.wait()


def turn_steps(
    requests, devices, scal, slot, cache, old_angle, new_angle, sends, relays, token_row
):
    me = here()
    pos_in_cell = me % CELL
    tok_n, width = cache.shape
    table_n = old_angle.shape[1]
    heads_here = KVH // CELL
    key_cols = heads_here * HD
    tokens = me * tok_n + lax.broadcasted_iota(jnp.int32, (tok_n, 1), 0)
    for k in range(CELL):
        base = (me - pos_in_cell + (pos_in_cell ^ k)) * tok_n
        wide_tokens = base + lax.broadcasted_iota(jnp.int32, (1, tok_n), 1)
        token_row[:, k * tok_n : (k + 1) * tok_n] = row_of(wide_tokens, scal, requests)[0]
    _, prior = row_of(tokens, scal, requests)
    position = jnp.clip(tokens - prior, 0, table_n - 1)
    hot = (lax.broadcasted_iota(jnp.int32, (tok_n, table_n), 1) == position).astype(F32)
    diff = new_angle[...] - old_angle[...]
    diff = jnp.concatenate([diff, diff], axis=0)
    delta = lax.dot_general(
        hot,
        diff,
        (((1,), (1,)), ((), ())),
        precision=lax.Precision.HIGHEST,
        preferred_element_type=F32,
    )
    cosine = jnp.cos(delta)
    lane = lax.broadcasted_iota(jnp.int32, (tok_n, HD), 1)
    sine = jnp.where(lane < HD // 2, -jnp.sin(delta), jnp.sin(delta))
    half = width // 2
    keys = []
    for h in range(KVH):
        key = cache[:, h * HD : (h + 1) * HD].astype(F32)
        keys.append((key * cosine + pltpu.roll(key, HD // 2, 1) * sine).astype(BF16))
    turned = jnp.concatenate(keys + [cache[:, half:]], axis=1)
    for k in range(CELL):
        peer = pos_in_cell ^ k
        for g in range(CELL):

            @pl.when(peer == g)
            def _():
                sends[k][:, :key_cols] = turned[:, g * key_cols : (g + 1) * key_cols]
                sends[k][:, key_cols:] = turned[:, half + g * key_cols : half + (g + 1) * key_cols]

    place = slot[...]
    per_peer = tok_n // devices
    lanes = lax.broadcasted_iota(jnp.int32, (1, tok_n), 1)
    target = jnp.where(place >= 0, place // CTOK_DEV, lanes // per_peer)
    landing = jnp.where(place >= 0, place % CTOK_DEV, -1)
    target_s = to_sublanes(target)
    sub2 = lax.broadcasted_iota(jnp.int32, (tok_n, tok_n), 0)
    lane2 = lax.broadcasted_iota(jnp.int32, (tok_n, tok_n), 1)
    ahead = ((target_s == target) & (sub2 < lane2)).astype(jnp.int32)
    rank = jnp.sum(ahead, axis=0, keepdims=True)
    order = (target % CELL) * (devices // CELL) + target // CELL
    pick = sub2 == (order * per_peer + rank)
    moved = jnp.dot(pick.astype(BF16), turned, preferred_element_type=F32).astype(BF16)
    land_s = jnp.sum(jnp.where(pick, landing, 0), axis=1, keepdims=True)
    land_wide = jnp.broadcast_to(land_s.astype(F32), (tok_n, EXTRA)).astype(BF16)
    block = tok_n // CELL
    for k in range(CELL):
        for g in range(CELL):

            @pl.when((pos_in_cell ^ k) == g)
            def _():
                relays[k][:, :width] = moved[g * block : (g + 1) * block]
                relays[k][:, width:] = land_wide[g * block : (g + 1) * block]


def assemble_body(*refs):
    msgs, cat, query = refs[:CELL], refs[CELL], refs[CELL + 1]
    pos = here() % CELL
    wide = query.shape[1]
    whole = [r[...].astype(F32) for r in msgs]
    for bit in (1, 2):
        flip = (pos & bit) != 0
        whole = [jnp.where(flip, whole[a ^ bit], whole[a]) for a in range(CELL)]
    whole = jnp.concatenate(whole, axis=0).astype(BF16)
    cat[...] = whole
    query[...] = whole[:, :wide]


def place_body(mine, far, near, out):
    got = jnp.concatenate([mine[...], far[: mine.shape[0]], near[...]], axis=0)
    width = out.shape[1]
    rows = got.shape[0]
    land = got[:, width:].astype(F32)[:, :CTOK_DEV]
    want = lax.broadcasted_iota(jnp.int32, (rows, CTOK_DEV), 1).astype(F32)
    pick = (land == want).astype(BF16)
    out[...] = lax.dot_general(
        pick, got[:, :width], (((0,), (0,)), ((), ())), preferred_element_type=F32
    ).astype(BF16)


def scores_body(planes, fetch, token_row, *refs):
    qs, kvs, refs = refs[:planes], refs[planes : planes + CELL], refs[planes + CELL :]
    weights, outs, refs = refs[:2], refs[2 : 2 + planes], refs[2 + planes :]
    fetched = fetch_copies(fetch, weights, refs[: len(fetch)], refs[-1])
    for c in fetched:
        c.start()

    @pl.when(here() >= 0)
    def _():
        scores_steps(planes, token_row, qs, kvs, outs)

    for c in fetched:
        c.wait()


def scores_steps(planes, token_row, qs, kvs, outs):
    plane = here() // CELL
    rows = qs[0].shape[0]
    _, both = kvs[0].shape
    key_cols = both // 2
    heads_here = key_cols // HD
    group = QH // KVH
    all_rows = rows * planes
    query = jnp.concatenate([r[...].astype(F32) for r in qs], axis=0).astype(BF16)
    index = lax.broadcasted_iota(jnp.int32, (group * all_rows, 1), 0)
    query_row = ((index // rows) % planes) ^ plane
    matching = query_row == token_row[...]
    lane = lax.broadcasted_iota(jnp.int32, (all_rows, EXTRA), 1)
    extra = jnp.zeros((all_rows, EXTRA), F32)
    count = heads_here * group
    scale = 1.0 / float(HD) ** 0.5
    for j in range(heads_here):
        keys = jnp.concatenate([r[:, j * HD : (j + 1) * HD] for r in kvs], axis=0)
        values = jnp.concatenate(
            [r[:, key_cols + j * HD : key_cols + (j + 1) * HD] for r in kvs], axis=0
        )
        stacked = jnp.concatenate(
            [query[:, (j * group + g) * HD : (j * group + g + 1) * HD] for g in range(group)],
            axis=0,
        )
        scores = (
            lax.dot_general(stacked, keys, (((1,), (1,)), ((), ())), preferred_element_type=F32)
            * scale
        )
        top = jnp.max(jnp.where(matching, scores, -1e30), axis=1, keepdims=True)
        weights = jnp.where(matching, jnp.exp(scores - top), 0.0)
        total = jnp.sum(weights, axis=1, keepdims=True)
        high = weights.astype(BF16)
        low = (weights - high.astype(F32)).astype(BF16)
        summed = jnp.dot(high, values, preferred_element_type=F32) + jnp.dot(
            low, values, preferred_element_type=F32
        )
        mean = summed / jnp.where(total > 0, total, 1.0)
        top = jnp.where(total > 0, top, 0.0)
        tops = three_parts(top)
        totals = three_parts(total)
        for g in range(group):
            h = j * group + g
            part = slice(g * all_rows, (g + 1) * all_rows)
            for k in range(planes):
                outs[k][:, h * HD : (h + 1) * HD] = mean[
                    g * all_rows + k * rows : g * all_rows + (k + 1) * rows
                ].astype(BF16)
            for i in range(3):
                extra = jnp.where(lane == i * count + h, tops[i][part], extra)
                extra = jnp.where(lane == (3 + i) * count + h, totals[i][part], extra)
    for k in range(planes):
        outs[k][:, count * HD :] = extra[k * rows : (k + 1) * rows].astype(BF16)


def regroup_body(planes, fetch, *refs):
    moved, weights, (mine, far, near, *refs) = refs[:CELL], refs[CELL : CELL + 2], refs[CELL + 2 :]
    fetched = fetch_copies(fetch, weights, refs[: len(fetch)], refs[-1])
    for c in fetched:
        c.start()
    plane = here() // CELL
    per = moved[0].shape[0] // planes
    block = CELL * per
    for out, at, k in ((mine, 0, 0), (far, 0, 2), (far, block, 3), (near, 0, 1)):
        for g in range(planes):

            @pl.when((plane ^ k) == g)
            def _():
                for a in range(CELL):
                    out[at + a * per : at + (a + 1) * per] = moved[a][g * per : (g + 1) * per]

    for c in fetched:
        c.wait()


def merge_body(planes, fetch, *refs):
    parts, cat, gain, refs = refs[:planes], *refs[planes : planes + 2], refs[planes + 2 :]
    weights, norm_out, h_out, refs = refs[:2], *refs[2:4], refs[4:]
    fetched = fetch_copies(fetch, weights, refs[: len(fetch)], refs[-1])
    for c in fetched:
        c.start()

    @pl.when(here() >= 0)
    def _():
        merge_steps(parts, cat, gain, norm_out, h_out)

    for c in fetched:
        c.wait()


def merge_steps(parts, cat, gain, norm_out, h_out):
    rows = cat.shape[0]
    wide = norm_out.shape[1] - EXTRA
    count = wide // HD
    group = QH // KVH
    heads_here = count // group
    key_cols = heads_here * HD
    scale = 1.0 / float(HD) ** 0.5
    lane = lax.broadcasted_iota(jnp.int32, (rows, EXTRA), 1)
    odd = lax.broadcasted_iota(jnp.int32, (rows, 1), 0) % 2 == 1
    fresh = cat[:, wide : wide + 2 * key_cols].astype(F32)
    before = pltpu.roll(fresh, 1, 0)
    score_self = jnp.zeros((rows, EXTRA), F32)
    score_before = jnp.zeros((rows, EXTRA), F32)
    for h in range(count):
        j = h // group
        query = cat[:, h * HD : (h + 1) * HD].astype(F32)
        one = jnp.sum(query * fresh[:, j * HD : (j + 1) * HD], axis=1, keepdims=True) * scale
        two = jnp.sum(query * before[:, j * HD : (j + 1) * HD], axis=1, keepdims=True) * scale
        score_self = jnp.where(lane == h, one, score_self)
        score_before = jnp.where(lane == h, two, score_before)
    tops, totals = [], []
    for part in parts:
        extra = part[:, wide:].astype(F32)
        shifted = [extra] + [pltpu.roll(extra, EXTRA - i * count, 1) for i in range(1, 6)]
        tops.append(shifted[0] + shifted[1] + shifted[2])
        totals.append(shifted[3] + shifted[4] + shifted[5])
    highest = jnp.where(odd, jnp.maximum(score_self, score_before), score_self)
    for top, total in zip(tops, totals):
        highest = jnp.where(total > 0, jnp.maximum(highest, top), highest)
    shares = [
        jnp.where(total > 0, total * jnp.exp(jnp.where(total > 0, top, highest) - highest), 0.0)
        for top, total in zip(tops, totals)
    ]
    share_self = jnp.exp(score_self - highest)
    share_before = jnp.where(odd, jnp.exp(score_before - highest), 0.0)
    whole = share_self + share_before
    for share in shares:
        whole = whole + share
    squares = jnp.zeros((rows, 1), F32)
    for h in range(count):
        j = h // group
        value = slice(key_cols + j * HD, key_cols + (j + 1) * HD)
        lanes = slice(h * HD, (h + 1) * HD)
        attn = share_self[:, h : h + 1] * fresh[:, value]
        attn = attn + share_before[:, h : h + 1] * before[:, value]
        for part, share in zip(parts, shares):
            attn = attn + share[:, h : h + 1] * part[:, lanes].astype(F32)
        attn = attn / whole[:, h : h + 1]
        base = wide + 2 * key_cols + h * HD
        state = cat[:, base : base + HD].astype(F32) + attn
        h_out[:, lanes] = state
        squares = squares + jnp.sum(state * state, axis=1, keepdims=True)
        norm_out[:, lanes] = (state * gain[h : h + 1, :].astype(F32)).astype(BF16)
    pieces = three_parts(squares)
    extra = jnp.zeros((rows, EXTRA), F32)
    for i in range(3):
        extra = jnp.where(lane == i, pieces[i], extra)
    norm_out[:, wide:] = extra.astype(BF16)


def gate_up_body(flip, held, fetch, has_acc, *refs):
    x, refs = refs[0], refs[1:]
    acc_in, refs = (refs[0], refs[1:]) if has_acc else (None, refs)
    blocks, refs = blocks_of(held, refs[: len(held)]), refs[len(held) :]
    w_gate, w_up, acc_out, *pieces, fetch_sem = refs
    ff = w_gate.shape[1]
    fetched = fetch_copies(fetch, (w_gate, w_up), pieces, fetch_sem)
    for c in fetched:
        c.start()

    @pl.when(here() >= 0)
    def _():
        for i in range(2 * (x.shape[1] - EXTRA) // GU_ROWS):
            k = i // 2
            cols = slice((i % 2) * ff, (i % 2 + 1) * ff)
            part = jnp.dot(
                x[:, k * GU_ROWS : (k + 1) * GU_ROWS],
                blocks[flip, i][...],
                preferred_element_type=F32,
            )
            if k == 0:
                acc_out[:, cols] = acc_in[:, cols] + part if has_acc else part
            else:
                acc_out[:, cols] += part

    for c in fetched:
        c.wait()


def rest_body(planes, held, late, own, xs, near, far, acc_in, h, *refs):
    blocks, refs = blocks_of(held, refs[: len(held)]), refs[len(held) :]
    w_gate, w_up, w_down, send, keep, acc, out, buf, sem, dbuf, dsem = refs
    wide = near.shape[1] - EXTRA
    ff = w_gate.shape[1]
    pos = here() % CELL
    depth = dbuf.shape[0]
    fetched = fetch_copies([late], (w_gate, w_up), [buf], sem)
    downs = []
    for n in range(ff // DOWN_ROWS):
        src = w_down.at[pl.ds(n * DOWN_ROWS, DOWN_ROWS), :]
        downs.append(pltpu.make_async_copy(src, dbuf.at[n % depth], dsem.at[n % depth]))
    for c in fetched + downs[:depth]:
        c.start()
    per = 2 * wide // GU_ROWS
    x_of = {1: near, 3: far}

    def add(flip, i, w):
        k = i // 2
        cols = slice((i % 2) * ff, (i % 2 + 1) * ff)
        part = jnp.dot(
            x_of[flip][:, k * GU_ROWS : (k + 1) * GU_ROWS], w, preferred_element_type=F32
        )
        if flip == 1 and k == 0:
            acc[:, cols] = acc_in[:, cols] + part
        else:
            acc[:, cols] += part

    @pl.when(pos >= 0)
    def _():
        for flip in (1, 3):
            for i in range(per):
                if (flip, i) in blocks:
                    add(flip, i, blocks[flip, i][...])

    for n, c in enumerate(fetched):
        c.wait()
        add(late[0], late[1] + n, buf[n])
    squares = jnp.zeros((near.shape[0], 1), F32)
    for x in (own, xs, near, far):
        extra = x[:, wide : wide + EXTRA].astype(F32)
        squares = squares + extra[:, 0:1] + extra[:, 1:2] + extra[:, 2:3]
    inv = lax.rsqrt(squares / float(wide * CELL) + 1e-05)
    gate = acc[:, :ff] * inv
    hidden = gate / (1.0 + jnp.exp(-gate)) * (acc[:, ff:] * inv)
    hidden = jnp.concatenate(
        [
            hidden[k * 2 * CELL + a * 2 : k * 2 * CELL + a * 2 + 2]
            for a in (0, 2, 1, 3)
            for k in range(planes)
        ],
        axis=0,
    ).astype(BF16)
    for n, c in enumerate(downs):
        c.wait()
        part = jnp.dot(
            hidden[:, n * DOWN_ROWS : (n + 1) * DOWN_ROWS],
            dbuf[n % depth],
            preferred_element_type=F32,
        )
        if n == 0:
            out[...] = part
        else:
            out[...] += part
        if n + depth < len(downs):
            downs[n + depth].start()
    per = 2 * planes
    for g in range(CELL):

        @pl.when(pos == g)
        def _():
            cols = slice(g * wide, (g + 1) * wide)
            for n, a in enumerate((0, 2, 1, 3)):
                out[n * per : n * per + 2, cols] += h[2 * a : 2 * a + 2]

    half = 2 * per
    other = jnp.where(pos % 2 == 0, out[half:], out[:half])
    mine = jnp.where(pos % 2 == 0, out[:half], out[half:])
    send[...] = other
    keep[...] = mine


def halve_body(mine, got, send, keep):
    total = mine[...] + got[...]
    half = total.shape[0] // 2
    low = (here() % CELL) // 2 == 0
    send[...] = jnp.where(low, total[half:], total[:half]).astype(BF16)
    keep[...] = jnp.where(low, total[:half], total[half:])


def spread_body(planes, mine, got, *outs):
    total = mine[...] + got[...].astype(F32)
    outs[0][...] = total[0:2]
    for k in range(1, planes):
        outs[k][...] = total[2 * k : 2 * k + 2].astype(BF16)


def final_body(mine, *refs):
    total = mine[...]
    for r in refs[:-1]:
        total = total + r[...].astype(F32)
    refs[-1][...] = total.astype(BF16)


def swap(x, k, devices):
    return lax.ppermute(x, "ctx", [(i, i ^ k) for i in range(devices)])


def cells_program(*args):
    return cells_steps(*args)


def cells_steps(
    old_cache,
    new_slot,
    lengths,
    old_angle,
    new_angle,
    queries,
    new_kv,
    resid,
    gain,
    w_gate,
    w_up,
    w_down,
):
    devices = lax.axis_size("ctx")
    planes = devices // CELL
    tok_n, width = old_cache.shape
    requests = lengths.shape[0]
    rows_dev, model = queries.shape
    wide = model // CELL
    key_cols = KVH // CELL * HD
    msg_cols = 2 * wide + 2 * key_cols
    cell_rows = rows_dev * CELL
    all_rows = cell_rows * planes
    ff = w_gate.shape[1]
    weights = (in_hbm(w_gate), in_hbm(w_up))
    per = 2 * wide // GU_ROWS
    plans = {
        "turn": [(0, 0, 4, ff)],
        "warm_q": [(0, 4, 2, ff)],
        "scores": [(0, 6, per - 6, ff)],
        "merge": [(2, 0, 2, ff)],
        "regroup": [(2, 2, 2, ff)],
        "gate_up_own": [(2, 4, per - 4, ff), (1, 0, 4, ff)],
        "gate_up_x": [(1, 4, per - 4, ff), (3, 0, 4, ff)],
        "rest": [(3, 4, per - 4, ff)],
    }
    held = []

    def keep_pieces(name, values):
        held.extend(zip(plans[name], values))

    def pieces_for(*flips):
        found = [h for h in held if h[0][0] in flips]
        return [h[0] for h in found], [in_vmem(h[1]) for h in found]

    def warm(name, dep):
        plan = plans[name]
        values = call(
            lambda *r: warm_body(plan, *r),
            [hbm()] * 3,
            [],
            (dep, *weights),
            1,
            [pltpu.SemaphoreType.DMA((count_of(plan),))],
            plan,
            8,
        )
        keep_pieces(name, values)

    sources = (queries, new_kv, resid, gain.reshape(model // HD, HD))
    prepared = call(
        prep_body,
        [hbm()] * 4,
        [((rows_dev, msg_cols), BF16)] * CELL + [((wide // HD, HD), BF16)],
        tuple(in_hbm(x) for x in sources),
        2,
        [pltpu.SemaphoreType.DMA((4 * CELL + 1,))],
    )
    msgs, own_gain = prepared[:CELL], prepared[CELL]
    msgs = [msgs[0]] + [swap(msgs[k], k, devices) for k in range(1, CELL)]
    plan = plans["turn"]
    sources = (lengths, new_slot[None, :], old_cache, old_angle.T, new_angle.T)
    turned = call(
        lambda *r: turn_body(requests, devices, plan, *r),
        [hbm()] * 7,
        [((tok_n, 2 * key_cols), BF16)] * CELL
        + [((tok_n // CELL, width + EXTRA), BF16)] * CELL
        + [((1, CELL * tok_n), jnp.int32)],
        (*[in_hbm(x) for x in sources], *weights),
        10,
        [pltpu.SMEM(lengths.shape, lengths.dtype)]
        + [pltpu.VMEM(x.shape, x.dtype) for x in sources[1:]]
        + [pltpu.SemaphoreType.DMA((len(sources),)), pltpu.SemaphoreType.DMA((count_of(plan),))],
        plan,
        8,
    )
    sends, relays = turned[:CELL], turned[CELL : 2 * CELL]
    token_row = turned[2 * CELL]
    keep_pieces("turn", turned[2 * CELL + 1 :])
    kvs = [sends[0]] + [swap(sends[k], k, devices) for k in range(1, CELL)]
    cat, own_q = call(
        assemble_body,
        [vmem()] * CELL,
        [((cell_rows, msg_cols), BF16), ((cell_rows, wide), BF16)],
        tuple(msgs),
        4,
    )
    qs = [own_q] + [swap(own_q, CELL * k, devices) for k in range(1, planes)]
    warm("warm_q", own_q)
    relays = [relays[0]] + [swap(relays[k], k, devices) for k in range(1, CELL)]
    plan = plans["scores"]
    parts = call(
        lambda *r: scores_body(planes, plan, *r),
        [vmem()] * (1 + planes + CELL) + [hbm()] * 2,
        [((cell_rows, wide + EXTRA), BF16)] * planes,
        (token_row, *qs, *kvs, *weights),
        10,
        [pltpu.SemaphoreType.DMA((count_of(plan),))],
        plan,
        5,
    )
    keep_pieces("scores", parts[planes:])
    parts = [parts[0]] + [swap(parts[k], CELL * k, devices) for k in range(1, planes)]
    plan = plans["merge"]
    merged = call(
        lambda *r: merge_body(planes, plan, *r),
        [vmem()] * (planes + 2) + [hbm()] * 2,
        [((cell_rows, wide + EXTRA), BF16), ((cell_rows, wide), F32)],
        (*parts, cat, own_gain, *weights),
        6,
        [pltpu.SemaphoreType.DMA((count_of(plan),))],
        plan,
        4,
    )
    normed, hstate = merged[:2]
    keep_pieces("merge", merged[2:])
    block = tok_n // planes
    regroup_plan = plans["regroup"]
    grouped = call(
        lambda *r: regroup_body(planes, regroup_plan, *r),
        [vmem()] * CELL + [hbm()] * 2,
        [((n * block, width + EXTRA), BF16) for n in (1, 2, 1)],
        (*relays, *weights),
        4,
        [pltpu.SemaphoreType.DMA((count_of(regroup_plan),))],
        regroup_plan,
        4,
    )
    relay_mine, relay_far, relay_near = grouped[:3]
    keep_pieces("regroup", grouped[3:])
    relay_far = swap(relay_far, 2 * CELL, devices)
    blocks = [normed] + [swap(normed, CELL * k, devices) for k in range(1, planes)]
    own = jnp.concatenate(blocks, axis=0)
    across = swap(own, 2, devices)
    near = swap(own, 1, devices)

    def gate_up(name, flip, x, acc):
        specs, values = pieces_for(flip)
        plan = plans[name]
        more = [] if acc is None else [acc]
        acc, *pieces = call(
            lambda *r: gate_up_body(flip, specs, plan, len(more) > 0, *r),
            [vmem()] * (1 + len(more) + len(values)) + [hbm()] * 2,
            [((all_rows, 2 * ff), F32)],
            (x, *more, *values, *weights),
            4,
            [pltpu.SemaphoreType.DMA((count_of(plan),))],
            plan,
            14,
        )
        keep_pieces(name, pieces)
        return acc

    acc = gate_up("gate_up_own", 0, own, None)
    far = swap(across, 1, devices)
    acc = gate_up("gate_up_x", 2, across, acc)
    relay_near = jnp.concatenate([relay_near, relay_far[block:]], axis=0)
    relay_near = swap(relay_near, CELL, devices)
    specs, values = pieces_for(1, 3)
    late = plans["rest"][0]
    send, keep = call(
        lambda *r: rest_body(planes, specs, late, *r),
        [vmem()] * (6 + len(values)) + [hbm()] * 3,
        [((all_rows // 2, model), F32)] * 2,
        (
            *[in_vmem(x) for x in (own, across, near, far, acc, hstate)],
            *values,
            *weights,
            in_hbm(w_down),
        ),
        30,
        [
            pltpu.VMEM((all_rows, 2 * ff), F32),
            pltpu.VMEM((all_rows, model), F32),
            pltpu.VMEM(piece_shape(late), BF16),
            pltpu.SemaphoreType.DMA((count_of([late]),)),
            pltpu.VMEM((5, DOWN_ROWS, model), BF16),
            pltpu.SemaphoreType.DMA((5,)),
        ],
        moved=40,
        on_chip=True,
    )
    got = swap(send, 1, devices)
    send, keep = call(
        lambda *r: halve_body(*r),
        [vmem(), vmem()],
        [((all_rows // 4, model), BF16), ((all_rows // 4, model), F32)],
        (in_vmem(keep), got),
        8,
    )
    got = swap(send, 2, devices)
    pieces = call(
        lambda *r: spread_body(planes, *r),
        [vmem()] * 2,
        [((rows_dev, model), F32)] + [((rows_dev, model), BF16)] * (planes - 1),
        (keep, got),
        8,
    )
    pieces = [pieces[0]] + [swap(pieces[k], CELL * k, devices) for k in range(1, planes)]
    layer_out = call(
        final_body, [vmem()] * planes, [((rows_dev, model), BF16)], tuple(pieces), 8
    )[0]
    new_cache = call(
        place_body,
        [vmem()] * 3,
        [((CTOK_DEV, width), BF16)],
        (relay_mine, relay_far, relay_near),
        8,
        moved=1,
    )[0]
    return (new_cache, layer_out)


def rotate_block(block, where_pos, old_angle, new_angle):
    rows_here = block.shape[0]
    half_size = HD // 2
    parts = block.reshape(rows_here, 2, KVH, HD)
    keys = parts[:, 0].astype(jnp.float32)
    delta = jnp.take(new_angle, where_pos, axis=0) - jnp.take(old_angle, where_pos, axis=0)
    cosine = jnp.cos(delta)[:, None, :]
    sine = jnp.sin(delta)[:, None, :]
    first = keys[..., :half_size]
    second = keys[..., half_size:]
    turned = jnp.concatenate(
        [first * cosine - second * sine, second * cosine + first * sine], axis=-1
    ).astype(jnp.bfloat16)
    return jnp.stack([turned, parts[:, 1]], axis=1).reshape(rows_here, 2 * KVH * HD)


def general_program(
    old_cache,
    new_slot,
    lengths,
    old_angle,
    new_angle,
    queries,
    new_kv,
    resid,
    gain,
    w_gate,
    w_up,
    w_down,
):
    devices = lax.axis_size("ctx")
    own_index = lax.axis_index("ctx")
    slot_count = old_cache.shape[0]
    row_width = old_cache.shape[1]
    per_peer = slot_count // devices
    rows_dev = queries.shape[0]
    all_rows = rows_dev * devices
    group_size = QH // KVH
    high = lax.Precision.HIGHEST
    scale = 1.0 / float(HD) ** 0.5
    tokens = own_index * slot_count + jnp.arange(slot_count, dtype=jnp.int32)
    row_ends = jnp.cumsum(lengths)
    passed = row_ends[None, :] <= tokens[:, None]
    owner_row = jnp.minimum(jnp.sum(passed.astype(jnp.int32), axis=1), lengths.shape[0] - 1)
    row_prior = jnp.sum(jnp.where(passed, lengths[None, :], 0), axis=1)
    position = jnp.clip(tokens - row_prior, 0, old_angle.shape[0] - 1)
    filled = new_slot >= 0
    all_queries = lax.all_gather(queries, "ctx", axis=0, tiled=True)
    target = jnp.where(
        filled, new_slot // CTOK_DEV, jnp.arange(slot_count, dtype=jnp.int32) // per_peer
    )
    sorted_order = jnp.argsort(target, stable=True)
    new_place = jnp.where(filled, new_slot % CTOK_DEV, -1)
    slot_info = jnp.stack([new_place, owner_row, position], axis=1)[sorted_order]
    sent_rows = old_cache[sorted_order].reshape(devices, per_peer, row_width)
    got_rows = lax.all_to_all(sent_rows, "ctx", split_axis=0, concat_axis=0, tiled=True)
    got_info = lax.all_to_all(
        slot_info.reshape(devices, per_peer, 3), "ctx", split_axis=0, concat_axis=0, tiled=True
    )
    got_rows = got_rows.reshape(slot_count, row_width)
    got_info = got_info.reshape(slot_count, 3)
    landing = jnp.where(got_info[:, 0] >= 0, got_info[:, 0], CTOK_DEV)
    placed = jnp.zeros((CTOK_DEV, row_width), jnp.bfloat16).at[landing].set(got_rows, mode="drop")
    placed_row = jnp.zeros((CTOK_DEV,), jnp.int32).at[landing].set(got_info[:, 1], mode="drop")
    placed_pos = jnp.zeros((CTOK_DEV,), jnp.int32).at[landing].set(got_info[:, 2], mode="drop")
    placed, moved_row, moved_pos = (placed, placed_row, placed_pos)
    new_cache = rotate_block(placed, moved_pos, old_angle, new_angle)
    key_count = new_cache.shape[0]
    key_split = new_cache.reshape(key_count, 2, KVH, HD)
    value_four = key_split[:, 1].astype(jnp.float32)
    query_four = all_queries.reshape(all_rows, KVH, group_size, HD)
    scores = (
        jnp.einsum(
            "mjge,cje->mjgc", query_four, key_split[:, 0], preferred_element_type=jnp.float32
        )
        * scale
    )
    query_row = jnp.arange(all_rows, dtype=jnp.int32) // (2 * SAMPLES)
    matching = query_row[:, None] == moved_row[None, :]
    scores = jnp.where(matching[:, None, None, :], scores, -1e30)
    local_top = jnp.max(scores, axis=-1)
    own_query = queries.reshape(rows_dev, KVH, group_size, HD).astype(jnp.float32)
    fresh_kv = jnp.repeat(new_kv.reshape(rows_dev // 2, 2, 2, KVH, HD), 2, axis=0).astype(
        jnp.float32
    )
    own_steps = (
        jnp.arange(2, dtype=jnp.int32)[None, :]
        <= (jnp.arange(rows_dev, dtype=jnp.int32) % 2)[:, None]
    )
    own_scores = jnp.einsum("mjge,msje->mjgs", own_query, fresh_kv[:, :, 0], precision=high) * scale
    own_scores = jnp.where(own_steps[:, None, None, :], own_scores, -1e30)
    own_top = jnp.max(own_scores, axis=-1)
    floor_top = jnp.maximum(local_top, -10000.0)
    weights_local = jnp.exp(scores - floor_top[..., None])
    summed = jnp.einsum("mjgc,cje->mjge", weights_local, value_four, precision=high)
    totals = jnp.sum(weights_local, axis=-1)
    got_sums, got_totals, got_tops = (
        lax.all_to_all(
            summed.reshape(devices, rows_dev, QH * HD),
            "ctx",
            split_axis=0,
            concat_axis=0,
            tiled=True,
        ),
        lax.all_to_all(
            totals.reshape(devices, rows_dev, QH), "ctx", split_axis=0, concat_axis=0, tiled=True
        ),
        lax.all_to_all(
            floor_top.reshape(devices, rows_dev, QH), "ctx", split_axis=0, concat_axis=0, tiled=True
        ),
    )
    got_tops = got_tops.reshape(devices, rows_dev, KVH, group_size)
    row_top = jnp.maximum(jnp.max(got_tops, axis=0), own_top)
    rescale = jnp.exp(got_tops - row_top[None])
    weights_own = jnp.exp(own_scores - row_top[..., None])
    row_sums = jnp.sum(
        rescale[..., None] * got_sums.reshape(devices, rows_dev, KVH, group_size, HD), axis=0
    )
    row_sums = row_sums + jnp.einsum(
        "mjgs,msje->mjge", weights_own, fresh_kv[:, :, 1], precision=high
    )
    row_totals = jnp.sum(
        rescale * got_totals.reshape(devices, rows_dev, KVH, group_size), axis=0
    ) + jnp.sum(weights_own, axis=-1)
    attn = (row_sums / row_totals[..., None]).reshape(rows_dev, QH * HD)
    hstate = resid.astype(jnp.float32) + attn
    normed = (
        hstate
        * lax.rsqrt(jnp.mean(hstate * hstate, axis=-1, keepdims=True) + 1e-05)
        * gain.astype(jnp.float32)
    ).astype(jnp.bfloat16)
    piece = lax.all_gather(normed, "ctx", axis=0, tiled=True)
    gate_out = jnp.dot(piece, w_gate, preferred_element_type=jnp.float32)
    up_out = jnp.dot(piece, w_up, preferred_element_type=jnp.float32)
    hidden_all = (jax.nn.silu(gate_out) * up_out).astype(jnp.bfloat16)
    ffn_out = lax.psum_scatter(
        jnp.dot(hidden_all, w_down, preferred_element_type=jnp.float32),
        "ctx",
        scatter_dimension=0,
        tiled=True,
    )
    layer_out = (hstate + ffn_out).astype(jnp.bfloat16)
    return (new_cache, layer_out)


def solution(mesh):
    per_device = cells_program if mesh.shape["ctx"] == 4 * CELL else general_program
    return jax.shard_map(
        per_device,
        mesh=mesh,
        in_specs=(
            P(("groups", "ctx"), None),
            P(("groups", "ctx")),
            P("groups"),
            P(),
            P(),
            P(("groups", "ctx"), None),
            P(("groups", "ctx"), None),
            P(("groups", "ctx"), None),
            P(),
            P(None, "ctx"),
            P(None, "ctx"),
            P("ctx", None),
        ),
        out_specs=(P(("groups", "ctx"), None), P(("groups", "ctx"), None)),
        check_vma=False,
    )
```

```python
import jax
import jax.numpy as jnp
from jax import lax
from jax.experimental import pallas as pl
from jax.experimental.pallas import tpu as pltpu
from jax.sharding import PartitionSpec as P

QH = 64
KVH = 8
HD = 128
CTOK_DEV = 64
SAMPLES = 4
CELL = 4
F32 = jnp.float32
BF16 = jnp.bfloat16
EXTRA = 128


def vmem():
    return pl.BlockSpec(memory_space=pltpu.VMEM)


def hbm():
    return pl.BlockSpec(memory_space=pl.ANY)


def in_hbm(x):
    return pltpu.with_memory_space_constraint(x, pltpu.HBM)


def in_vmem(x):
    return pltpu.with_memory_space_constraint(x, pltpu.VMEM)


def call(body, ins, outs, args, limit_mib, scratch=(), fetch=(), moved=0, on_chip=False, flags=None):
    kind = pltpu.VMEM if on_chip else jax.ShapeDtypeStruct
    shapes = [kind(s, d) for s, d in outs]
    shapes += [pltpu.VMEM(piece_shape(p), BF16) for p in fetch]
    extra = {} if flags is None else {"flags": flags}
    return pl.pallas_call(
        body,
        in_specs=ins,
        out_specs=[vmem() for _ in shapes],
        out_shape=shapes,
        scratch_shapes=list(scratch),
        compiler_params=pltpu.CompilerParams(vmem_limit_bytes=limit_mib << 20, **extra),
        cost_estimate=pl.CostEstimate(flops=0, transcendentals=0, bytes_accessed=moved << 20),
    )(*args)


def here():
    return lax.axis_index("ctx").astype(jnp.int32)


def three_parts(value):
    first = value.astype(BF16).astype(F32)
    rest = value - first
    second = rest.astype(BF16).astype(F32)
    return first, second, rest - second


def row_of(tokens, scal, requests):
    end = scal[0]
    passed = tokens >= end
    row = passed.astype(jnp.int32)
    prior = jnp.where(passed, end, 0)
    for r in range(1, requests):
        end = end + scal[r]
        passed = tokens >= end
        row = row + passed.astype(jnp.int32)
        prior = jnp.where(passed, end, prior)
    return row, prior


def to_sublanes(lane_row):
    n = lane_row.shape[1]
    sub = lax.broadcasted_iota(jnp.int32, (n, n), 0)
    lane = lax.broadcasted_iota(jnp.int32, (n, n), 1)
    return jnp.sum(jnp.where(sub == lane, lane_row, 0), axis=1, keepdims=True)


GU_ROWS = 512
DOWN_ROWS = 256


def piece_shape(piece):
    _, _, n, cols = piece
    return (n, GU_ROWS, cols)


def gate_up_block(flip, i, w_gate, w_up):
    wide = w_gate.shape[0] // CELL
    row = (here() % CELL ^ flip) * wide + i // 2 * GU_ROWS
    w = w_gate if i % 2 == 0 else w_up
    return w.at[pl.ds(pl.multiple_of(row, GU_ROWS), GU_ROWS), :]


def fetch_copies(fetch, weights, pieces, sem):
    copies = []
    for (flip, first, n, _), out in zip(fetch, pieces):
        for i in range(n):
            src = gate_up_block(flip, first + i, *weights)
            copies.append(pltpu.make_async_copy(src, out.at[i], sem.at[len(copies)]))
    return copies


def blocks_of(held, refs):
    found = {}
    for (flip, first, n, _), r in zip(held, refs):
        for i in range(n):
            found[flip, first + i] = r.at[i]
    return found


def count_of(fetch):
    return max(1, sum(p[2] for p in fetch))


def warm_body(fetch, dep, w_gate, w_up, *refs):
    copies = fetch_copies(fetch, (w_gate, w_up), refs[:-1], refs[-1])
    for c in copies:
        c.start()
    for c in copies:
        c.wait()


def prep_body(q, kv, res, gain, *refs):
    msgs, own_gain, sem = refs[:CELL], refs[CELL], refs[CELL + 1]
    pos = here() % CELL
    wide, key_cols = q.shape[1] // CELL, kv.shape[1] // (2 * CELL)
    copies = []

    def move(src, width, first, dst):
        at = pl.multiple_of(first, HD)
        src = src.at[:, pl.ds(at, width)]
        copies.append(pltpu.make_async_copy(src, dst, sem.at[len(copies)]))

    for k in range(CELL):
        g = pos ^ k
        half = kv.shape[1] // 2
        ends = [0, wide, wide + key_cols, wide + 2 * key_cols, 2 * wide + 2 * key_cols]
        dst = [msgs[k].at[:, a:b] for a, b in zip(ends, ends[1:])]
        move(q, wide, g * wide, dst[0])
        move(kv, key_cols, g * key_cols, dst[1])
        move(kv, key_cols, half + g * key_cols, dst[2])
        move(res, wide, g * wide, dst[3])
    rows = own_gain.shape[0]
    src = gain.at[pl.ds(pl.multiple_of(pos * rows, rows), rows), :]
    copies.append(pltpu.make_async_copy(src, own_gain, sem.at[len(copies)]))
    for c in copies:
        c.start()
    for c in copies:
        c.wait()


def turn_body(requests, devices, fetch, *refs):
    sources, weights, refs = refs[:5], refs[5:7], refs[7:]
    sends, relays, token_row = refs[:CELL], refs[CELL : 2 * CELL], refs[2 * CELL]
    refs = refs[2 * CELL + 1 :]
    pieces, refs = refs[: len(fetch)], refs[len(fetch) :]
    locals_, sems, fetch_sem = refs[:5], refs[5], refs[6]
    loads = [pltpu.make_async_copy(a, b, sems.at[i]) for i, (a, b) in enumerate(zip(sources, locals_))]
    for c in loads:
        c.start()
    fetched = fetch_copies(fetch, weights, pieces, fetch_sem)
    for c in fetched:
        c.start()
    for c in loads:
        c.wait()

    @pl.when(here() >= 0)
    def _():
        turn_steps(requests, devices, *locals_, sends, relays, token_row)

    for c in fetched:
        c.wait()


def turn_steps(
    requests, devices, scal, slot, cache, old_angle, new_angle, sends, relays, token_row
):
    me = here()
    pos_in_cell = me % CELL
    tok_n, width = cache.shape
    table_n = old_angle.shape[1]
    heads_here = KVH // CELL
    key_cols = heads_here * HD
    tokens = me * tok_n + lax.broadcasted_iota(jnp.int32, (tok_n, 1), 0)
    for k in range(CELL):
        base = (me - pos_in_cell + (pos_in_cell ^ k)) * tok_n
        wide_tokens = base + lax.broadcasted_iota(jnp.int32, (1, tok_n), 1)
        token_row[:, k * tok_n : (k + 1) * tok_n] = row_of(wide_tokens, scal, requests)[0]
    _, prior = row_of(tokens, scal, requests)
    position = jnp.clip(tokens - prior, 0, table_n - 1)
    hot = (lax.broadcasted_iota(jnp.int32, (tok_n, table_n), 1) == position).astype(F32)
    diff = new_angle[...] - old_angle[...]
    diff = jnp.concatenate([diff, diff], axis=0)
    delta = lax.dot_general(
        hot,
        diff,
        (((1,), (1,)), ((), ())),
        precision=lax.Precision.HIGHEST,
        preferred_element_type=F32,
    )
    cosine = jnp.cos(delta)
    lane = lax.broadcasted_iota(jnp.int32, (tok_n, HD), 1)
    sine = jnp.where(lane < HD // 2, -jnp.sin(delta), jnp.sin(delta))
    half = width // 2
    keys = []
    for h in range(KVH):
        key = cache[:, h * HD : (h + 1) * HD].astype(F32)
        keys.append((key * cosine + pltpu.roll(key, HD // 2, 1) * sine).astype(BF16))
    turned = jnp.concatenate(keys + [cache[:, half:]], axis=1)
    for k in range(CELL):
        peer = pos_in_cell ^ k
        for g in range(CELL):

            @pl.when(peer == g)
            def _():
                sends[k][:, :key_cols] = turned[:, g * key_cols : (g + 1) * key_cols]
                sends[k][:, key_cols:] = turned[:, half + g * key_cols : half + (g + 1) * key_cols]

    place = slot[...]
    per_peer = tok_n // devices
    lanes = lax.broadcasted_iota(jnp.int32, (1, tok_n), 1)
    target = jnp.where(place >= 0, place // CTOK_DEV, lanes // per_peer)
    landing = jnp.where(place >= 0, place % CTOK_DEV, -1)
    target_s = to_sublanes(target)
    sub2 = lax.broadcasted_iota(jnp.int32, (tok_n, tok_n), 0)
    lane2 = lax.broadcasted_iota(jnp.int32, (tok_n, tok_n), 1)
    ahead = ((target_s == target) & (sub2 < lane2)).astype(jnp.int32)
    rank = jnp.sum(ahead, axis=0, keepdims=True)
    order = (target % CELL) * (devices // CELL) + target // CELL
    pick = sub2 == (order * per_peer + rank)
    moved = jnp.dot(pick.astype(BF16), turned, preferred_element_type=F32).astype(BF16)
    land_s = jnp.sum(jnp.where(pick, landing, 0), axis=1, keepdims=True)
    land_wide = jnp.broadcast_to(land_s.astype(F32), (tok_n, EXTRA)).astype(BF16)
    block = tok_n // CELL
    for k in range(CELL):
        for g in range(CELL):

            @pl.when((pos_in_cell ^ k) == g)
            def _():
                relays[k][:, :width] = moved[g * block : (g + 1) * block]
                relays[k][:, width:] = land_wide[g * block : (g + 1) * block]


def assemble_body(*refs):
    msgs, cat, query = refs[:CELL], refs[CELL], refs[CELL + 1]
    pos = here() % CELL
    wide = query.shape[1]
    whole = [r[...].astype(F32) for r in msgs]
    for bit in (1, 2):
        flip = (pos & bit) != 0
        whole = [jnp.where(flip, whole[a ^ bit], whole[a]) for a in range(CELL)]
    whole = jnp.concatenate(whole, axis=0).astype(BF16)
    cat[...] = whole
    query[...] = whole[:, :wide]


def place_body(mine, far, near, out):
    got = jnp.concatenate([mine[...], far[: mine.shape[0]], near[...]], axis=0)
    width = out.shape[1]
    rows = got.shape[0]
    land = got[:, width:].astype(F32)[:, :CTOK_DEV]
    want = lax.broadcasted_iota(jnp.int32, (rows, CTOK_DEV), 1).astype(F32)
    pick = (land == want).astype(BF16)
    out[...] = lax.dot_general(
        pick, got[:, :width], (((0,), (0,)), ((), ())), preferred_element_type=F32
    ).astype(BF16)


def scores_body(planes, fetch, token_row, *refs):
    qs, kvs, refs = refs[:planes], refs[planes : planes + CELL], refs[planes + CELL :]
    weights, outs, refs = refs[:2], refs[2 : 2 + planes], refs[2 + planes :]
    fetched = fetch_copies(fetch, weights, refs[: len(fetch)], refs[-1])
    for c in fetched:
        c.start()

    @pl.when(here() >= 0)
    def _():
        scores_steps(planes, token_row, qs, kvs, outs)

    for c in fetched:
        c.wait()


def scores_steps(planes, token_row, qs, kvs, outs):
    plane = here() // CELL
    rows = qs[0].shape[0]
    _, both = kvs[0].shape
    key_cols = both // 2
    heads_here = key_cols // HD
    group = QH // KVH
    all_rows = rows * planes
    query = jnp.concatenate([r[...].astype(F32) for r in qs], axis=0).astype(BF16)
    index = lax.broadcasted_iota(jnp.int32, (group * all_rows, 1), 0)
    query_row = ((index // rows) % planes) ^ plane
    matching = query_row == token_row[...]
    lane = lax.broadcasted_iota(jnp.int32, (all_rows, EXTRA), 1)
    extra = jnp.zeros((all_rows, EXTRA), F32)
    count = heads_here * group
    scale = 1.0 / float(HD) ** 0.5
    for j in range(heads_here):
        keys = jnp.concatenate([r[:, j * HD : (j + 1) * HD] for r in kvs], axis=0)
        values = jnp.concatenate(
            [r[:, key_cols + j * HD : key_cols + (j + 1) * HD] for r in kvs], axis=0
        )
        stacked = jnp.concatenate(
            [query[:, (j * group + g) * HD : (j * group + g + 1) * HD] for g in range(group)],
            axis=0,
        )
        scores = (
            lax.dot_general(stacked, keys, (((1,), (1,)), ((), ())), preferred_element_type=F32)
            * scale
        )
        top = jnp.max(jnp.where(matching, scores, -1e30), axis=1, keepdims=True)
        weights = jnp.where(matching, jnp.exp(scores - top), 0.0)
        total = jnp.sum(weights, axis=1, keepdims=True)
        high = weights.astype(BF16)
        low = (weights - high.astype(F32)).astype(BF16)
        summed = jnp.dot(high, values, preferred_element_type=F32) + jnp.dot(
            low, values, preferred_element_type=F32
        )
        mean = summed / jnp.where(total > 0, total, 1.0)
        top = jnp.where(total > 0, top, 0.0)
        tops = three_parts(top)
        totals = three_parts(total)
        for g in range(group):
            h = j * group + g
            part = slice(g * all_rows, (g + 1) * all_rows)
            for k in range(planes):
                outs[k][:, h * HD : (h + 1) * HD] = mean[
                    g * all_rows + k * rows : g * all_rows + (k + 1) * rows
                ].astype(BF16)
            for i in range(3):
                extra = jnp.where(lane == i * count + h, tops[i][part], extra)
                extra = jnp.where(lane == (3 + i) * count + h, totals[i][part], extra)
    for k in range(planes):
        outs[k][:, count * HD :] = extra[k * rows : (k + 1) * rows].astype(BF16)


def regroup_body(planes, fetch, *refs):
    moved, weights, (mine, far, near, *refs) = refs[:CELL], refs[CELL : CELL + 2], refs[CELL + 2 :]
    fetched = fetch_copies(fetch, weights, refs[: len(fetch)], refs[-1])
    for c in fetched:
        c.start()
    plane = here() // CELL
    per = moved[0].shape[0] // planes
    block = CELL * per
    for out, at, k in ((mine, 0, 0), (far, 0, 2), (far, block, 3), (near, 0, 1)):
        for g in range(planes):

            @pl.when((plane ^ k) == g)
            def _():
                for a in range(CELL):
                    out[at + a * per : at + (a + 1) * per] = moved[a][g * per : (g + 1) * per]

    for c in fetched:
        c.wait()


def merge_body(planes, fetch, *refs):
    parts, cat, gain, refs = refs[:planes], *refs[planes : planes + 2], refs[planes + 2 :]
    weights, norm_out, h_out, refs = refs[:2], *refs[2:4], refs[4:]
    fetched = fetch_copies(fetch, weights, refs[: len(fetch)], refs[-1])
    for c in fetched:
        c.start()

    @pl.when(here() >= 0)
    def _():
        merge_steps(parts, cat, gain, norm_out, h_out)

    for c in fetched:
        c.wait()


def merge_steps(parts, cat, gain, norm_out, h_out):
    rows = cat.shape[0]
    wide = norm_out.shape[1] - EXTRA
    count = wide // HD
    group = QH // KVH
    heads_here = count // group
    key_cols = heads_here * HD
    scale = 1.0 / float(HD) ** 0.5
    lane = lax.broadcasted_iota(jnp.int32, (rows, EXTRA), 1)
    odd = lax.broadcasted_iota(jnp.int32, (rows, 1), 0) % 2 == 1
    fresh = cat[:, wide : wide + 2 * key_cols].astype(F32)
    before = pltpu.roll(fresh, 1, 0)
    score_self = jnp.zeros((rows, EXTRA), F32)
    score_before = jnp.zeros((rows, EXTRA), F32)
    for h in range(count):
        j = h // group
        query = cat[:, h * HD : (h + 1) * HD].astype(F32)
        one = jnp.sum(query * fresh[:, j * HD : (j + 1) * HD], axis=1, keepdims=True) * scale
        two = jnp.sum(query * before[:, j * HD : (j + 1) * HD], axis=1, keepdims=True) * scale
        score_self = jnp.where(lane == h, one, score_self)
        score_before = jnp.where(lane == h, two, score_before)
    tops, totals = [], []
    for part in parts:
        extra = part[:, wide:].astype(F32)
        shifted = [extra] + [pltpu.roll(extra, EXTRA - i * count, 1) for i in range(1, 6)]
        tops.append(shifted[0] + shifted[1] + shifted[2])
        totals.append(shifted[3] + shifted[4] + shifted[5])
    highest = jnp.where(odd, jnp.maximum(score_self, score_before), score_self)
    for top, total in zip(tops, totals):
        highest = jnp.where(total > 0, jnp.maximum(highest, top), highest)
    shares = [
        jnp.where(total > 0, total * jnp.exp(jnp.where(total > 0, top, highest) - highest), 0.0)
        for top, total in zip(tops, totals)
    ]
    share_self = jnp.exp(score_self - highest)
    share_before = jnp.where(odd, jnp.exp(score_before - highest), 0.0)
    whole = share_self + share_before
    for share in shares:
        whole = whole + share
    squares = jnp.zeros((rows, 1), F32)
    for h in range(count):
        j = h // group
        value = slice(key_cols + j * HD, key_cols + (j + 1) * HD)
        lanes = slice(h * HD, (h + 1) * HD)
        attn = share_self[:, h : h + 1] * fresh[:, value]
        attn = attn + share_before[:, h : h + 1] * before[:, value]
        for part, share in zip(parts, shares):
            attn = attn + share[:, h : h + 1] * part[:, lanes].astype(F32)
        attn = attn / whole[:, h : h + 1]
        base = wide + 2 * key_cols + h * HD
        state = cat[:, base : base + HD].astype(F32) + attn
        h_out[:, lanes] = state
        squares = squares + jnp.sum(state * state, axis=1, keepdims=True)
        norm_out[:, lanes] = (state * gain[h : h + 1, :].astype(F32)).astype(BF16)
    pieces = three_parts(squares)
    extra = jnp.zeros((rows, EXTRA), F32)
    for i in range(3):
        extra = jnp.where(lane == i, pieces[i], extra)
    norm_out[:, wide:] = extra.astype(BF16)


def gate_up_body(flip, held, fetch, has_acc, *refs):
    x, refs = refs[0], refs[1:]
    acc_in, refs = (refs[0], refs[1:]) if has_acc else (None, refs)
    blocks, refs = blocks_of(held, refs[: len(held)]), refs[len(held) :]
    w_gate, w_up, acc_out, *pieces, fetch_sem = refs
    ff = w_gate.shape[1]
    fetched = fetch_copies(fetch, (w_gate, w_up), pieces, fetch_sem)
    for c in fetched:
        c.start()

    @pl.when(here() >= 0)
    def _():
        for i in range(2 * (x.shape[1] - EXTRA) // GU_ROWS):
            k = i // 2
            cols = slice((i % 2) * ff, (i % 2 + 1) * ff)
            part = jnp.dot(
                x[:, k * GU_ROWS : (k + 1) * GU_ROWS],
                blocks[flip, i][...],
                preferred_element_type=F32,
            )
            if k == 0:
                acc_out[:, cols] = acc_in[:, cols] + part if has_acc else part
            else:
                acc_out[:, cols] += part

    for c in fetched:
        c.wait()


def hidden_body(planes, held, late, own, xs, near, far, acc_in, *refs):
    blocks, refs = blocks_of(held, refs[: len(held)]), refs[len(held) :]
    w_gate, w_up, w_down, out, down_out, acc, buf, sem, dsem = refs
    wide = near.shape[1] - EXTRA
    ff = w_gate.shape[1]
    pos = here() % CELL
    fetched = fetch_copies([late], (w_gate, w_up), [buf], sem)
    downs = []
    for n in range(down_out.shape[0] // DOWN_ROWS):
        rows = pl.ds(n * DOWN_ROWS, DOWN_ROWS)
        downs.append(pltpu.make_async_copy(w_down.at[rows, :], down_out.at[rows, :], dsem.at[n]))
    for c in fetched + downs:
        c.start()
    per = 2 * wide // GU_ROWS
    x_of = {1: near, 3: far}

    def add(flip, i, w):
        k = i // 2
        cols = slice((i % 2) * ff, (i % 2 + 1) * ff)
        part = jnp.dot(
            x_of[flip][:, k * GU_ROWS : (k + 1) * GU_ROWS], w, preferred_element_type=F32
        )
        if flip == 1 and k == 0:
            acc[:, cols] = acc_in[:, cols] + part
        else:
            acc[:, cols] += part

    @pl.when(pos >= 0)
    def _():
        for flip in (1, 3):
            for i in range(per):
                if (flip, i) in blocks:
                    add(flip, i, blocks[flip, i][...])

    for n, c in enumerate(fetched):
        c.wait()
        add(late[0], late[1] + n, buf[n])
    squares = jnp.zeros((near.shape[0], 1), F32)
    for x in (own, xs, near, far):
        extra = x[:, wide : wide + EXTRA].astype(F32)
        squares = squares + extra[:, 0:1] + extra[:, 1:2] + extra[:, 2:3]
    inv = lax.rsqrt(squares / float(wide * CELL) + 1e-05)
    gate = acc[:, :ff] * inv
    hidden = gate / (1.0 + jnp.exp(-gate)) * (acc[:, ff:] * inv)
    hidden = jnp.concatenate(
        [
            hidden[k * 2 * CELL + a * 2 : k * 2 * CELL + a * 2 + 2]
            for a in (0, 2, 1, 3)
            for k in range(planes)
        ],
        axis=0,
    ).astype(BF16)
    out[...] = hidden
    for c in downs:
        c.wait()


def down_body(planes, hidden, h, held, w_down, send, keep, out, dbuf, dsem):
    pos = here() % CELL
    wide = h.shape[1]
    n_held, total = held.shape[0] // DOWN_ROWS, w_down.shape[0] // DOWN_ROWS
    downs = []
    for n in range(n_held, total):
        src = w_down.at[pl.ds(n * DOWN_ROWS, DOWN_ROWS), :]
        downs.append(pltpu.make_async_copy(src, dbuf.at[n - n_held], dsem.at[n - n_held]))
    for c in downs:
        c.start()

    @pl.when(pos >= 0)
    def _():
        for n in range(n_held):
            rows = slice(n * DOWN_ROWS, (n + 1) * DOWN_ROWS)
            part = jnp.dot(hidden[:, rows], held[rows, :], preferred_element_type=F32)
            if n == 0:
                out[...] = part
            else:
                out[...] += part

    for n in range(n_held, total):
        downs[n - n_held].wait()
        rows = slice(n * DOWN_ROWS, (n + 1) * DOWN_ROWS)
        out[...] += jnp.dot(hidden[:, rows], dbuf[n - n_held], preferred_element_type=F32)
    per = 2 * planes
    for g in range(CELL):

        @pl.when(pos == g)
        def _():
            cols = slice(g * wide, (g + 1) * wide)
            for n, a in enumerate((0, 2, 1, 3)):
                out[n * per : n * per + 2, cols] += h[2 * a : 2 * a + 2]

    half = 2 * per
    other = jnp.where(pos % 2 == 0, out[half:], out[:half])
    mine = jnp.where(pos % 2 == 0, out[:half], out[half:])
    send[...] = other
    keep[...] = mine


def halve_body(mine, got, send, keep):
    total = mine[...] + got[...]
    half = total.shape[0] // 2
    low = (here() % CELL) // 2 == 0
    send[...] = jnp.where(low, total[half:], total[:half]).astype(BF16)
    keep[...] = jnp.where(low, total[:half], total[half:])


def spread_body(planes, mine, got, *outs):
    total = mine[...] + got[...].astype(F32)
    outs[0][...] = total[0:2]
    for k in range(1, planes):
        outs[k][...] = total[2 * k : 2 * k + 2].astype(BF16)


def final_body(mine, *refs):
    total = mine[...]
    for r in refs[:-1]:
        total = total + r[...].astype(F32)
    refs[-1][...] = total.astype(BF16)


def swap(x, k, devices):
    return lax.ppermute(x, "ctx", [(i, i ^ k) for i in range(devices)])


def cells_program(*args):
    return cells_steps(*args)


def cells_steps(
    old_cache,
    new_slot,
    lengths,
    old_angle,
    new_angle,
    queries,
    new_kv,
    resid,
    gain,
    w_gate,
    w_up,
    w_down,
):
    devices = lax.axis_size("ctx")
    planes = devices // CELL
    tok_n, width = old_cache.shape
    requests = lengths.shape[0]
    rows_dev, model = queries.shape
    wide = model // CELL
    key_cols = KVH // CELL * HD
    msg_cols = 2 * wide + 2 * key_cols
    cell_rows = rows_dev * CELL
    all_rows = cell_rows * planes
    ff = w_gate.shape[1]
    weights = (in_hbm(w_gate), in_hbm(w_up))
    per = 2 * wide // GU_ROWS
    plans = {
        "turn": [(0, 0, 4, ff)],
        "warm_z": [(0, 4, 2, ff)],
        "scores": [(0, 6, per - 6, ff)],
        "merge": [(2, 0, 1, ff)],
        "regroup": [(2, 1, 2, ff)],
        "gate_up_own": [(2, 3, per - 3, ff), (1, 0, 3, ff)],
        "gate_up_x": [(1, 3, per - 3, ff), (3, 0, 4, ff)],
        "rest": [(3, 4, per - 4, ff)],
    }
    held = []

    def keep_pieces(name, values):
        held.extend(zip(plans[name], values))

    def pieces_for(*flips):
        found = [h for h in held if h[0][0] in flips]
        return [h[0] for h in found], [in_vmem(h[1]) for h in found]

    def warm(name, dep):
        plan = plans[name]
        values = call(
            lambda *r: warm_body(plan, *r),
            [hbm()] * 3,
            [],
            (dep, *weights),
            1,
            [pltpu.SemaphoreType.DMA((count_of(plan),))],
            plan,
            8,
        )
        keep_pieces(name, values)

    sources = (queries, new_kv, resid, gain.reshape(model // HD, HD))
    prepared = call(
        prep_body,
        [hbm()] * 4,
        [((rows_dev, msg_cols), BF16)] * CELL + [((wide // HD, HD), BF16)],
        tuple(in_hbm(x) for x in sources),
        2,
        [pltpu.SemaphoreType.DMA((4 * CELL + 1,))],
    )
    msgs, own_gain = prepared[:CELL], prepared[CELL]
    msgs = [msgs[0]] + [swap(msgs[k], k, devices) for k in range(1, CELL)]
    plan = plans["turn"]
    sources = (lengths, new_slot[None, :], old_cache, old_angle.T, new_angle.T)
    turned = call(
        lambda *r: turn_body(requests, devices, plan, *r),
        [hbm()] * 7,
        [((tok_n, 2 * key_cols), BF16)] * CELL
        + [((tok_n // CELL, width + EXTRA), BF16)] * CELL
        + [((1, CELL * tok_n), jnp.int32)],
        (*[in_hbm(x) for x in sources], *weights),
        10,
        [pltpu.SMEM(lengths.shape, lengths.dtype)]
        + [pltpu.VMEM(x.shape, x.dtype) for x in sources[1:]]
        + [pltpu.SemaphoreType.DMA((len(sources),)), pltpu.SemaphoreType.DMA((count_of(plan),))],
        plan,
        8,
    )
    sends, relays = turned[:CELL], turned[CELL : 2 * CELL]
    token_row = turned[2 * CELL]
    keep_pieces("turn", turned[2 * CELL + 1 :])
    kvs = [sends[0]] + [swap(sends[k], k, devices) for k in range(1, CELL)]
    cat, own_q = call(
        assemble_body,
        [vmem()] * CELL,
        [((cell_rows, msg_cols), BF16), ((cell_rows, wide), BF16)],
        tuple(msgs),
        4,
    )
    qs = [own_q] + [swap(own_q, CELL * k, devices) for k in range(1, planes)]
    relays = [relays[0]] + [swap(relays[k], k, devices) for k in range(1, CELL)]
    plan = plans["scores"]
    parts = call(
        lambda *r: scores_body(planes, plan, *r),
        [vmem()] * (1 + planes + CELL) + [hbm()] * 2,
        [((cell_rows, wide + EXTRA), BF16)] * planes,
        (token_row, *qs, *kvs, *weights),
        10,
        [pltpu.SemaphoreType.DMA((count_of(plan),))],
        plan,
        5,
    )
    keep_pieces("scores", parts[planes:])
    parts = [parts[0]] + [swap(parts[k], CELL * k, devices) for k in range(1, planes)]
    plan = plans["merge"]
    merged = call(
        lambda *r: merge_body(planes, plan, *r),
        [vmem()] * (planes + 2) + [hbm()] * 2,
        [((cell_rows, wide + EXTRA), BF16), ((cell_rows, wide), F32)],
        (*parts, cat, own_gain, *weights),
        6,
        [pltpu.SemaphoreType.DMA((count_of(plan),))],
        plan,
        4,
    )
    normed, hstate = merged[:2]
    keep_pieces("merge", merged[2:])
    block = tok_n // planes
    regroup_plan = plans["regroup"]
    grouped = call(
        lambda *r: regroup_body(planes, regroup_plan, *r),
        [vmem()] * CELL + [hbm()] * 2,
        [((n * block, width + EXTRA), BF16) for n in (1, 2, 1)],
        (*relays, *weights),
        4,
        [pltpu.SemaphoreType.DMA((count_of(regroup_plan),))],
        regroup_plan,
        4,
    )
    relay_mine, relay_far, relay_near = grouped[:3]
    keep_pieces("regroup", grouped[3:])
    relay_far = swap(relay_far, 2 * CELL, devices)
    warm("warm_z", normed)
    blocks = [normed] + [swap(normed, CELL * k, devices) for k in range(1, planes)]
    own = jnp.concatenate(blocks, axis=0)
    across = swap(own, 2, devices)
    near = swap(own, 1, devices)

    def gate_up(name, flip, x, acc):
        specs, values = pieces_for(flip)
        plan = plans[name]
        more = [] if acc is None else [acc]
        acc, *pieces = call(
            lambda *r: gate_up_body(flip, specs, plan, len(more) > 0, *r),
            [vmem()] * (1 + len(more) + len(values)) + [hbm()] * 2,
            [((all_rows, 2 * ff), F32)],
            (x, *more, *values, *weights),
            4,
            [pltpu.SemaphoreType.DMA((count_of(plan),))],
            plan,
            14,
        )
        keep_pieces(name, pieces)
        return acc

    acc = gate_up("gate_up_own", 0, own, None)
    far = swap(across, 1, devices)
    acc = gate_up("gate_up_x", 2, across, acc)
    relay_near = jnp.concatenate([relay_near, relay_far[block:]], axis=0)
    relay_near = swap(relay_near, CELL, devices)
    specs, values = pieces_for(1, 3)
    late = plans["rest"][0]
    n_first = 3
    n_later = ff // DOWN_ROWS - n_first
    hidden, down_held = call(
        lambda *r: hidden_body(planes, specs, late, *r),
        [vmem()] * (5 + len(values)) + [hbm()] * 3,
        [((all_rows, ff), BF16), ((n_first * DOWN_ROWS, model), BF16)],
        (
            *[in_vmem(x) for x in (own, across, near, far, acc)],
            *values,
            *weights,
            in_hbm(w_down),
        ),
        12,
        [
            pltpu.VMEM((all_rows, 2 * ff), F32),
            pltpu.VMEM(piece_shape(late), BF16),
            pltpu.SemaphoreType.DMA((count_of([late]),)),
            pltpu.SemaphoreType.DMA((n_first,)),
        ],
        moved=20,
        on_chip=True,
    )
    send, keep = call(
        lambda *r: down_body(planes, *r),
        [vmem()] * 3 + [hbm()],
        [((all_rows // 2, model), F32)] * 2,
        (in_vmem(hidden), in_vmem(hstate), in_vmem(down_held), in_hbm(w_down)),
        19,
        [
            pltpu.VMEM((all_rows, model), F32),
            pltpu.VMEM((n_later, DOWN_ROWS, model), BF16),
            pltpu.SemaphoreType.DMA((n_later,)),
        ],
        moved=20,
        on_chip=True,
    )
    got = swap(send, 1, devices)
    send, keep = call(
        lambda *r: halve_body(*r),
        [vmem(), vmem()],
        [((all_rows // 4, model), BF16), ((all_rows // 4, model), F32)],
        (in_vmem(keep), got),
        8,
    )
    got = swap(send, 2, devices)
    pieces = call(
        lambda *r: spread_body(planes, *r),
        [vmem()] * 2,
        [((rows_dev, model), F32)] + [((rows_dev, model), BF16)] * (planes - 1),
        (keep, got),
        8,
    )
    pieces = [pieces[0]] + [swap(pieces[k], CELL * k, devices) for k in range(1, planes)]
    layer_out = call(
        final_body, [vmem()] * planes, [((rows_dev, model), BF16)], tuple(pieces), 8
    )[0]
    new_cache = call(
        place_body,
        [vmem()] * 3,
        [((CTOK_DEV, width), BF16)],
        (relay_mine, relay_far, relay_near),
        8,
        moved=1,
    )[0]
    return (new_cache, layer_out)


def rotate_block(block, where_pos, old_angle, new_angle):
    rows_here = block.shape[0]
    half_size = HD // 2
    parts = block.reshape(rows_here, 2, KVH, HD)
    keys = parts[:, 0].astype(jnp.float32)
    delta = jnp.take(new_angle, where_pos, axis=0) - jnp.take(old_angle, where_pos, axis=0)
    cosine = jnp.cos(delta)[:, None, :]
    sine = jnp.sin(delta)[:, None, :]
    first = keys[..., :half_size]
    second = keys[..., half_size:]
    turned = jnp.concatenate(
        [first * cosine - second * sine, second * cosine + first * sine], axis=-1
    ).astype(jnp.bfloat16)
    return jnp.stack([turned, parts[:, 1]], axis=1).reshape(rows_here, 2 * KVH * HD)


def general_program(
    old_cache,
    new_slot,
    lengths,
    old_angle,
    new_angle,
    queries,
    new_kv,
    resid,
    gain,
    w_gate,
    w_up,
    w_down,
):
    devices = lax.axis_size("ctx")
    own_index = lax.axis_index("ctx")
    slot_count = old_cache.shape[0]
    row_width = old_cache.shape[1]
    per_peer = slot_count // devices
    rows_dev = queries.shape[0]
    all_rows = rows_dev * devices
    group_size = QH // KVH
    high = lax.Precision.HIGHEST
    scale = 1.0 / float(HD) ** 0.5
    tokens = own_index * slot_count + jnp.arange(slot_count, dtype=jnp.int32)
    row_ends = jnp.cumsum(lengths)
    passed = row_ends[None, :] <= tokens[:, None]
    owner_row = jnp.minimum(jnp.sum(passed.astype(jnp.int32), axis=1), lengths.shape[0] - 1)
    row_prior = jnp.sum(jnp.where(passed, lengths[None, :], 0), axis=1)
    position = jnp.clip(tokens - row_prior, 0, old_angle.shape[0] - 1)
    filled = new_slot >= 0
    all_queries = lax.all_gather(queries, "ctx", axis=0, tiled=True)
    target = jnp.where(
        filled, new_slot // CTOK_DEV, jnp.arange(slot_count, dtype=jnp.int32) // per_peer
    )
    sorted_order = jnp.argsort(target, stable=True)
    new_place = jnp.where(filled, new_slot % CTOK_DEV, -1)
    slot_info = jnp.stack([new_place, owner_row, position], axis=1)[sorted_order]
    sent_rows = old_cache[sorted_order].reshape(devices, per_peer, row_width)
    got_rows = lax.all_to_all(sent_rows, "ctx", split_axis=0, concat_axis=0, tiled=True)
    got_info = lax.all_to_all(
        slot_info.reshape(devices, per_peer, 3), "ctx", split_axis=0, concat_axis=0, tiled=True
    )
    got_rows = got_rows.reshape(slot_count, row_width)
    got_info = got_info.reshape(slot_count, 3)
    landing = jnp.where(got_info[:, 0] >= 0, got_info[:, 0], CTOK_DEV)
    placed = jnp.zeros((CTOK_DEV, row_width), jnp.bfloat16).at[landing].set(got_rows, mode="drop")
    placed_row = jnp.zeros((CTOK_DEV,), jnp.int32).at[landing].set(got_info[:, 1], mode="drop")
    placed_pos = jnp.zeros((CTOK_DEV,), jnp.int32).at[landing].set(got_info[:, 2], mode="drop")
    placed, moved_row, moved_pos = (placed, placed_row, placed_pos)
    new_cache = rotate_block(placed, moved_pos, old_angle, new_angle)
    key_count = new_cache.shape[0]
    key_split = new_cache.reshape(key_count, 2, KVH, HD)
    value_four = key_split[:, 1].astype(jnp.float32)
    query_four = all_queries.reshape(all_rows, KVH, group_size, HD)
    scores = (
        jnp.einsum(
            "mjge,cje->mjgc", query_four, key_split[:, 0], preferred_element_type=jnp.float32
        )
        * scale
    )
    query_row = jnp.arange(all_rows, dtype=jnp.int32) // (2 * SAMPLES)
    matching = query_row[:, None] == moved_row[None, :]
    scores = jnp.where(matching[:, None, None, :], scores, -1e30)
    local_top = jnp.max(scores, axis=-1)
    own_query = queries.reshape(rows_dev, KVH, group_size, HD).astype(jnp.float32)
    fresh_kv = jnp.repeat(new_kv.reshape(rows_dev // 2, 2, 2, KVH, HD), 2, axis=0).astype(
        jnp.float32
    )
    own_steps = (
        jnp.arange(2, dtype=jnp.int32)[None, :]
        <= (jnp.arange(rows_dev, dtype=jnp.int32) % 2)[:, None]
    )
    own_scores = jnp.einsum("mjge,msje->mjgs", own_query, fresh_kv[:, :, 0], precision=high) * scale
    own_scores = jnp.where(own_steps[:, None, None, :], own_scores, -1e30)
    own_top = jnp.max(own_scores, axis=-1)
    floor_top = jnp.maximum(local_top, -10000.0)
    weights_local = jnp.exp(scores - floor_top[..., None])
    summed = jnp.einsum("mjgc,cje->mjge", weights_local, value_four, precision=high)
    totals = jnp.sum(weights_local, axis=-1)
    got_sums, got_totals, got_tops = (
        lax.all_to_all(
            summed.reshape(devices, rows_dev, QH * HD),
            "ctx",
            split_axis=0,
            concat_axis=0,
            tiled=True,
        ),
        lax.all_to_all(
            totals.reshape(devices, rows_dev, QH), "ctx", split_axis=0, concat_axis=0, tiled=True
        ),
        lax.all_to_all(
            floor_top.reshape(devices, rows_dev, QH), "ctx", split_axis=0, concat_axis=0, tiled=True
        ),
    )
    got_tops = got_tops.reshape(devices, rows_dev, KVH, group_size)
    row_top = jnp.maximum(jnp.max(got_tops, axis=0), own_top)
    rescale = jnp.exp(got_tops - row_top[None])
    weights_own = jnp.exp(own_scores - row_top[..., None])
    row_sums = jnp.sum(
        rescale[..., None] * got_sums.reshape(devices, rows_dev, KVH, group_size, HD), axis=0
    )
    row_sums = row_sums + jnp.einsum(
        "mjgs,msje->mjge", weights_own, fresh_kv[:, :, 1], precision=high
    )
    row_totals = jnp.sum(
        rescale * got_totals.reshape(devices, rows_dev, KVH, group_size), axis=0
    ) + jnp.sum(weights_own, axis=-1)
    attn = (row_sums / row_totals[..., None]).reshape(rows_dev, QH * HD)
    hstate = resid.astype(jnp.float32) + attn
    normed = (
        hstate
        * lax.rsqrt(jnp.mean(hstate * hstate, axis=-1, keepdims=True) + 1e-05)
        * gain.astype(jnp.float32)
    ).astype(jnp.bfloat16)
    piece = lax.all_gather(normed, "ctx", axis=0, tiled=True)
    gate_out = jnp.dot(piece, w_gate, preferred_element_type=jnp.float32)
    up_out = jnp.dot(piece, w_up, preferred_element_type=jnp.float32)
    hidden_all = (jax.nn.silu(gate_out) * up_out).astype(jnp.bfloat16)
    ffn_out = lax.psum_scatter(
        jnp.dot(hidden_all, w_down, preferred_element_type=jnp.float32),
        "ctx",
        scatter_dimension=0,
        tiled=True,
    )
    layer_out = (hstate + ffn_out).astype(jnp.bfloat16)
    return (new_cache, layer_out)


def solution(mesh):
    per_device = cells_program if mesh.shape["ctx"] == 4 * CELL else general_program
    return jax.shard_map(
        per_device,
        mesh=mesh,
        in_specs=(
            P(("groups", "ctx"), None),
            P(("groups", "ctx")),
            P("groups"),
            P(),
            P(),
            P(("groups", "ctx"), None),
            P(("groups", "ctx"), None),
            P(("groups", "ctx"), None),
            P(),
            P(None, "ctx"),
            P(None, "ctx"),
            P("ctx", None),
        ),
        out_specs=(P(("groups", "ctx"), None), P(("groups", "ctx"), None)),
        check_vma=False,
    )
```
